32 devices in a mesh: dp: 8 (over z, y), row: 2 (over core), col: 2 (over x).
Axes of the slice: x: 2, y: 2, z: 4, core: 2. Of those that a mesh axis runs over, the one named last changes fastest.
Arguments:
- x_in: float32 [4096, 768], P(('dp', 'row'), 'col'), may hold values from -6 to 6
- cotangent: float32 [4096, 768], P(('dp', 'row'), 'col'), may hold values from -6 to 6
- segment_ids: int32 [8, 512], P('dp'), may hold values from 0 to 3, never falling along the last dimension, each value on 1 to 256 neighbouring positions
- norm1_gain: float32 [2, 768], P(None, 'col'), may hold values from 0.3 to 3.7
- norm1_bias: float32 [2, 768], P(None, 'col'), may hold values from -1.5 to 1.5
- norm2_gain: float32 [2, 768], P(None, 'col'), may hold values from 0.3 to 3.7
- norm2_bias: float32 [2, 768], P(None, 'col'), may hold values from -1.5 to 1.5
- w_qkv: bfloat16 [2, 768, 2304], P(None, 'col', 'row'), may hold values from -0.21875 to 0.21875
- b_qkv: float32 [2, 2304], P(None, ('row', 'col')), may hold values from -2.5 to 2.5
- w_up: bfloat16 [2, 768, 3072], P(None, 'col', 'row'), may hold values from -0.21875 to 0.21875
- b_up: float32 [2, 3072], P(None, ('row', 'col')), may hold values from -2.5 to 2.5
- w_out: bfloat16 [2, 768, 768], P(None, ('row', 'col')), may hold values from -0.875 to 0.875
- b_out: float32 [2, 768], P(None, 'col'), may hold values from -1.5 to 1.5
- w_down: bfloat16 [2, 3072, 768], P(None, ('row', 'col')), may hold values from -0.109375 to 0.109375
- b_down: float32 [2, 768], P(None, 'col'), may hold values from -1.5 to 1.5
Outputs:
- y_out: float32 [4096, 768], P(('dp', 'row'), 'col')
- x_grad: float32 [4096, 768], P(('dp', 'row'), 'col')
- g_norm1_gain: float32 [2, 768], P(None, 'col')
- g_norm1_bias: float32 [2, 768], P(None, 'col')
- g_norm2_gain: float32 [2, 768], P(None, 'col')
- g_norm2_bias: float32 [2, 768], P(None, 'col')
- g_w_qkv: float32 [2, 768, 2304], P(None, 'col', 'row')
- g_b_qkv: float32 [2, 2304], P(None, ('row', 'col'))
- g_w_up: float32 [2, 768, 3072], P(None, 'col', 'row')
- g_b_up: float32 [2, 3072], P(None, ('row', 'col'))
- g_w_out: float32 [2, 768, 768], P(None, ('row', 'col'))
- g_b_out: float32 [2, 768], P(None, 'col')
- g_w_down: float32 [2, 3072, 768], P(None, ('row', 'col'))
- g_b_down: float32 [2, 768], P(None, 'col')
The draws below stay inside these ranges and needn't reach their ends.
Inputs may be any that keep to these rules, and one draw needn't show every extreme that they name: `segment_ids`: along a sequence the ids never fall; each of the 4 documents of a sequence holds 1 to 256 tokens, one exactly 256.
All inputs are finite; a program needn't handle non-finite values.
Results may differ from the reference program's by a relative error of at most 0.035.
Values may be sent and summed in bfloat16 or wider, within the bound.
A program may use at most 128 MiB of HBM per device.

```python
import math
import jax
import jax.numpy as jnp
import numpy as np
from jax import lax

D = 768
H = 12
HD = 64
ROT = 16
FF = 3072
SEQ = 512
LAYERS = 2
DOCS = 4
DOC_MOST = 256
SEQS = 8
TOKENS = 4096


def ramp_gain(key):
    place = jnp.arange(D, dtype=jnp.float32) / (D - 1.0)
    low = 0.6
    ratio = 5.0
    noise = jnp.clip(0.05 * jax.random.normal(key, (LAYERS, D), jnp.float32), -0.1, 0.1)
    profile = low * jnp.exp(jnp.log(ratio) * place)
    return (profile[None, :] * (1.0 + noise)).astype(jnp.float32)


def draw_norm1_gain(key, part):
    return ramp_gain(jax.random.fold_in(key, 11))


def draw_norm2_gain(key, part):
    return ramp_gain(jax.random.fold_in(key, 23))


def levels(key, shape, shards, least, top_value):
    gain, own = 1.0, jax.random.fold_in(key, 6)
    for dim, shards_of in shards:
        draws = jnp.exp(jax.random.uniform(jax.random.fold_in(own, dim), (shards_of,), jnp.float32, least / len(shards), top_value / len(shards)))
        gain = gain * jnp.repeat(draws, shape[dim] // shards_of).reshape([-1 if axis == dim else 1 for axis in range(len(shape))])
    return gain


def split_up(count, total, limit, lean):
    loads = [(1 << 20) // math.isqrt(rank ** lean) + 1 for rank in range(2, count + 1)]
    surplus, holding = total - limit - (count - 1), [1] * (count - 1)
    while surplus > 0:
        candidates = [i for i in range(count - 1) if holding[i] < limit]
        mass, remaining = sum([loads[i] for i in candidates]), surplus
        for i in candidates:
            more = min(limit - holding[i], max(1, remaining * loads[i] // mass), surplus)
            holding[i] = holding[i] + more
            surplus = surplus - more
    return np.array([limit] + holding)


def uneven(stream_key, count, total, most, slope):
    if count == 2:
        one = jax.random.randint(stream_key, (), max(1, total - most), min(most, total - 1) + 1)
        return jnp.stack([one, total - one])
    lengths = jnp.asarray(split_up(count, total, most, slope), jnp.int32)
    pairs = (count - 1) // 2
    donor, sink = lengths[1:1 + 2 * pairs:2], lengths[2:2 + 2 * pairs:2]
    room = jnp.minimum(donor - 1, most - sink)
    shifted = jax.random.randint(jax.random.fold_in(stream_key, 1), (pairs,), 0, 1 << 20) % (room + 1)
    lengths = lengths.at[1:1 + 2 * pairs:2].set(donor - shifted).at[2:2 + 2 * pairs:2].set(sink + shifted)
    return lengths[jax.random.permutation(jax.random.fold_in(stream_key, 2), count)]


def scatter_about(key, shape, scale, most, split=(), kind=jnp.bfloat16):
    values = scale * jax.random.normal(key, shape, jnp.float32)
    if split:
        values = values * levels(key, shape, split, -0.22, 0.18)
    return jnp.clip(values, -most, most).astype(kind)


def setup_inputs(seed: int = 0) -> dict:
    key_of = jax.random.split(jax.random.key(seed), 16)
    return {
        "x_in": scatter_about(key_of[0], (TOKENS, D), 1.0, 6.0, ((0, 16), (1, 2)), jnp.float32),
        "cotangent": scatter_about(key_of[1], (TOKENS, D), 1.0, 6.0, ((0, 16), (1, 2)), jnp.float32),
        "segment_ids": jax.vmap(lambda own: jnp.searchsorted(jnp.cumsum(uneven(own, DOCS, SEQ, DOC_MOST, 1)), jnp.arange(SEQ), side="right"))(jax.random.split(key_of[2], SEQS)).reshape((SEQS, SEQ)).astype(jnp.int32),
        "norm1_gain": draw_norm1_gain(jax.random.fold_in(key_of[15], 71), 0),
        "norm1_bias": scatter_about(key_of[4], (LAYERS, D), 0.3, 1.5, ((1, 2),), jnp.float32),
        "norm2_gain": draw_norm2_gain(jax.random.fold_in(key_of[15], 71), 0),
        "norm2_bias": scatter_about(key_of[6], (LAYERS, D), 0.3, 1.5, ((1, 2),), jnp.float32),
        "w_qkv": scatter_about(key_of[7], (LAYERS, D, 3 * D), D ** -0.5, 0.21875, ((1, 2), (2, 2))),
        "b_qkv": scatter_about(key_of[8], (LAYERS, 3 * D), 0.5, 2.5, ((1, 4),), jnp.float32),
        "w_up": scatter_about(key_of[9], (LAYERS, D, FF), D ** -0.5, 0.21875, ((1, 2), (2, 2))),
        "b_up": scatter_about(key_of[10], (LAYERS, FF), 0.5, 2.5, ((1, 4),), jnp.float32),
        "w_out": scatter_about(key_of[11], (LAYERS, D, D), (D // 16) ** -0.5, 0.875, ((1, 4),)),
        "b_out": scatter_about(key_of[12], (LAYERS, D), 0.3, 1.5, ((1, 2),), jnp.float32),
        "w_down": scatter_about(key_of[13], (LAYERS, FF, D), FF ** -0.5, 0.109375, ((1, 4),)),
        "b_down": scatter_about(key_of[14], (LAYERS, D), 0.3, 1.5, ((1, 2),), jnp.float32),
    }


EPS = 1e-05
NEG = -1e+30
SCALE = 0.125
INV_ROOT2 = 0.7071067811865476
INV_ROOT_TWO_PI = 0.3989422804014327

def rope_tables(length):
    half = ROT // 2
    freq = 10000.0 ** (-(jnp.arange(half, dtype=jnp.float32) * 2.0) / ROT)
    angle = jnp.arange(length, dtype=jnp.float32)[:, None] * freq[None, :]
    cosine = jnp.concatenate([jnp.cos(angle), jnp.cos(angle)], axis=1)
    sine = jnp.concatenate([jnp.sin(angle), jnp.sin(angle)], axis=1)
    return (cosine, sine)

def rotate(values, cosine, sine):
    part = values[..., :ROT]
    lower = part[..., :ROT // 2]
    upper = part[..., ROT // 2:]
    turned = jnp.concatenate([-upper, lower], axis=-1)
    moved = part * cosine[:, None, :] + turned * sine[:, None, :]
    return jnp.concatenate([moved, values[..., ROT:]], axis=-1)

def unrotate(grads, cosine, sine):
    part = grads[..., :ROT]
    lower = part[..., :ROT // 2]
    upper = part[..., ROT // 2:]
    turned = jnp.concatenate([upper, -lower], axis=-1)
    moved = part * cosine[:, None, :] + turned * sine[:, None, :]
    return jnp.concatenate([moved, grads[..., ROT:]], axis=-1)

def gelu_exact(values):
    return 0.5 * values * (1.0 + jax.scipy.special.erf(values * INV_ROOT2))

def gelu_slope(values):
    return 0.5 * (1.0 + jax.scipy.special.erf(values * INV_ROOT2)) + values * jnp.exp(-0.5 * values * values) * INV_ROOT_TWO_PI

def make_scores(query, key, allowed):
    scores = jnp.einsum('qhd,khd->hqk', query.astype(jnp.float32), key.astype(jnp.float32)) * SCALE
    return jnp.where(allowed[None], scores, NEG)

def attend(query, key, value, allowed):
    scores = make_scores(query, key, allowed)
    top = lax.optimization_barrier(jnp.max(scores, axis=-1, keepdims=True))
    total = lax.optimization_barrier(jnp.sum(jnp.exp(scores - top), axis=-1, keepdims=True))
    lse = top + jnp.log(total)
    probs = jnp.exp(scores - lse).astype(jnp.bfloat16)
    mixed = jnp.einsum('hqk,khd->qhd', probs.astype(jnp.float32), value.astype(jnp.float32))
    return (mixed.astype(jnp.bfloat16), lse)

def attend_back(query, key, value, mixed, grad_mixed, lse, allowed):
    scores = make_scores(query, key, allowed)
    probs = jnp.exp(scores - lse)
    delta = jnp.einsum('qhd,qhd->hq', grad_mixed.astype(jnp.float32), mixed.astype(jnp.float32))
    grad_value = jnp.einsum('hqk,qhd->khd', probs.astype(jnp.bfloat16).astype(jnp.float32), grad_mixed.astype(jnp.float32))
    grad_probs = jnp.einsum('qhd,khd->hqk', grad_mixed.astype(jnp.float32), value.astype(jnp.float32))
    grad_scores = (probs * (grad_probs - delta[:, :, None]) * SCALE).astype(jnp.bfloat16).astype(jnp.float32)
    grad_query = jnp.einsum('hqk,khd->qhd', grad_scores, key.astype(jnp.float32))
    grad_key = jnp.einsum('hqk,qhd->khd', grad_scores, query.astype(jnp.float32))
    return (grad_query, grad_key, grad_value)

def layer_forward(state, allowed, cosine, sine, params):
    gain1, bias1, gain2, bias2, w_qkv, b_qkv, w_up, b_up, w_out, b_out, w_down, b_down = params
    mean = lax.optimization_barrier(jnp.mean(state, axis=1, keepdims=True))
    spread = lax.optimization_barrier(jnp.mean(state * state, axis=1, keepdims=True)) - mean * mean
    inverse = lax.rsqrt(spread + EPS)
    normed = (state - mean) * inverse
    first = (normed * gain1 + bias1).astype(jnp.bfloat16)
    second = (normed * gain2 + bias2).astype(jnp.bfloat16)
    qkv = (jnp.dot(first, w_qkv, preferred_element_type=jnp.float32) + b_qkv).reshape(-1, H, 3, HD)
    query = rotate(qkv[:, :, 0], cosine, sine).astype(jnp.bfloat16)
    key = rotate(qkv[:, :, 1], cosine, sine).astype(jnp.bfloat16)
    value = qkv[:, :, 2].astype(jnp.bfloat16)
    mixed, lse = attend(query, key, value, allowed)
    up = jnp.dot(second, w_up, preferred_element_type=jnp.float32) + b_up
    act = gelu_exact(up).astype(jnp.bfloat16)
    flat = mixed.reshape(-1, D)
    branches = jnp.dot(flat, w_out, preferred_element_type=jnp.float32) + jnp.dot(act, w_down, preferred_element_type=jnp.float32)
    result = state + branches + b_out + b_down
    return (result, (normed, inverse, first, second, query, key, value, mixed, lse, up, act))

def layer_backward(grad, allowed, cosine, sine, params, cache):
    gain1, bias1, gain2, bias2, w_qkv, b_qkv, w_up, b_up, w_out, b_out, w_down, b_down = params
    normed, inverse, first, second, query, key, value, mixed, lse, up, act = cache
    grad_b = grad.astype(jnp.bfloat16)
    flat = mixed.reshape(-1, D)
    g_wout = jnp.dot(flat.T, grad_b, preferred_element_type=jnp.float32)
    g_wdown = jnp.dot(act.T, grad_b, preferred_element_type=jnp.float32)
    g_bout = lax.optimization_barrier(jnp.sum(grad, axis=0))
    grad_mixed = jnp.dot(grad_b, w_out.T, preferred_element_type=jnp.float32).astype(jnp.bfloat16).reshape(-1, H, HD)
    grad_act = jnp.dot(grad_b, w_down.T, preferred_element_type=jnp.float32)
    grad_up = grad_act * gelu_slope(up)
    g_bup = lax.optimization_barrier(jnp.sum(grad_up, axis=0))
    grad_up_b = grad_up.astype(jnp.bfloat16)
    grad_query, grad_key, grad_value = attend_back(query, key, value, mixed, grad_mixed, lse, allowed)
    grad_query = unrotate(grad_query, cosine, sine)
    grad_key = unrotate(grad_key, cosine, sine)
    grad_qkv = jnp.stack([grad_query, grad_key, grad_value], axis=2).reshape(-1, 3 * D)
    g_bqkv = lax.optimization_barrier(jnp.sum(grad_qkv, axis=0))
    grad_qkv_b = grad_qkv.astype(jnp.bfloat16)
    g_wqkv = jnp.dot(first.T, grad_qkv_b, preferred_element_type=jnp.float32)
    g_wup = jnp.dot(second.T, grad_up_b, preferred_element_type=jnp.float32)
    grad_first = jnp.dot(grad_qkv_b, w_qkv.T, preferred_element_type=jnp.float32)
    grad_second = jnp.dot(grad_up_b, w_up.T, preferred_element_type=jnp.float32)
    g_gain1 = lax.optimization_barrier(jnp.sum(grad_first * normed, axis=0))
    g_bias1 = lax.optimization_barrier(jnp.sum(grad_first, axis=0))
    g_gain2 = lax.optimization_barrier(jnp.sum(grad_second * normed, axis=0))
    g_bias2 = lax.optimization_barrier(jnp.sum(grad_second, axis=0))
    grad_norm = grad_first * gain1 + grad_second * gain2
    centred = grad_norm - lax.optimization_barrier(jnp.mean(grad_norm, axis=1, keepdims=True)) - normed * lax.optimization_barrier(jnp.mean(grad_norm * normed, axis=1, keepdims=True))
    grad_x = grad + inverse * centred
    grads = (g_gain1, g_bias1, g_gain2, g_bias2, g_wqkv, g_bqkv, g_wup, g_bup, g_wout, g_bout, g_wdown, g_bout)
    return (grad_x, grads)

def reference(x_in, cotangent, segment_ids, norm1_gain, norm1_bias, norm2_gain, norm2_bias, w_qkv, b_qkv, w_up, b_up, w_out, b_out, w_down, b_down):
    stacked = (norm1_gain, norm1_bias, norm2_gain, norm2_bias, w_qkv, b_qkv, w_up, b_up, w_out, b_out, w_down, b_down)
    cosine, sine = rope_tables(SEQ)
    places = jnp.arange(SEQ, dtype=jnp.int32)
    causal = places[:, None] >= places[None, :]

    def group(totals, item):
        state, grad, seg = item
        allowed = causal & (seg[:, None] == seg[None, :])
        caches = []
        for layer in range(LAYERS):
            params = tuple((p[layer] for p in stacked))
            state, cache = layer_forward(state, allowed, cosine, sine, params)
            caches.append(cache)
        per_layer = [None] * LAYERS
        for layer in reversed(range(LAYERS)):
            params = tuple((p[layer] for p in stacked))
            grad, grads = layer_backward(grad, allowed, cosine, sine, params, caches[layer])
            per_layer[layer] = grads
        joined = tuple((jnp.stack([g[index] for g in per_layer]) for index in range(12)))
        totals = tuple((a + b for a, b in zip(totals, joined)))
        return (totals, (state, grad))
    zeros = tuple((jnp.zeros(p.shape, jnp.float32) for p in stacked))
    items = (x_in.reshape(SEQS, SEQ, D), cotangent.reshape(SEQS, SEQ, D), segment_ids)
    totals, (outputs, grads_in) = lax.scan(group, zeros, items)
    return (outputs.reshape(TOKENS, D), grads_in.reshape(TOKENS, D), totals[0], totals[1], totals[2], totals[3], totals[4], totals[5], totals[6], totals[7], totals[8], totals[9], totals[10], totals[11])
```

```python
import jax
import jax.numpy as jnp
from jax import lax
from jax.experimental import pallas as pl
from jax.experimental.pallas import tpu as pltpu
from jax.sharding import PartitionSpec as P

D = 768
HD = 64
ROT = 16
LAYERS = 2


EPS = 1e-05
NEG = -1e30
SCALE = 0.125
INV_ROOT2 = 0.7071067811865476
INV_ROOT_TWO_PI = 0.3989422804014327


def rope_tables(length):
    half = ROT // 2
    freq = 10000.0 ** (-(jnp.arange(half, dtype=jnp.float32) * 2.0) / ROT)
    angle = jnp.arange(length, dtype=jnp.float32)[:, None] * freq[None, :]
    cosine = jnp.concatenate([jnp.cos(angle), jnp.cos(angle)], axis=1)
    sine = jnp.concatenate([jnp.sin(angle), jnp.sin(angle)], axis=1)
    return (cosine, sine)


def rotate(values, cosine, sine):
    part = values[..., :ROT]
    lower = part[..., : ROT // 2]
    upper = part[..., ROT // 2 :]
    turned = jnp.concatenate([-upper, lower], axis=-1)
    moved = part * cosine[:, None, :] + turned * sine[:, None, :]
    return jnp.concatenate([moved, values[..., ROT:]], axis=-1)


def unrotate(grads, cosine, sine):
    part = grads[..., :ROT]
    lower = part[..., : ROT // 2]
    upper = part[..., ROT // 2 :]
    turned = jnp.concatenate([upper, -lower], axis=-1)
    moved = part * cosine[:, None, :] + turned * sine[:, None, :]
    return jnp.concatenate([moved, grads[..., ROT:]], axis=-1)


def gelu_exact(values):
    return 0.5 * values * (1.0 + jax.scipy.special.erf(values * INV_ROOT2))


def gelu_slope(values):
    return (
        0.5 * (1.0 + jax.scipy.special.erf(values * INV_ROOT2))
        + values * jnp.exp(-0.5 * values * values) * INV_ROOT_TWO_PI
    )


BF = jnp.bfloat16
F32 = jnp.float32
MESH_ID = pl.DeviceIdType.MESH
PIECES = 4


def greet():
    row = 1 - lax.axis_index("row")
    col = 1 - lax.axis_index("col")
    barrier = pltpu.get_barrier_semaphore()
    pl.semaphore_signal(barrier, inc=1, device_id={"row": row}, device_id_type=MESH_ID)
    pl.semaphore_signal(barrier, inc=1, device_id={"col": col}, device_id_type=MESH_ID)
    pl.semaphore_wait(barrier, 2)
    return row, col


def reduce_body(*refs):
    if len(refs) == 7:
        part, out, got_row, mine, got_col, send, recv = refs
        extra = None
    else:
        part, extra, out, extra_out, got_row, mine, got_col, pair, got_extra, send, recv = refs
    half = mine.shape[0]
    piece = half // PIECES
    row, col = greet()
    own = (1 - row) * half
    theirs = row * half
    first, second, third = [], [], []
    for k in range(PIECES):
        at = pl.multiple_of(theirs + k * piece, piece)
        copy = pltpu.make_async_remote_copy(
            part.at[pl.ds(at, piece)], got_row.at[pl.ds(k * piece, piece)],
            send.at[0, k], recv.at[0, k], device_id={"row": row}, device_id_type=MESH_ID)
        copy.start()
        first.append(copy)
    if extra is not None:
        over_row = pltpu.make_async_remote_copy(
            extra, got_extra.at[0], send.at[3, 0], recv.at[3, 0],
            device_id={"row": row}, device_id_type=MESH_ID)
        over_row.start()
    for k in range(PIECES):
        here = pl.ds(k * piece, piece)
        at = pl.multiple_of(own + k * piece, piece)
        first[k].wait_recv()
        mine[here, :] = (part[pl.ds(at, piece), :] + got_row[here, :]).astype(BF)
        copy = pltpu.make_async_remote_copy(
            mine.at[here], got_col.at[here], send.at[1, k], recv.at[1, k],
            device_id={"col": col}, device_id_type=MESH_ID)
        copy.start()
        second.append(copy)
    if extra is not None:
        over_row.wait_recv()
        pair[...] = extra[...] + got_extra[0]
        over_col = pltpu.make_async_remote_copy(
            pair, got_extra.at[1], send.at[3, 1], recv.at[3, 1],
            device_id={"col": col}, device_id_type=MESH_ID)
        over_col.start()
    for k in range(PIECES):
        here = pl.ds(k * piece, piece)
        at = pl.multiple_of(own + k * piece, piece)
        second[k].wait_recv()
        out[pl.ds(at, piece), :] = mine[here, :].astype(F32) + got_col[here, :].astype(F32)
        copy = pltpu.make_async_remote_copy(
            out.at[pl.ds(at, piece)], out.at[pl.ds(at, piece)], send.at[2, k], recv.at[2, k],
            device_id={"row": row}, device_id_type=MESH_ID)
        copy.start()
        third.append(copy)
    if extra is not None:
        over_col.wait_recv()
        extra_out[...] = pair[...] + got_extra[1]
        over_row.wait_send()
        over_col.wait_send()
    for k in range(PIECES):
        third[k].wait_recv()
        for copy in (first[k], second[k], third[k]):
            copy.wait_send()


def group_sum(part, extra=None):
    rows, width = part.shape
    half = rows // lax.axis_size("row")
    vmem = pl.BlockSpec(memory_space=pltpu.VMEM)
    out_shape = [jax.ShapeDtypeStruct((rows, width), F32)]
    scratch = [pltpu.VMEM((half, width), F32), pltpu.VMEM((half, width), BF),
               pltpu.VMEM((half, width), BF)]
    args = [part]
    if extra is not None:
        args.append(extra)
        out_shape.append(jax.ShapeDtypeStruct(extra.shape, F32))
        scratch += [pltpu.VMEM(extra.shape, F32), pltpu.VMEM((2,) + extra.shape, F32)]
    result = pl.pallas_call(
        reduce_body,
        out_shape=out_shape,
        in_specs=[vmem] * len(args),
        out_specs=[vmem] * len(out_shape),
        scratch_shapes=scratch + [
            pltpu.SemaphoreType.DMA((4, PIECES)), pltpu.SemaphoreType.DMA((4, PIECES))],
        compiler_params=pltpu.CompilerParams(
            collective_id=0 if extra is None else 2, has_side_effects=True),
        name="group_sum",
    )(*args)
    return result[0] if extra is None else result


def gather_body(x, cot, vec, x_out, cot_out, vec_out, send, recv):
    half, width = x.shape
    row, col = greet()
    my_rows = pl.ds(pl.multiple_of((1 - row) * half, half), half)
    my_cols = pl.ds(pl.multiple_of((1 - col) * width, width), width)
    their_cols = pl.ds(pl.multiple_of(col * width, width), width)
    every = pl.ds(0, vec.shape[0])
    jobs = [(x, x_out, my_rows), (vec, vec_out, every), (cot, cot_out, my_rows)]
    copies = []
    first = []
    for k, (own, out, rows) in enumerate(jobs):
        copy = pltpu.make_async_remote_copy(
            own, out.at[rows, my_cols], send.at[0, k], recv.at[0, k],
            device_id={"col": col}, device_id_type=MESH_ID)
        copy.start()
        first.append(copy)
    for k, (own, out, rows) in enumerate(jobs):
        if rows is my_rows:
            copy = pltpu.make_async_remote_copy(
                own, out.at[rows, my_cols], send.at[1, k], recv.at[1, k],
                device_id={"row": row}, device_id_type=MESH_ID)
            copy.start()
            copies.append(copy)
    for own, out, rows in jobs:
        out[rows, my_cols] = own[...]
    for k, (own, out, rows) in enumerate(jobs):
        first[k].wait_recv()
        if rows is my_rows:
            copy = pltpu.make_async_remote_copy(
                out.at[rows, their_cols], out.at[rows, their_cols], send.at[2, k], recv.at[2, k],
                device_id={"row": row}, device_id_type=MESH_ID)
            copy.start()
            copies.append(copy)
    for copy in copies:
        copy.wait_recv()
    for copy in first + copies:
        copy.wait_send()


def group_gather(x, cot, vec):
    half, width = x.shape
    rows, wide = half * lax.axis_size("row"), width * lax.axis_size("col")
    vmem = pl.BlockSpec(memory_space=pltpu.VMEM)
    return pl.pallas_call(
        gather_body,
        out_shape=[
            jax.ShapeDtypeStruct((rows, wide), x.dtype),
            jax.ShapeDtypeStruct((rows, wide), cot.dtype),
            jax.ShapeDtypeStruct((vec.shape[0], wide), vec.dtype),
        ],
        in_specs=[vmem] * 3,
        out_specs=[vmem] * 3,
        scratch_shapes=[pltpu.SemaphoreType.DMA((3, 3)), pltpu.SemaphoreType.DMA((3, 3))],
        compiler_params=pltpu.CompilerParams(collective_id=1, has_side_effects=True),
        name="group_gather",
    )(x, cot, vec)


def make_scores(query, key, allowed):
    scores = jnp.einsum("hqd,hkd->hqk", query, key, preferred_element_type=F32) * SCALE
    return jnp.where(allowed[None], scores, NEG)


def swap_col(value):
    return lax.ppermute(value, "col", [(0, 1), (1, 0)])


def columns_whole(own, gate):
    col = lax.axis_index("col")
    depth, width = own.shape[1], own.shape[2] // 2
    later = (gate.reshape(-1)[0].astype(F32) * 0.0).astype(jnp.int32)
    got = swap_col(lax.dynamic_slice_in_dim(own, (1 - col) * width + later, width, 2))
    kept = lax.dynamic_slice_in_dim(own, col * width, width, 2)
    low = jnp.where(col == 0, kept, got)
    high = jnp.where(col == 0, got, kept)
    return jnp.concatenate([low, high], axis=1)


def rows_whole(grad):
    col = lax.axis_index("col")
    depth = grad.shape[0] // 2
    got = swap_col(lax.dynamic_slice_in_dim(grad, (1 - col) * depth, depth, 0))
    kept = lax.dynamic_slice_in_dim(grad, col * depth, depth, 0)
    low = jnp.where(col == 0, kept, got)
    high = jnp.where(col == 0, got, kept)
    return jnp.concatenate([low, high], axis=1)


def forward_layer(state, allowed, cosine, sine, params):
    gain1, bias1, gain2, bias2, w_qkv, b_qkv, w_up, b_up, w_out, w_down, b_both = params
    width = state.shape[1]
    mean = jnp.sum(state, axis=1, keepdims=True) / width
    squares = jnp.sum(state * state, axis=1, keepdims=True) / width
    inverse = lax.rsqrt(squares - mean * mean + EPS)
    normed = (state - mean) * inverse
    first = (normed * gain1 + bias1).astype(BF)
    second = (normed * gain2 + bias2).astype(BF)
    rows = state.shape[0]
    qkv = (jnp.dot(first, w_qkv, preferred_element_type=F32) + b_qkv).reshape(rows, -1, 3, HD)
    query = rotate(qkv[:, :, 0], cosine, sine).astype(BF).transpose(1, 0, 2)
    key = rotate(qkv[:, :, 1], cosine, sine).astype(BF).transpose(1, 0, 2)
    value = qkv[:, :, 2].astype(BF).transpose(1, 0, 2)
    scores = make_scores(query, key, allowed)
    top = jnp.max(scores, axis=-1, keepdims=True)
    lse = top + jnp.log(jnp.sum(jnp.exp(scores - top), axis=-1, keepdims=True))
    probs = jnp.exp(scores - lse).astype(BF)
    mixed = jnp.einsum("hqk,hkd->qhd", probs, value, preferred_element_type=F32)
    mixed = mixed.astype(BF).reshape(rows, -1)
    up = jnp.dot(second, w_up, preferred_element_type=F32) + b_up
    act = gelu_exact(up).astype(BF)
    part = jnp.dot(mixed, w_out, preferred_element_type=F32) + jnp.dot(
        act, w_down, preferred_element_type=F32)
    return part, (normed, inverse, first, second, query, key, value, mixed, lse, up, act)


def backward_layer(grad, allowed, cosine, sine, params, cache):
    gain1, bias1, gain2, bias2, w_qkv, b_qkv, w_up, b_up, w_out, w_down, b_both = params
    normed, inverse, first, second, query, key, value, mixed, lse, up, act = cache
    rows, width = grad.shape
    grad_b = grad.astype(BF)
    g_bout = jnp.sum(grad, axis=0)
    grad_mixed = jnp.einsum("td,kd->tk", grad_b, w_out, preferred_element_type=F32).astype(BF)
    grad_act = jnp.einsum("td,kd->tk", grad_b, w_down, preferred_element_type=F32)
    grad_up = grad_act * gelu_slope(up)
    g_bup = jnp.sum(grad_up, axis=0)
    grad_up_b = grad_up.astype(BF)
    scores = make_scores(query, key, allowed)
    probs = jnp.exp(scores - lse)
    grad_heads = grad_mixed.reshape(rows, -1, HD).transpose(1, 0, 2)
    mixed_heads = mixed.reshape(rows, -1, HD).transpose(1, 0, 2)
    delta = jnp.sum(grad_heads.astype(F32) * mixed_heads.astype(F32), axis=-1, keepdims=True)
    grad_value = jnp.einsum("hqk,hqd->khd", probs.astype(BF), grad_heads, preferred_element_type=F32)
    grad_probs = jnp.einsum("hqd,hkd->hqk", grad_heads, value, preferred_element_type=F32)
    grad_scores = (probs * (grad_probs - delta) * SCALE).astype(BF)
    grad_query = jnp.einsum("hqk,hkd->qhd", grad_scores, key, preferred_element_type=F32)
    grad_key = jnp.einsum("hqk,hqd->khd", grad_scores, query, preferred_element_type=F32)
    grad_query = unrotate(grad_query, cosine, sine)
    grad_key = unrotate(grad_key, cosine, sine)
    grad_qkv = jnp.stack([grad_query, grad_key, grad_value], axis=2).reshape(rows, -1)
    g_bqkv = jnp.sum(grad_qkv, axis=0)
    grad_qkv_b = grad_qkv.astype(BF)
    part_first = jnp.einsum("tn,dn->td", grad_qkv_b, w_qkv, preferred_element_type=F32)
    part_second = jnp.einsum("tn,dn->td", grad_up_b, w_up, preferred_element_type=F32)
    part = part_first * gain1 + part_second * gain2
    g_wout = jnp.einsum("tk,td->kd", mixed, grad_b, preferred_element_type=F32)
    g_wdown = jnp.einsum("tk,td->kd", act, grad_b, preferred_element_type=F32)
    g_wqkv = jnp.einsum("td,tn->dn", first, grad_qkv_b, preferred_element_type=F32)
    g_wup = jnp.einsum("td,tn->dn", second, grad_up_b, preferred_element_type=F32)
    shares = lax.axis_size("row") * lax.axis_size("col")
    narrow = jnp.concatenate([
        jnp.stack([
            jnp.sum(part_first * normed, axis=0), jnp.sum(part_first, axis=0),
            jnp.sum(part_second * normed, axis=0), jnp.sum(part_second, axis=0),
            g_bout / shares,
        ]),
        jnp.zeros((3, width), F32),
    ])
    grad_norm, narrow = group_sum(part, narrow)
    centred = (
        grad_norm
        - jnp.sum(grad_norm, axis=1, keepdims=True) / width
        - normed * (jnp.sum(grad_norm * normed, axis=1, keepdims=True) / width)
    )
    grad_x = grad + inverse * centred
    heavy = (g_wqkv.astype(BF), g_wup.astype(BF), g_wout.astype(BF), g_wdown.astype(BF))
    return grad_x, heavy, (g_bqkv, g_bup), narrow


def per_device_plain(
    x_in, cotangent, segment_ids, norm1_gain, norm1_bias, norm2_gain, norm2_bias,
    w_qkv, b_qkv, w_up, b_up, w_out, b_out, w_down, b_down,
):
    half, part_width = x_in.shape
    row = lax.axis_index("row")
    col = lax.axis_index("col")
    length = segment_ids.shape[1]
    layers = w_qkv.shape[0]
    cosine, sine = rope_tables(length)
    places = jnp.arange(length, dtype=jnp.int32)
    labels = segment_ids[0]
    allowed = (places[:, None] >= places[None, :]) & (labels[:, None] == labels[None, :])
    vec = jnp.stack([norm1_gain, norm1_bias, norm2_gain, norm2_bias, b_out + b_down])
    vec = vec.reshape(-1, part_width)
    pad = -vec.shape[0] % 8
    state_in, cot, vec = group_gather(x_in, cotangent.astype(BF), jnp.pad(vec, ((0, pad), (0, 0))))
    grad_in = cot.astype(F32)
    vectors = vec[: vec.shape[0] - pad].reshape(5, layers, -1)
    wide_qkv, wide_up, gate = [], [], vec
    for l in range(layers):
        wide_qkv.append(columns_whole(w_qkv[l : l + 1], gate)[0])
        wide_up.append(columns_whole(w_up[l : l + 1], gate)[0])
        gate = wide_qkv[-1]

    def own(whole):
        return lax.dynamic_slice(whole, (row * half, col * part_width), (half, part_width))

    params = [
        (vectors[0, l], vectors[1, l], vectors[2, l], vectors[3, l], wide_qkv[l], b_qkv[l],
         wide_up[l], b_up[l], w_out[l], w_down[l], vectors[4, l])
        for l in range(layers)
    ]
    state = state_in
    caches = []
    for layer in range(layers):
        part, cache = forward_layer(state, allowed, cosine, sine, params[layer])
        caches.append(cache)
        if layer < layers - 1:
            state = state + group_sum(part) + params[layer][-1]
    y_base = x_in + own(state - state_in + params[-1][-1])
    grad = grad_in
    heavy = [None] * layers
    thin = [None] * layers
    narrow = [None] * layers
    for layer in reversed(range(layers)):
        grad, heavy[layer], thin[layer], narrow[layer] = backward_layer(
            grad, allowed, cosine, sine, params[layer], caches[layer])
    x_grad = cotangent + own(grad - grad_in)
    y_out = y_base + own(group_sum(part))
    summed = []
    for layer in range(layers):
        a, b, c, d = heavy[layer]
        summed.append(lax.psum((rows_whole(a), rows_whole(b), c, d), "dp"))
    g_bqkv, g_bup, narrow = lax.psum((
        jnp.stack([t[0] for t in thin]), jnp.stack([t[1] for t in thin]),
        jnp.stack([t[:5] for t in narrow])), "dp")
    g_wqkv, g_wup, g_wout, g_wdown = (
        jnp.stack([h[k] for h in summed]).astype(F32) for k in range(4))
    narrow = lax.dynamic_slice_in_dim(narrow, col * part_width, part_width, 2)
    g_bout = narrow[:, 4]
    return (
        y_out, x_grad, narrow[:, 0], narrow[:, 1], narrow[:, 2], narrow[:, 3],
        g_wqkv, g_bqkv, g_wup, g_bup, g_wout, g_bout, g_wdown, g_bout,
    )


BLK = 128


def tdot(a, b):
    return lax.dot_general(a, b, (((0,), (0,)), ((), ())), preferred_element_type=F32)


def ntdot(a, b):
    return lax.dot_general(a, b, (((1,), (1,)), ((), ())), preferred_element_type=F32)


def ndot(a, b):
    return jnp.dot(a, b, preferred_element_type=F32)


def whole_body(
    n, x, cot, seg, n1g, n1b, n2g, n2b, bq, bu, bo, bd, cosr, sinr, wq_in, wu_in, wo_in, wd_in,
    y, xg, odp, odm, ou, oq, osm,
    wq, wu, wo, wd, xb, cb, vec, mask, st, nrm, inv, fst, snd, act, slope, qkv_t, qh, p_t, m_t,
    gm_t, gub, gqb_t, gq, gb, own, sb, got_row, mine, got_col, back, back_got,
    idp, idm, iu, iq, ism, rdp, rdm, ru, rq, rsm, swu, swq,
    nar, nar_got, thin, send, recv, local,
):
    layers = wq.shape[0]
    gq_t = qkv_t
    half, cols = x.shape
    length, width = half * 2, cols * 2
    hid = wu.shape[2]
    heads = p_t.shape[1]
    qw = heads * 3 * HD
    row, col, here = lax.axis_index("row"), lax.axis_index("col"), lax.axis_index("dp")
    orow, ocol = 1 - row, 1 - col
    odd = lax.rem(here, 2)
    pos = here // 2 + odd * (n - 1 - 2 * (here // 2))

    def device(place):
        late = place // (n // 2)
        return 2 * (place + late * (n - 1 - 2 * place)) + late

    targets = (device(lax.rem(pos + 1, n)), device(lax.rem(pos + n - 1, n)))
    barrier = pltpu.get_barrier_semaphore()
    pl.semaphore_signal(barrier, inc=1, device_id={"dp": targets[0]}, device_id_type=MESH_ID)
    pl.semaphore_signal(barrier, inc=1, device_id={"dp": targets[1]}, device_id_type=MESH_ID)
    pl.semaphore_signal(barrier, inc=1, device_id={"col": ocol}, device_id_type=MESH_ID)
    pl.semaphore_signal(barrier, inc=1, device_id={"row": orow}, device_id_type=MESH_ID)

    count = [0]
    sent = []

    def rc(src, dst, axis, target):
        k = count[0]
        count[0] += 1
        copy = pltpu.make_async_remote_copy(
            src, dst, send.at[k], recv.at[k], device_id={axis: target}, device_id_type=MESH_ID)
        copy.start()
        sent.append(copy)
        return copy

    def over_row(src, dst):
        return rc(src, dst, "row", orow)

    def over_col(src, dst):
        return rc(src, dst, "col", ocol)

    def at(base, size, step=None):
        return pl.ds(pl.multiple_of(base, step or size), size)

    my_rows, their_rows = at(row * half, half), at(orow * half, half)
    my_cols, their_cols = at(col * cols, cols), at(ocol * cols, cols)
    shift = wq_in.shape[2] - wq.shape[2]
    my_heads, their_heads = at(col * shift, wq.shape[2], BLK), at(ocol * shift, wq.shape[2], BLK)
    my_hid, their_hid = at(col * hid, hid), at(ocol * hid, hid)

    loads = []
    for l in range(layers):
        loads.append([
            pltpu.make_async_copy(wq_in.at[l, :, my_heads], wq.at[l, my_cols], local.at[l, 0]),
            pltpu.make_async_copy(wu_in.at[l, :, my_hid], wu.at[l, my_cols], local.at[l, 1]),
            pltpu.make_async_copy(wo_in.at[l], wo.at[l], local.at[l, 2]),
            pltpu.make_async_copy(wd_in.at[l], wd.at[l], local.at[l, 3]),
        ])
        for copy in loads[-1]:
            copy.start()

    xb[my_rows, my_cols] = x[...].astype(BF)
    cb[my_rows, my_cols] = cot[...].astype(BF)
    for k, ref in enumerate((n1g, n1b, n2g, n2b)):
        vec[2 * k : 2 * k + 2, my_cols] = ref[...]
    vec[8:10, my_cols] = bo[...] + bd[...]
    pl.semaphore_wait(barrier, 4)

    x_col = over_col(xb.at[my_rows, my_cols], xb.at[my_rows, my_cols])
    x_row = over_row(xb.at[my_rows, my_cols], xb.at[my_rows, my_cols])
    v_col = over_col(vec.at[:, my_cols], vec.at[:, my_cols])

    def weight_q(l):
        return over_col(wq_in.at[l, :, their_heads], wq.at[l, my_cols])

    def weight_u(l):
        return over_col(wu_in.at[l, :, their_hid], wu.at[l, my_cols])

    w_q, w_u = [weight_q(0)], [weight_u(0)]
    c_row = over_row(cb.at[my_rows, my_cols], cb.at[my_rows, my_cols])

    label = seg[...].astype(F32)
    tall = jnp.broadcast_to(label, (BLK, length)).T
    for k in range(length // BLK):
        here_rows = slice(k * BLK, (k + 1) * BLK)
        key_at = lax.broadcasted_iota(jnp.int32, (BLK, length), 0) + k * BLK
        query_at = lax.broadcasted_iota(jnp.int32, (BLK, length), 1)
        same = tall[here_rows, 0:1] == label
        mask[here_rows, :] = jnp.where(same & (key_at <= query_at), 0.0, NEG)
    nar[...] = jnp.zeros_like(nar)
    offset = col * (wq.shape[2] - qw)

    x_col.wait_recv()
    x_over = over_row(xb.at[my_rows, their_cols], xb.at[my_rows, their_cols])
    v_col.wait_recv()
    x_row.wait_recv()
    x_over.wait_recv()

    def gain(k, l):
        return vec[2 * k + l : 2 * k + l + 1, :]

    blocks = length // BLK

    def norm_step(l):
        @pl.loop(0, blocks)
        def _(i):
            rows = at(i * BLK, BLK)
            s = xb[rows, :].astype(F32) if l == 0 else st[rows, :]
            mean = jnp.sum(s, axis=1, keepdims=True) / width
            squares = jnp.sum(s * s, axis=1, keepdims=True) / width
            inverse = lax.rsqrt(squares - mean * mean + EPS)
            normed = (s - mean) * inverse
            inv[l, rows, :] = inverse
            nrm[l, rows, :] = normed.astype(BF)
            fst[l, rows, :] = (normed * gain(0, l) + gain(1, l)).astype(BF)
            snd[l, rows, :] = (normed * gain(2, l) + gain(3, l)).astype(BF)

    def qkv_step(l):
        @pl.loop(0, blocks)
        def _(i):
            rows = at(i * BLK, BLK)
            got = ndot(fst[l, rows, :], wq[l]) + bq[l : l + 1, :]
            qkv_t[:, rows] = got.T

    def turn(v, sign):
        a, b = v[0:8], v[8:16]
        c, s = cosr[...], sinr[...] * sign
        return jnp.concatenate([a * c - b * s, b * c + a * s, v[16:]], axis=0)

    QB = length // 2

    def attention_step(l):
        @pl.loop(0, heads)
        def _(h):
            base = offset + h * (3 * HD)
            q = turn(qkv_t[at(base, HD), :], 1.0).astype(BF)
            k = turn(qkv_t[at(base + HD, HD), :], 1.0).astype(BF)
            v = qkv_t[at(base + 2 * HD, HD), :].astype(BF)
            spot = h * (3 * HD)
            qh[l, at(spot, HD), :] = q
            qh[l, at(spot + HD, HD), :] = k
            qh[l, at(spot + 2 * HD, HD), :] = v
            q = q * jnp.asarray(SCALE, BF)
            for b in range(2):
                keys, these = slice(0, (b + 1) * QB), slice(b * QB, (b + 1) * QB)
                scores = tdot(k[:, keys], q[:, these]) + mask[keys, these]
                top = jnp.max(scores, axis=0, keepdims=True)
                e = jnp.exp(scores - top)
                total = jnp.sum(e, axis=0, keepdims=True)
                probs = (e * (1.0 / total)).astype(BF)
                p_t[l, h, keys, these] = probs
                m_t[l, at(h * HD, HD), these] = ndot(v[:, keys], probs).astype(BF)

    def up_step(l):
        @pl.loop(0, blocks)
        def _(i):
            rows = at(i * BLK, BLK)
            up = ndot(snd[l, rows, :], wu[l]) + bu[l : l + 1, :]
            phi = 0.5 * (1.0 + lax.erf(up * INV_ROOT2))
            act[l, rows, :] = (up * phi).astype(BF)
            slope[l, rows, :] = (phi + up * jnp.exp(-0.5 * up * up) * INV_ROOT_TWO_PI).astype(BF)

    def part_rows(l):
        def run(base):
            rows = at(base, BLK)
            return tdot(m_t[l, :, rows], wo[l]) + ndot(act[l, rows, :], wd[l])
        return run

    pieces = half // BLK

    def sum_begin(k, fn):
        flight = []
        for p in range(pieces):
            here = slice(p * BLK, (p + 1) * BLK)
            sb[k, here, :] = fn(orow * half + p * BLK).astype(BF)
            flight.append(over_row(sb.at[k, here], got_row.at[k, here]))
        for p in range(pieces):
            here = slice(p * BLK, (p + 1) * BLK)
            own[k % 2, here, :] = fn(row * half + p * BLK)
        return flight

    def sum_cross(k, flight, narrow=False):
        crossing = []
        for p in range(pieces):
            here = slice(p * BLK, (p + 1) * BLK)
            flight[p].wait_recv()
            t = own[k % 2, here, :] + got_row[k, here, :].astype(F32)
            own[k % 2, here, :] = t
            mine[k, here, :] = t.astype(BF)
            if narrow:
                crossing.append(over_col(
                    mine.at[k, here, their_cols], got_col.at[k, here, their_cols]))
            else:
                crossing.append(over_col(mine.at[k, here], got_col.at[k, here]))
        return crossing


    norm_step(0)
    loads[0][0].wait()
    w_q[0].wait_recv()
    qkv_step(0)
    w_q.append(weight_q(1))
    c_col = over_col(cb.at[my_rows, my_cols], cb.at[my_rows, my_cols])
    attention_step(0)
    loads[0][1].wait()
    w_u[0].wait_recv()
    up_step(0)
    loads[0][2].wait()
    loads[0][3].wait()
    flight = sum_begin(0, part_rows(0))
    crossing = sum_cross(0, flight)
    w_u.append(weight_u(1))
    c_col.wait_recv()
    c_over = over_row(cb.at[my_rows, their_cols], cb.at[my_rows, their_cols])
    both = vec[8:9, :]
    returned = []
    for p in range(pieces):
        here = slice(p * BLK, (p + 1) * BLK)
        crossing[p].wait_recv()
        total = own[0, here, :] + got_col[0, here, :].astype(F32)
        own[0, here, :] = total
        back[0, here, :] = total.astype(BF)
        returned.append(over_row(back.at[0, here], back_got.at[0, here]))
    for p in range(pieces):
        here = slice(p * BLK, (p + 1) * BLK)
        rows = at(row * half + p * BLK, BLK)
        st[rows, :] = xb[rows, :].astype(F32) + own[0, here, :] + both
    y[...] = x[...] + own[0, :, my_cols] + vec[8:9, my_cols] + vec[9:10, my_cols]
    for p in range(pieces):
        here = slice(p * BLK, (p + 1) * BLK)
        returned[p].wait_recv()
        rows = at(orow * half + p * BLK, BLK)
        st[rows, :] = xb[rows, :].astype(F32) + back_got[0, here, :].astype(F32) + both

    norm_step(1)
    loads[1][0].wait()
    w_q[1].wait_recv()
    qkv_step(1)
    attention_step(1)
    loads[1][1].wait()
    w_u[1].wait_recv()
    up_step(1)
    loads[1][2].wait()
    loads[1][3].wait()

    def chunk(d, behind):
        sign = 1 if d == 0 else -1
        return lax.rem(pos - sign * behind + 2 * n, n)

    def stream(d, rin, got, out, swap=None):
        def go(src, dst):
            return rc(src, dst, "dp", targets[d])
        copy = go(rin(chunk(d, 0)), got(0))
        for s in range(n - 1):
            yield
            copy.wait_recv()
            got(s)[...] = got(s)[...] + rin(chunk(d, s + 1))[...]
            if s < n - 2:
                copy = go(got(s), got(s + 1))
        last, where = got(n - 2), chunk(d, n - 1)
        if swap is None:
            out(where)[...] = last[...]
        else:
            over = over_col(last.at[ocol], swap)
            out(where).at[col][...] = last[col]
            yield
            over.wait_recv()
            out(where).at[ocol][...] = swap[...]
        copy = go(out(where), out(where))
        for s in range(n - 1):
            yield
            copy.wait_recv()
            if s < n - 2:
                where = chunk(d, s)
                copy = go(out(where), out(where))

    active = []

    def launch(*args, **kw):
        g = stream(*args, **kw)
        next(g)
        active.append(g)

    def pump(times=1):
        for _ in range(times):
            for g in list(active):
                try:
                    next(g)
                except StopIteration:
                    active.remove(g)

    def down_step(l, g):
        for k in range(2):
            f = slice(k * (hid // 2), (k + 1) * (hid // 2))
            got = tdot(act[l, :, f], g[...]).astype(BF)
            got = got.reshape(n // 2, hid // n, width)
            cut = idp.shape[2]
            idp[l, k * (n // 2) : (k + 1) * (n // 2)] = got[:, :cut]
            idm[l, k * (n // 2) : (k + 1) * (n // 2), 0 : hid // n - cut] = got[:, cut:]
        got = ndot(m_t[l], g[...]).reshape(n, -1, width)
        pad = idm.shape[2] - (hid // n - cut) - got.shape[1]
        got = jnp.concatenate([got, jnp.zeros((n, pad, width), F32)], axis=1)
        idm[l, :, hid // n - cut :] = got.astype(BF)
        launch(0, lambda c: idp.at[l, c], lambda s: rdp.at[l, s], lambda c: odp.at[l, c])
        launch(1, lambda c: idm.at[l, c], lambda s: rdm.at[l, s], lambda c: odm.at[l, c])

    def up_grad_step(l):
        for k in range(2):
            f = slice(k * cols, (k + 1) * cols)
            got = tdot(snd[l, :, f], gub[...]).astype(BF)
            iu[l, :, k] = got.reshape(n, -1, hid)
        launch(0, lambda c: iu.at[l, c], lambda s: ru.at[l, s], lambda c: ou.at[l, c], swap=swu.at[l])

    def qkv_grad_step(l):
        for k in range(2):
            f = slice(k * cols, (k + 1) * cols)
            got = ntdot(fst[l, :, f].T, gqb_t[...]).astype(BF)
            iq[l, :, k] = got.reshape(n, -1, qw)
        launch(1, lambda c: iq.at[l, c], lambda s: rq.at[l, s], lambda c: oq.at[l, c], swap=swq.at[l])

    def grad_up_step(l, g):
        def block(i, total):
            rows = at(i * BLK, BLK)
            gu = ntdot(g[rows, :], wd[l]) * slope[l, rows, :].astype(F32)
            gub[rows, :] = gu.astype(BF)
            return total + jnp.sum(gu, axis=0, keepdims=True)
        total = lax.fori_loop(0, blocks, block, jnp.zeros((1, hid), F32))
        thin[l, 1:2, 0:hid] = total

    def attention_back_step(l, g):
        gm_t[...] = ntdot(wo[l], g[...]).astype(BF)

        @pl.loop(0, heads)
        def _(h):
            spot = h * (3 * HD)
            q = qh[l, at(spot, HD), :]
            k = qh[l, at(spot + HD, HD), :]
            v = qh[l, at(spot + 2 * HD, HD), :]
            gm = gm_t[at(h * HD, HD), :]
            mixed = m_t[l, at(h * HD, HD), :]
            delta = jnp.sum(gm.astype(F32) * mixed.astype(F32), axis=0, keepdims=True)
            gqs, gks, gvs = [], [], []
            for b in range(2):
                keys, these = slice(0, (b + 1) * QB), slice(b * QB, (b + 1) * QB)
                probs = p_t[l, h, keys, these]
                gp = tdot(v[:, keys], gm[:, these])
                ds = (probs.astype(F32) * (gp - delta[:, these])).astype(BF)
                gqs.append(ndot(k[:, keys], ds))
                gks.append(ntdot(q[:, these], ds))
                gvs.append(ntdot(gm[:, these], probs))
            gq_h = jnp.concatenate(gqs, axis=1) * SCALE
            gk_h = jnp.concatenate([gks[0] + gks[1][:, :QB], gks[1][:, QB:]], axis=1) * SCALE
            gv_h = jnp.concatenate([gvs[0] + gvs[1][:, :QB], gvs[1][:, QB:]], axis=1)
            base = offset + spot
            for k3, value in enumerate((turn(gq_h, -1.0), turn(gk_h, -1.0), gv_h)):
                gq_t[at(base + k3 * HD, HD), :] = value
                gqb_t[at(spot + k3 * HD, HD), :] = value.astype(BF)

        total = jnp.zeros((1, gq_t.shape[0]), F32)
        for i in range(blocks):
            flat = gq_t[:, i * BLK : (i + 1) * BLK].T
            gq[i * BLK : (i + 1) * BLK, :] = flat.astype(BF)
            total = total + jnp.sum(flat, axis=0, keepdims=True)
        thin[l, 0:1, 0 : gq_t.shape[0]] = total

    def back_rows(l):
        def run(base):
            rows = at(base, BLK)
            gf = ntdot(gq[rows, :], wq[l])
            gs = ntdot(gub[rows, :], wu[l])
            normed = nrm[l, rows, :].astype(F32)
            for k, value in enumerate((gf * normed, gf, gs * normed, gs)):
                nar[l, 0, k : k + 1, :] += jnp.sum(value, axis=0, keepdims=True)
            return gf * gain(0, l) + gs * gain(2, l)
        return run

    def centred(l, rows, total):
        normed = nrm[l, rows, :].astype(F32)
        return inv[l, rows, :] * (
            total - jnp.sum(total, axis=1, keepdims=True) / width
            - normed * (jnp.sum(total * normed, axis=1, keepdims=True) / width))

    gq_t[...] = jnp.zeros_like(gq_t)
    shares = 0.25
    c_row.wait_recv()
    c_over.wait_recv()
    nar[1, 0, 4:5, :] = jnp.sum(cb[...].astype(F32), axis=0, keepdims=True) * shares
    down_step(1, cb)
    grad_up_step(1, cb)
    attention_back_step(1, cb)
    pump()
    flight = sum_begin(1, back_rows(1))
    nar_row = over_row(nar.at[1, 0], nar_got.at[1, 0])
    crossing = sum_cross(1, flight)
    pump()
    up_grad_step(1)
    returned = []
    for p in range(pieces):
        here = slice(p * BLK, (p + 1) * BLK)
        crossing[p].wait_recv()
        total = own[1, here, :] + got_col[1, here, :].astype(F32)
        own[1, here, :] = total
        back[1, here, :] = total.astype(BF)
        returned.append(over_row(back.at[1, here], back_got.at[1, here]))
    bout = jnp.zeros((1, width), F32)
    for p in range(pieces):
        here = slice(p * BLK, (p + 1) * BLK)
        rows = at(row * half + p * BLK, BLK)
        change = centred(1, rows, own[1, here, :])
        own[1, here, :] = change
        grad = cb[rows, :].astype(F32) + change
        gb[rows, :] = grad.astype(BF)
        bout = bout + jnp.sum(grad, axis=0, keepdims=True)
    xg[...] = cot[...] + own[1, :, my_cols]
    for p in range(pieces):
        here = slice(p * BLK, (p + 1) * BLK)
        returned[p].wait_recv()
        rows = at(orow * half + p * BLK, BLK)
        grad = cb[rows, :].astype(F32) + centred(1, rows, back_got[1, here, :].astype(F32))
        gb[rows, :] = grad.astype(BF)
        bout = bout + jnp.sum(grad, axis=0, keepdims=True)
    nar[0, 0, 4:5, :] = bout * shares
    nar_row.wait_recv()
    nar[1, 1] = nar[1, 0] + nar_got[1, 0]
    nar_col = over_col(nar.at[1, 1], nar_got.at[1, 1])
    qkv_grad_step(1)
    pump()
    down_step(0, gb)
    pump()
    grad_up_step(0, gb)
    pump()
    attention_back_step(0, gb)
    pump()
    flight_x = sum_begin(3, back_rows(0))
    nar_row0 = over_row(nar.at[0, 0], nar_got.at[0, 0])
    crossing_x = sum_cross(3, flight_x)
    nar_row0.wait_recv()
    nar[0, 1] = nar[0, 0] + nar_got[0, 0]
    nar_col0 = over_col(nar.at[0, 1], nar_got.at[0, 1])
    pump()
    up_grad_step(0)
    pump()
    qkv_grad_step(0)
    pump()
    nar_col.wait_recv()
    nar_col0.wait_recv()
    ism[...] = jnp.zeros_like(ism)
    ism[0] = jnp.concatenate(
        [v for l in range(layers) for v in (
            nar[l, 1, 0:5, :] + nar_got[l, 1, 0:5, :], thin[l, 0:2, :], jnp.zeros((1, width), F32))],
        axis=0).astype(BF)
    launch(0, lambda c: ism.at[c], lambda s: rsm.at[s], lambda c: osm.at[c])
    pump()
    flight_y = sum_begin(2, part_rows(1))
    crossing_y = sum_cross(2, flight_y, narrow=True)
    pump()
    for p in range(pieces):
        here = slice(p * BLK, (p + 1) * BLK)
        crossing_x[p].wait_recv()
        rows = at(row * half + p * BLK, BLK)
        own[1, here, :] = centred(0, rows, own[1, here, :] + got_col[3, here, :].astype(F32))
    xg[...] += own[1, :, my_cols]
    pump()
    for p in range(pieces):
        crossing_y[p].wait_recv()
    y[...] += own[0, :, my_cols] + got_col[2, :, my_cols].astype(F32)
    while active:
        pump()
    for copy in sent:
        copy.wait_send()


def whole_step(x, cot, seg, n1g, n1b, n2g, n2b, wq_in, bq, wu_in, bu, wo_in, bo, wd_in, bd):
    n = lax.axis_size("dp")
    half, cols = x.shape
    layers, _, both_heads = wq_in.shape
    length, width = 2 * half, 2 * cols
    hid = wu_in.shape[2] // 2
    qw = both_heads // 2
    heads = qw // (3 * HD)
    wide = -(-qw // BLK) * BLK
    mix = wo_in.shape[1]
    col = lax.axis_index("col")
    cosine, sine = rope_tables(length)
    cosr, sinr = cosine[:, : ROT // 2].T, sine[:, : ROT // 2].T
    bq = lax.dynamic_update_slice(jnp.zeros((layers, wide), F32), bq, (0, col * (wide - qw)))
    per, deep, flat = width // 2 // n, hid // n, mix // n
    cut = deep // 2
    lower = deep - cut + flat
    lower += -lower % 16
    small = 8 * layers
    vmem = pl.BlockSpec(memory_space=pltpu.VMEM)
    anyw = pl.BlockSpec(memory_space=pl.ANY)
    V = pltpu.VMEM
    sums = 4
    sems = 256
    out = pl.pallas_call(
        lambda *refs: whole_body(n, *refs),
        out_shape=[
            jax.ShapeDtypeStruct((half, cols), F32), jax.ShapeDtypeStruct((half, cols), F32),
            jax.ShapeDtypeStruct((layers, n, cut, width), BF),
            jax.ShapeDtypeStruct((layers, n, lower, width), BF),
            jax.ShapeDtypeStruct((layers, n, 2, per, hid), BF),
            jax.ShapeDtypeStruct((layers, n, 2, per, qw), BF),
            jax.ShapeDtypeStruct((n, small, width), BF),
        ],
        in_specs=[vmem] * 13 + [anyw] * 4,
        out_specs=[vmem] * 7,
        scratch_shapes=[
            V((layers, width, wide), BF), V((layers, width, hid), BF),
            V((layers, mix, width), BF), V((layers, hid, width), BF),
            V((length, width), BF), V((length, width), BF), V((16, width), F32),
            V((length, length), F32), V((length, width), F32),
            V((layers, length, width), BF), V((layers, length, 1), F32),
            V((layers, length, width), BF), V((layers, length, width), BF),
            V((layers, length, hid), BF), V((layers, length, hid), BF),
            V((wide, length), F32), V((layers, qw, length), BF),
            V((layers, heads, length, length), BF), V((layers, mix, length), BF),
            V((mix, length), BF), V((length, hid), BF),
            V((qw, length), BF), V((length, wide), BF), V((length, width), BF),
            V((2, half, width), F32), V((sums, half, width), BF), V((sums, half, width), BF),
            V((sums, half, width), BF), V((sums, half, width), BF),
            V((2, half, width), BF), V((2, half, width), BF),
            V((layers, n, cut, width), BF), V((layers, n, lower, width), BF),
            V((layers, n, 2, per, hid), BF), V((layers, n, 2, per, qw), BF),
            V((n, small, width), BF),
            V((layers, n - 1, cut, width), BF), V((layers, n - 1, lower, width), BF),
            V((layers, n - 1, 2, per, hid), BF), V((layers, n - 1, 2, per, qw), BF),
            V((n - 1, small, width), BF),
            V((layers, per, hid), BF), V((layers, per, qw), BF),
            V((layers, 2, 8, width), F32), V((layers, 2, 8, width), F32),
            V((layers, 2, width), F32),
            pltpu.SemaphoreType.DMA((sems,)), pltpu.SemaphoreType.DMA((sems,)),
            pltpu.SemaphoreType.DMA((layers, 4)),
        ],
        compiler_params=pltpu.CompilerParams(
            collective_id=5, has_side_effects=True, vmem_limit_bytes=62 * 1024 * 1024),
        name="whole_step",
    )(x, cot, seg, n1g, n1b, n2g, n2b, bq, bu, bo, bd, cosr, sinr, wq_in, wu_in, wo_in, wd_in)
    y, xg, dp, dm, u, q, s = out
    g_wqkv = q.transpose(0, 1, 3, 2, 4).reshape(layers, width // 2, 2 * qw).astype(F32)
    g_wup = u.transpose(0, 1, 3, 2, 4).reshape(layers, width // 2, 2 * hid).astype(F32)
    g_wdown = jnp.concatenate([dp, dm[:, :, : deep - cut]], axis=2).reshape(layers, hid, width).astype(F32)
    g_wout = dm[:, :, deep - cut : deep - cut + flat].reshape(layers, mix, width).astype(F32)
    s = s[0].astype(F32).reshape(layers, 8, width)
    narrow = lax.dynamic_slice_in_dim(s[:, :5], col * cols, cols, 2)
    g_bqkv = lax.dynamic_slice_in_dim(s[:, 5], col * (wide - qw), qw, 1)
    g_bup = s[:, 6, :hid]
    g_bout = narrow[:, 4]
    return (
        y, xg, narrow[:, 0], narrow[:, 1], narrow[:, 2], narrow[:, 3],
        g_wqkv, g_bqkv, g_wup, g_bup, g_wout, g_bout, g_wdown, g_bout)


def per_device(*args):
    x, wq, wo, wd = args[0], args[7], args[11], args[13]
    n = lax.axis_size("dp")
    parts = lax.axis_size("row"), lax.axis_size("col")
    cols = x.shape[1]
    fits = (
        parts == (2, 2) and n % 2 == 0 and n >= 4 and cols % n == 0 and (cols // n) % 16 == 0
        and (wd.shape[1] // n) % 32 == 0 and (wo.shape[1] // n) % 8 == 0 and wq.shape[0] == 2)
    return whole_step(*args) if fits else per_device_plain(*args)


def solution(mesh):
    in_specs = (
        P(("dp", "row"), "col"),
        P(("dp", "row"), "col"),
        P("dp", None),
        P(None, "col"),
        P(None, "col"),
        P(None, "col"),
        P(None, "col"),
        P(None, "col", "row"),
        P(None, ("row", "col")),
        P(None, "col", "row"),
        P(None, ("row", "col")),
        P(None, ("row", "col"), None),
        P(None, "col"),
        P(None, ("row", "col"), None),
        P(None, "col"),
    )
    out_specs = (
        P(("dp", "row"), "col"),
        P(("dp", "row"), "col"),
        P(None, "col"),
        P(None, "col"),
        P(None, "col"),
        P(None, "col"),
        P(None, "col", "row"),
        P(None, ("row", "col")),
        P(None, "col", "row"),
        P(None, ("row", "col")),
        P(None, ("row", "col"), None),
        P(None, "col"),
        P(None, ("row", "col"), None),
        P(None, "col"),
    )
    return jax.shard_map(
        per_device, mesh=mesh, in_specs=in_specs, out_specs=out_specs, check_vma=False
    )
```

```python
import jax
import jax.numpy as jnp
import numpy as np
from jax import lax
from jax.experimental import pallas as pl
from jax.experimental.pallas import tpu as pltpu
from jax.sharding import PartitionSpec as P

D = 768
HD = 64
ROT = 16
LAYERS = 2


EPS = 1e-05
NEG = -1e30
SCALE = 0.125
INV_ROOT2 = 0.7071067811865476
INV_ROOT_TWO_PI = 0.3989422804014327


def rope_tables(length):
    half = ROT // 2
    freq = 10000.0 ** (-(jnp.arange(half, dtype=jnp.float32) * 2.0) / ROT)
    angle = jnp.arange(length, dtype=jnp.float32)[:, None] * freq[None, :]
    cosine = jnp.concatenate([jnp.cos(angle), jnp.cos(angle)], axis=1)
    sine = jnp.concatenate([jnp.sin(angle), jnp.sin(angle)], axis=1)
    return (cosine, sine)


def rotate(values, cosine, sine):
    part = values[..., :ROT]
    lower = part[..., : ROT // 2]
    upper = part[..., ROT // 2 :]
    turned = jnp.concatenate([-upper, lower], axis=-1)
    moved = part * cosine[:, None, :] + turned * sine[:, None, :]
    return jnp.concatenate([moved, values[..., ROT:]], axis=-1)


def unrotate(grads, cosine, sine):
    part = grads[..., :ROT]
    lower = part[..., : ROT // 2]
    upper = part[..., ROT // 2 :]
    turned = jnp.concatenate([upper, -lower], axis=-1)
    moved = part * cosine[:, None, :] + turned * sine[:, None, :]
    return jnp.concatenate([moved, grads[..., ROT:]], axis=-1)


def gelu_exact(values):
    return 0.5 * values * (1.0 + jax.scipy.special.erf(values * INV_ROOT2))


def gelu_slope(values):
    return (
        0.5 * (1.0 + jax.scipy.special.erf(values * INV_ROOT2))
        + values * jnp.exp(-0.5 * values * values) * INV_ROOT_TWO_PI
    )


BF = jnp.bfloat16
F32 = jnp.float32
MESH_ID = pl.DeviceIdType.MESH
PIECES = 4


def greet():
    row = 1 - lax.axis_index("row")
    col = 1 - lax.axis_index("col")
    barrier = pltpu.get_barrier_semaphore()
    pl.semaphore_signal(barrier, inc=1, device_id={"row": row}, device_id_type=MESH_ID)
    pl.semaphore_signal(barrier, inc=1, device_id={"col": col}, device_id_type=MESH_ID)
    pl.semaphore_wait(barrier, 2)
    return row, col


def reduce_body(*refs):
    if len(refs) == 7:
        part, out, got_row, mine, got_col, send, recv = refs
        extra = None
    else:
        part, extra, out, extra_out, got_row, mine, got_col, pair, got_extra, send, recv = refs
    half = mine.shape[0]
    piece = half // PIECES
    row, col = greet()
    own = (1 - row) * half
    theirs = row * half
    first, second, third = [], [], []
    for k in range(PIECES):
        at = pl.multiple_of(theirs + k * piece, piece)
        copy = pltpu.make_async_remote_copy(
            part.at[pl.ds(at, piece)], got_row.at[pl.ds(k * piece, piece)],
            send.at[0, k], recv.at[0, k], device_id={"row": row}, device_id_type=MESH_ID)
        copy.start()
        first.append(copy)
    if extra is not None:
        over_row = pltpu.make_async_remote_copy(
            extra, got_extra.at[0], send.at[3, 0], recv.at[3, 0],
            device_id={"row": row}, device_id_type=MESH_ID)
        over_row.start()
    for k in range(PIECES):
        here = pl.ds(k * piece, piece)
        at = pl.multiple_of(own + k * piece, piece)
        first[k].wait_recv()
        mine[here, :] = (part[pl.ds(at, piece), :] + got_row[here, :]).astype(BF)
        copy = pltpu.make_async_remote_copy(
            mine.at[here], got_col.at[here], send.at[1, k], recv.at[1, k],
            device_id={"col": col}, device_id_type=MESH_ID)
        copy.start()
        second.append(copy)
    if extra is not None:
        over_row.wait_recv()
        pair[...] = extra[...] + got_extra[0]
        over_col = pltpu.make_async_remote_copy(
            pair, got_extra.at[1], send.at[3, 1], recv.at[3, 1],
            device_id={"col": col}, device_id_type=MESH_ID)
        over_col.start()
    for k in range(PIECES):
        here = pl.ds(k * piece, piece)
        at = pl.multiple_of(own + k * piece, piece)
        second[k].wait_recv()
        out[pl.ds(at, piece), :] = mine[here, :].astype(F32) + got_col[here, :].astype(F32)
        copy = pltpu.make_async_remote_copy(
            out.at[pl.ds(at, piece)], out.at[pl.ds(at, piece)], send.at[2, k], recv.at[2, k],
            device_id={"row": row}, device_id_type=MESH_ID)
        copy.start()
        third.append(copy)
    if extra is not None:
        over_col.wait_recv()
        extra_out[...] = pair[...] + got_extra[1]
        over_row.wait_send()
        over_col.wait_send()
    for k in range(PIECES):
        third[k].wait_recv()
        for copy in (first[k], second[k], third[k]):
            copy.wait_send()


def group_sum(part, extra=None):
    rows, width = part.shape
    half = rows // lax.axis_size("row")
    vmem = pl.BlockSpec(memory_space=pltpu.VMEM)
    out_shape = [jax.ShapeDtypeStruct((rows, width), F32)]
    scratch = [pltpu.VMEM((half, width), F32), pltpu.VMEM((half, width), BF),
               pltpu.VMEM((half, width), BF)]
    args = [part]
    if extra is not None:
        args.append(extra)
        out_shape.append(jax.ShapeDtypeStruct(extra.shape, F32))
        scratch += [pltpu.VMEM(extra.shape, F32), pltpu.VMEM((2,) + extra.shape, F32)]
    result = pl.pallas_call(
        reduce_body,
        out_shape=out_shape,
        in_specs=[vmem] * len(args),
        out_specs=[vmem] * len(out_shape),
        scratch_shapes=scratch + [
            pltpu.SemaphoreType.DMA((4, PIECES)), pltpu.SemaphoreType.DMA((4, PIECES))],
        compiler_params=pltpu.CompilerParams(
            collective_id=0 if extra is None else 2, has_side_effects=True),
        name="group_sum",
    )(*args)
    return result[0] if extra is None else result


def gather_body(x, cot, vec, x_out, cot_out, vec_out, send, recv):
    half, width = x.shape
    row, col = greet()
    my_rows = pl.ds(pl.multiple_of((1 - row) * half, half), half)
    my_cols = pl.ds(pl.multiple_of((1 - col) * width, width), width)
    their_cols = pl.ds(pl.multiple_of(col * width, width), width)
    every = pl.ds(0, vec.shape[0])
    jobs = [(x, x_out, my_rows), (vec, vec_out, every), (cot, cot_out, my_rows)]
    copies = []
    first = []
    for k, (own, out, rows) in enumerate(jobs):
        copy = pltpu.make_async_remote_copy(
            own, out.at[rows, my_cols], send.at[0, k], recv.at[0, k],
            device_id={"col": col}, device_id_type=MESH_ID)
        copy.start()
        first.append(copy)
    for k, (own, out, rows) in enumerate(jobs):
        if rows is my_rows:
            copy = pltpu.make_async_remote_copy(
                own, out.at[rows, my_cols], send.at[1, k], recv.at[1, k],
                device_id={"row": row}, device_id_type=MESH_ID)
            copy.start()
            copies.append(copy)
    for own, out, rows in jobs:
        out[rows, my_cols] = own[...]
    for k, (own, out, rows) in enumerate(jobs):
        first[k].wait_recv()
        if rows is my_rows:
            copy = pltpu.make_async_remote_copy(
                out.at[rows, their_cols], out.at[rows, their_cols], send.at[2, k], recv.at[2, k],
                device_id={"row": row}, device_id_type=MESH_ID)
            copy.start()
            copies.append(copy)
    for copy in copies:
        copy.wait_recv()
    for copy in first + copies:
        copy.wait_send()


def group_gather(x, cot, vec):
    half, width = x.shape
    rows, wide = half * lax.axis_size("row"), width * lax.axis_size("col")
    vmem = pl.BlockSpec(memory_space=pltpu.VMEM)
    return pl.pallas_call(
        gather_body,
        out_shape=[
            jax.ShapeDtypeStruct((rows, wide), x.dtype),
            jax.ShapeDtypeStruct((rows, wide), cot.dtype),
            jax.ShapeDtypeStruct((vec.shape[0], wide), vec.dtype),
        ],
        in_specs=[vmem] * 3,
        out_specs=[vmem] * 3,
        scratch_shapes=[pltpu.SemaphoreType.DMA((3, 3)), pltpu.SemaphoreType.DMA((3, 3))],
        compiler_params=pltpu.CompilerParams(collective_id=1, has_side_effects=True),
        name="group_gather",
    )(x, cot, vec)


def make_scores(query, key, allowed):
    scores = jnp.einsum("hqd,hkd->hqk", query, key, preferred_element_type=F32) * SCALE
    return jnp.where(allowed[None], scores, NEG)


def swap_col(value):
    return lax.ppermute(value, "col", [(0, 1), (1, 0)])


def columns_whole(own, gate):
    col = lax.axis_index("col")
    depth, width = own.shape[1], own.shape[2] // 2
    later = (gate.reshape(-1)[0].astype(F32) * 0.0).astype(jnp.int32)
    got = swap_col(lax.dynamic_slice_in_dim(own, (1 - col) * width + later, width, 2))
    kept = lax.dynamic_slice_in_dim(own, col * width, width, 2)
    low = jnp.where(col == 0, kept, got)
    high = jnp.where(col == 0, got, kept)
    return jnp.concatenate([low, high], axis=1)


def rows_whole(grad):
    col = lax.axis_index("col")
    depth = grad.shape[0] // 2
    got = swap_col(lax.dynamic_slice_in_dim(grad, (1 - col) * depth, depth, 0))
    kept = lax.dynamic_slice_in_dim(grad, col * depth, depth, 0)
    low = jnp.where(col == 0, kept, got)
    high = jnp.where(col == 0, got, kept)
    return jnp.concatenate([low, high], axis=1)


def forward_layer(state, allowed, cosine, sine, params):
    gain1, bias1, gain2, bias2, w_qkv, b_qkv, w_up, b_up, w_out, w_down, b_both = params
    width = state.shape[1]
    mean = jnp.sum(state, axis=1, keepdims=True) / width
    squares = jnp.sum(state * state, axis=1, keepdims=True) / width
    inverse = lax.rsqrt(squares - mean * mean + EPS)
    normed = (state - mean) * inverse
    first = (normed * gain1 + bias1).astype(BF)
    second = (normed * gain2 + bias2).astype(BF)
    rows = state.shape[0]
    qkv = (jnp.dot(first, w_qkv, preferred_element_type=F32) + b_qkv).reshape(rows, -1, 3, HD)
    query = rotate(qkv[:, :, 0], cosine, sine).astype(BF).transpose(1, 0, 2)
    key = rotate(qkv[:, :, 1], cosine, sine).astype(BF).transpose(1, 0, 2)
    value = qkv[:, :, 2].astype(BF).transpose(1, 0, 2)
    scores = make_scores(query, key, allowed)
    top = jnp.max(scores, axis=-1, keepdims=True)
    lse = top + jnp.log(jnp.sum(jnp.exp(scores - top), axis=-1, keepdims=True))
    probs = jnp.exp(scores - lse).astype(BF)
    mixed = jnp.einsum("hqk,hkd->qhd", probs, value, preferred_element_type=F32)
    mixed = mixed.astype(BF).reshape(rows, -1)
    up = jnp.dot(second, w_up, preferred_element_type=F32) + b_up
    act = gelu_exact(up).astype(BF)
    part = jnp.dot(mixed, w_out, preferred_element_type=F32) + jnp.dot(
        act, w_down, preferred_element_type=F32)
    return part, (normed, inverse, first, second, query, key, value, mixed, lse, up, act)


def backward_layer(grad, allowed, cosine, sine, params, cache):
    gain1, bias1, gain2, bias2, w_qkv, b_qkv, w_up, b_up, w_out, w_down, b_both = params
    normed, inverse, first, second, query, key, value, mixed, lse, up, act = cache
    rows, width = grad.shape
    grad_b = grad.astype(BF)
    g_bout = jnp.sum(grad, axis=0)
    grad_mixed = jnp.einsum("td,kd->tk", grad_b, w_out, preferred_element_type=F32).astype(BF)
    grad_act = jnp.einsum("td,kd->tk", grad_b, w_down, preferred_element_type=F32)
    grad_up = grad_act * gelu_slope(up)
    g_bup = jnp.sum(grad_up, axis=0)
    grad_up_b = grad_up.astype(BF)
    scores = make_scores(query, key, allowed)
    probs = jnp.exp(scores - lse)
    grad_heads = grad_mixed.reshape(rows, -1, HD).transpose(1, 0, 2)
    mixed_heads = mixed.reshape(rows, -1, HD).transpose(1, 0, 2)
    delta = jnp.sum(grad_heads.astype(F32) * mixed_heads.astype(F32), axis=-1, keepdims=True)
    grad_value = jnp.einsum("hqk,hqd->khd", probs.astype(BF), grad_heads, preferred_element_type=F32)
    grad_probs = jnp.einsum("hqd,hkd->hqk", grad_heads, value, preferred_element_type=F32)
    grad_scores = (probs * (grad_probs - delta) * SCALE).astype(BF)
    grad_query = jnp.einsum("hqk,hkd->qhd", grad_scores, key, preferred_element_type=F32)
    grad_key = jnp.einsum("hqk,hqd->khd", grad_scores, query, preferred_element_type=F32)
    grad_query = unrotate(grad_query, cosine, sine)
    grad_key = unrotate(grad_key, cosine, sine)
    grad_qkv = jnp.stack([grad_query, grad_key, grad_value], axis=2).reshape(rows, -1)
    g_bqkv = jnp.sum(grad_qkv, axis=0)
    grad_qkv_b = grad_qkv.astype(BF)
    part_first = jnp.einsum("tn,dn->td", grad_qkv_b, w_qkv, preferred_element_type=F32)
    part_second = jnp.einsum("tn,dn->td", grad_up_b, w_up, preferred_element_type=F32)
    part = part_first * gain1 + part_second * gain2
    g_wout = jnp.einsum("tk,td->kd", mixed, grad_b, preferred_element_type=F32)
    g_wdown = jnp.einsum("tk,td->kd", act, grad_b, preferred_element_type=F32)
    g_wqkv = jnp.einsum("td,tn->dn", first, grad_qkv_b, preferred_element_type=F32)
    g_wup = jnp.einsum("td,tn->dn", second, grad_up_b, preferred_element_type=F32)
    shares = lax.axis_size("row") * lax.axis_size("col")
    narrow = jnp.concatenate([
        jnp.stack([
            jnp.sum(part_first * normed, axis=0), jnp.sum(part_first, axis=0),
            jnp.sum(part_second * normed, axis=0), jnp.sum(part_second, axis=0),
            g_bout / shares,
        ]),
        jnp.zeros((3, width), F32),
    ])
    grad_norm, narrow = group_sum(part, narrow)
    centred = (
        grad_norm
        - jnp.sum(grad_norm, axis=1, keepdims=True) / width
        - normed * (jnp.sum(grad_norm * normed, axis=1, keepdims=True) / width)
    )
    grad_x = grad + inverse * centred
    heavy = (g_wqkv.astype(BF), g_wup.astype(BF), g_wout.astype(BF), g_wdown.astype(BF))
    return grad_x, heavy, (g_bqkv, g_bup), narrow


def per_device_plain(
    x_in, cotangent, segment_ids, norm1_gain, norm1_bias, norm2_gain, norm2_bias,
    w_qkv, b_qkv, w_up, b_up, w_out, b_out, w_down, b_down,
):
    half, part_width = x_in.shape
    row = lax.axis_index("row")
    col = lax.axis_index("col")
    length = segment_ids.shape[1]
    layers = w_qkv.shape[0]
    cosine, sine = rope_tables(length)
    places = jnp.arange(length, dtype=jnp.int32)
    labels = segment_ids[0]
    allowed = (places[:, None] >= places[None, :]) & (labels[:, None] == labels[None, :])
    vec = jnp.stack([norm1_gain, norm1_bias, norm2_gain, norm2_bias, b_out + b_down])
    vec = vec.reshape(-1, part_width)
    pad = -vec.shape[0] % 8
    state_in, cot, vec = group_gather(x_in, cotangent.astype(BF), jnp.pad(vec, ((0, pad), (0, 0))))
    grad_in = cot.astype(F32)
    vectors = vec[: vec.shape[0] - pad].reshape(5, layers, -1)
    wide_qkv, wide_up, gate = [], [], vec
    for l in range(layers):
        wide_qkv.append(columns_whole(w_qkv[l : l + 1], gate)[0])
        wide_up.append(columns_whole(w_up[l : l + 1], gate)[0])
        gate = wide_qkv[-1]

    def own(whole):
        return lax.dynamic_slice(whole, (row * half, col * part_width), (half, part_width))

    params = [
        (vectors[0, l], vectors[1, l], vectors[2, l], vectors[3, l], wide_qkv[l], b_qkv[l],
         wide_up[l], b_up[l], w_out[l], w_down[l], vectors[4, l])
        for l in range(layers)
    ]
    state = state_in
    caches = []
    for layer in range(layers):
        part, cache = forward_layer(state, allowed, cosine, sine, params[layer])
        caches.append(cache)
        if layer < layers - 1:
            state = state + group_sum(part) + params[layer][-1]
    y_base = x_in + own(state - state_in + params[-1][-1])
    grad = grad_in
    heavy = [None] * layers
    thin = [None] * layers
    narrow = [None] * layers
    for layer in reversed(range(layers)):
        grad, heavy[layer], thin[layer], narrow[layer] = backward_layer(
            grad, allowed, cosine, sine, params[layer], caches[layer])
    x_grad = cotangent + own(grad - grad_in)
    y_out = y_base + own(group_sum(part))
    summed = []
    for layer in range(layers):
        a, b, c, d = heavy[layer]
        summed.append(lax.psum((rows_whole(a), rows_whole(b), c, d), "dp"))
    g_bqkv, g_bup, narrow = lax.psum((
        jnp.stack([t[0] for t in thin]), jnp.stack([t[1] for t in thin]),
        jnp.stack([t[:5] for t in narrow])), "dp")
    g_wqkv, g_wup, g_wout, g_wdown = (
        jnp.stack([h[k] for h in summed]).astype(F32) for k in range(4))
    narrow = lax.dynamic_slice_in_dim(narrow, col * part_width, part_width, 2)
    g_bout = narrow[:, 4]
    return (
        y_out, x_grad, narrow[:, 0], narrow[:, 1], narrow[:, 2], narrow[:, 3],
        g_wqkv, g_bqkv, g_wup, g_bup, g_wout, g_bout, g_wdown, g_bout,
    )


BLK = 128


def tdot(a, b):
    return lax.dot_general(a, b, (((0,), (0,)), ((), ())), preferred_element_type=F32)


def ntdot(a, b):
    return lax.dot_general(a, b, (((1,), (1,)), ((), ())), preferred_element_type=F32)


def ndot(a, b):
    return jnp.dot(a, b, preferred_element_type=F32)


def whole_body(
    n, x, cot, seg, n1g, n1b, n2g, n2b, bq, bu, bo, bd, cosr, sinr, wq_in, wu_in, wo_in, wd_in,
    y, xg, od, ow, ou, oq, osm,
    wq, wu, wo, wd, xb, cb, vec, mask, st, nrm, inv, fst, snd, act, slope, qkv_t, qh, p_t, m_t,
    gm_t, gub, gqb_t, gq, gb, own, sb, got_row, mine, got_col, back, back_got,
    ind, inw, iu, iq, ism, rdp, rdm, rw, ru, rq, rsm, swu, swq,
    nar, nar_got, thin, send, recv, local,
):
    layers = wq.shape[0]
    gq_t = qkv_t
    half, cols = x.shape
    length, width = half * 2, cols * 2
    hid = wu.shape[2]
    heads = p_t.shape[1]
    qw = heads * 3 * HD
    row, col, here = lax.axis_index("row"), lax.axis_index("col"), lax.axis_index("dp")
    orow, ocol = 1 - row, 1 - col
    odd = lax.rem(here, 2)
    pos = here // 2 + odd * (n - 1 - 2 * (here // 2))

    def device(place):
        late = place // (n // 2)
        return 2 * (place + late * (n - 1 - 2 * place)) + late

    targets = (device(lax.rem(pos + 1, n)), device(lax.rem(pos + n - 1, n)))
    beside = here + 1 - 2 * odd
    barrier = pltpu.get_barrier_semaphore()
    pl.semaphore_signal(barrier, inc=1, device_id={"dp": beside}, device_id_type=MESH_ID)
    pl.semaphore_signal(barrier, inc=1, device_id={"dp": targets[0]}, device_id_type=MESH_ID)
    pl.semaphore_signal(barrier, inc=1, device_id={"dp": targets[1]}, device_id_type=MESH_ID)
    pl.semaphore_signal(barrier, inc=1, device_id={"col": ocol}, device_id_type=MESH_ID)
    pl.semaphore_signal(barrier, inc=1, device_id={"row": orow}, device_id_type=MESH_ID)

    count = [0]
    sent = []

    def rc(src, dst, axis, target):
        k = count[0]
        count[0] += 1
        copy = pltpu.make_async_remote_copy(
            src, dst, send.at[k], recv.at[k], device_id={axis: target}, device_id_type=MESH_ID)
        copy.start()
        sent.append(copy)
        return copy

    def over_row(src, dst):
        return rc(src, dst, "row", orow)

    def over_col(src, dst):
        return rc(src, dst, "col", ocol)

    def at(base, size, step=None):
        return pl.ds(pl.multiple_of(base, step or size), size)

    my_rows, their_rows = at(row * half, half), at(orow * half, half)
    my_cols, their_cols = at(col * cols, cols), at(ocol * cols, cols)
    shift = wq_in.shape[2] - wq.shape[2]
    my_heads, their_heads = at(col * shift, wq.shape[2], BLK), at(ocol * shift, wq.shape[2], BLK)
    my_hid, their_hid = at(col * hid, hid), at(ocol * hid, hid)

    loads = []
    for l in range(layers):
        loads.append([
            pltpu.make_async_copy(wq_in.at[l, :, my_heads], wq.at[l, my_cols], local.at[l, 0]),
            pltpu.make_async_copy(wu_in.at[l, :, my_hid], wu.at[l, my_cols], local.at[l, 1]),
            pltpu.make_async_copy(wo_in.at[l], wo.at[l], local.at[l, 2]),
            pltpu.make_async_copy(wd_in.at[l], wd.at[l], local.at[l, 3]),
        ])
        for copy in loads[-1]:
            copy.start()

    xb[my_rows, my_cols] = x[...].astype(BF)
    cb[my_rows, my_cols] = cot[...].astype(BF)
    for k, ref in enumerate((n1g, n1b, n2g, n2b)):
        vec[2 * k : 2 * k + 2, my_cols] = ref[...]
    vec[8:10, my_cols] = bo[...] + bd[...]
    pl.semaphore_wait(barrier, 5)

    x_col = over_col(xb.at[my_rows, my_cols], xb.at[my_rows, my_cols])
    x_row = over_row(xb.at[my_rows, my_cols], xb.at[my_rows, my_cols])
    v_col = over_col(vec.at[:, my_cols], vec.at[:, my_cols])

    some = cols // 2
    sent_rows = at(col * cols + odd * some, some)
    got_rows = at(ocol * cols + odd * some, some)
    from_rows = at(odd * some, some)

    def weight_q(l):
        return over_col(wq_in.at[l, from_rows, their_heads], wq.at[l, sent_rows])

    def weight_u(l):
        return over_col(wu_in.at[l, from_rows, their_hid], wu.at[l, sent_rows])

    def pass_on(copy, ref, l):
        copy.wait_recv()
        return rc(ref.at[l, got_rows], ref.at[l, got_rows], "dp", beside)

    w_q, w_u = [weight_q(0)], [weight_u(0)]
    c_row = over_row(cb.at[my_rows, my_cols], cb.at[my_rows, my_cols])

    label = seg[...].astype(F32)
    tall = jnp.broadcast_to(label, (BLK, length)).T
    for k in range(length // BLK):
        here_rows = slice(k * BLK, (k + 1) * BLK)
        key_at = lax.broadcasted_iota(jnp.int32, (BLK, length), 0) + k * BLK
        query_at = lax.broadcasted_iota(jnp.int32, (BLK, length), 1)
        same = tall[here_rows, 0:1] == label
        mask[here_rows, :] = jnp.where(same & (key_at <= query_at), 0.0, NEG)
    nar[...] = jnp.zeros_like(nar)
    offset = col * (wq.shape[2] - qw)

    x_col.wait_recv()
    x_over = over_row(xb.at[my_rows, their_cols], xb.at[my_rows, their_cols])
    v_col.wait_recv()
    x_row.wait_recv()
    x_over.wait_recv()

    def gain(k, l):
        return vec[2 * k + l : 2 * k + l + 1, :]

    blocks = length // BLK

    def norm_step(l):
        @pl.loop(0, blocks)
        def _(i):
            rows = at(i * BLK, BLK)
            s = xb[rows, :].astype(F32) if l == 0 else st[rows, :]
            mean = jnp.sum(s, axis=1, keepdims=True) / width
            squares = jnp.sum(s * s, axis=1, keepdims=True) / width
            inverse = lax.rsqrt(squares - mean * mean + EPS)
            normed = (s - mean) * inverse
            inv[l, rows, :] = inverse
            nrm[l, rows, :] = normed.astype(BF)
            fst[l, rows, :] = (normed * gain(0, l) + gain(1, l)).astype(BF)
            snd[l, rows, :] = (normed * gain(2, l) + gain(3, l)).astype(BF)

    def qkv_step(l):
        @pl.loop(0, blocks)
        def _(i):
            rows = at(i * BLK, BLK)
            got = ndot(fst[l, rows, :], wq[l]) + bq[l : l + 1, :]
            qkv_t[:, rows] = got.T

    def turn(v, sign):
        a, b = v[0:8], v[8:16]
        c, s = cosr[...], sinr[...] * sign
        return jnp.concatenate([a * c - b * s, b * c + a * s, v[16:]], axis=0)

    QB = length // 2

    def attention_step(l):
        @pl.loop(0, heads)
        def _(h):
            base = offset + h * (3 * HD)
            q = turn(qkv_t[at(base, HD), :], 1.0).astype(BF)
            k = turn(qkv_t[at(base + HD, HD), :], 1.0).astype(BF)
            v = qkv_t[at(base + 2 * HD, HD), :].astype(BF)
            spot = h * (3 * HD)
            qh[l, at(spot, HD), :] = q
            qh[l, at(spot + HD, HD), :] = k
            qh[l, at(spot + 2 * HD, HD), :] = v
            q = q * jnp.asarray(SCALE, BF)
            for b in range(2):
                keys, these = slice(0, (b + 1) * QB), slice(b * QB, (b + 1) * QB)
                scores = tdot(k[:, keys], q[:, these]) + mask[keys, these]
                top = jnp.max(scores, axis=0, keepdims=True)
                e = jnp.exp(scores - top)
                total = jnp.sum(e, axis=0, keepdims=True)
                probs = (e * (1.0 / total)).astype(BF)
                p_t[l, h, keys, these] = probs
                m_t[l, at(h * HD, HD), these] = ndot(v[:, keys], probs).astype(BF)

    def up_step(l):
        @pl.loop(0, blocks)
        def _(i):
            rows = at(i * BLK, BLK)
            up = ndot(snd[l, rows, :], wu[l]) + bu[l : l + 1, :]
            phi = 0.5 * (1.0 + lax.erf(up * INV_ROOT2))
            act[l, rows, :] = (up * phi).astype(BF)
            slope[l, rows, :] = (phi + up * jnp.exp(-0.5 * up * up) * INV_ROOT_TWO_PI).astype(BF)

    def part_rows(l):
        def run(base):
            rows = at(base, BLK)
            return tdot(m_t[l, :, rows], wo[l]) + ndot(act[l, rows, :], wd[l])
        return run

    pieces = half // BLK

    def sum_begin(k, fn):
        flight = []
        for p in range(pieces):
            here = slice(p * BLK, (p + 1) * BLK)
            sb[k, here, :] = fn(orow * half + p * BLK).astype(BF)
            flight.append(over_row(sb.at[k, here], got_row.at[k, here]))
        for p in range(pieces):
            here = slice(p * BLK, (p + 1) * BLK)
            own[k % 2, here, :] = fn(row * half + p * BLK)
        return flight

    def sum_cross(k, flight, narrow=False):
        crossing = []
        for p in range(pieces):
            here = slice(p * BLK, (p + 1) * BLK)
            flight[p].wait_recv()
            t = own[k % 2, here, :] + got_row[k, here, :].astype(F32)
            own[k % 2, here, :] = t
            mine[k, here, :] = t.astype(BF)
            if narrow:
                crossing.append(over_col(
                    mine.at[k, here, their_cols], got_col.at[k, here, their_cols]))
            else:
                crossing.append(over_col(mine.at[k, here], got_col.at[k, here]))
        return crossing


    norm_step(0)
    q_on = pass_on(w_q[0], wq, 0)
    w_q.append(weight_q(1))
    u_on = pass_on(w_u[0], wu, 0)
    w_u.append(weight_u(1))
    c_col = over_col(cb.at[my_rows, my_cols], cb.at[my_rows, my_cols])
    loads[0][0].wait()
    q_on.wait_recv()
    qkv_step(0)
    attention_step(0)
    loads[0][1].wait()
    u_on.wait_recv()
    up_step(0)
    q_on = pass_on(w_q[1], wq, 1)
    loads[0][2].wait()
    loads[0][3].wait()
    flight = sum_begin(0, part_rows(0))
    crossing = sum_cross(0, flight)
    u_on = pass_on(w_u[1], wu, 1)
    c_col.wait_recv()
    c_over = over_row(cb.at[my_rows, their_cols], cb.at[my_rows, their_cols])
    both = vec[8:9, :]
    returned = []
    for p in range(pieces):
        here = slice(p * BLK, (p + 1) * BLK)
        crossing[p].wait_recv()
        total = own[0, here, :] + got_col[0, here, :].astype(F32)
        own[0, here, :] = total
        back[0, here, :] = total.astype(BF)
        returned.append(over_row(back.at[0, here], back_got.at[0, here]))
    for p in range(pieces):
        here = slice(p * BLK, (p + 1) * BLK)
        rows = at(row * half + p * BLK, BLK)
        st[rows, :] = xb[rows, :].astype(F32) + own[0, here, :] + both
    y[...] = x[...] + own[0, :, my_cols] + vec[8:9, my_cols] + vec[9:10, my_cols]
    for p in range(pieces):
        here = slice(p * BLK, (p + 1) * BLK)
        returned[p].wait_recv()
        rows = at(orow * half + p * BLK, BLK)
        st[rows, :] = xb[rows, :].astype(F32) + back_got[0, here, :].astype(F32) + both

    norm_step(1)
    loads[1][0].wait()
    q_on.wait_recv()
    qkv_step(1)
    attention_step(1)
    loads[1][1].wait()
    u_on.wait_recv()
    up_step(1)
    loads[1][2].wait()
    loads[1][3].wait()

    def chunk(d, behind):
        sign = 1 if d == 0 else -1
        return lax.rem(pos - sign * behind + 2 * n, n)

    def stream(d, parts, swap=None):
        def go(pairs):
            return [rc(src, dst, "dp", targets[d]) for src, dst in pairs]
        copies = go([(rin(chunk(d, 0)), got(0)) for rin, got, out in parts])
        for s in range(n - 1):
            yield
            for k, (rin, got, out) in enumerate(parts):
                copies[k].wait_recv()
                got(s)[...] = got(s)[...] + rin(chunk(d, s + 1))[...]
                if s < n - 2:
                    copies[k] = go([(got(s), got(s + 1))])[0]
        where = chunk(d, n - 1)
        if swap is None:
            for rin, got, out in parts:
                out(where)[...] = got(n - 2)[...]
        else:
            last, out = parts[0][1](n - 2), parts[0][2]
            over = over_col(last.at[ocol], swap)
            yield
            over.wait_recv()
            wide = last.shape[2]
            if wide % BLK == 0:
                out(where).at[:, at(col * wide, wide)][...] = last[col]
                out(where).at[:, at(ocol * wide, wide)][...] = swap[...]
            else:
                a, b = last[col].astype(F32), swap[...].astype(F32)
                first = col == 0
                out(where)[...] = jnp.concatenate(
                    [jnp.where(first, a, b), jnp.where(first, b, a)], axis=1).astype(BF)
        copies = go([(out(where), out(where)) for rin, got, out in parts])
        for s in range(n - 1):
            yield
            for k, (rin, got, out) in enumerate(parts):
                copies[k].wait_recv()
                if s < n - 2:
                    where = chunk(d, s)
                    copies[k] = go([(out(where), out(where))])[0]

    active = []

    def launch(*args, **kw):
        g = stream(*args, **kw)
        next(g)
        active.append(g)

    def pump(times=1):
        for _ in range(times):
            for g in list(active):
                try:
                    next(g)
                except StopIteration:
                    active.remove(g)

    deep = hid // n
    cut = deep // 2

    def down_step(l, g):
        for k in range(2):
            f = slice(k * (hid // 2), (k + 1) * (hid // 2))
            got = tdot(act[l, :, f], g[...]).astype(BF)
            ind[l, k * (n // 2) : (k + 1) * (n // 2)] = got.reshape(n // 2, deep, width)
        got = ndot(m_t[l], g[...]).reshape(n, -1, width)
        pad = jnp.zeros((n, inw.shape[2] - got.shape[1], width), F32)
        inw[l] = jnp.concatenate([got, pad], axis=1).astype(BF)
        launch(0, [(lambda c: ind.at[l, c, 0:cut], lambda s: rdp.at[l, s],
                    lambda c: od.at[l, at(c * deep, cut, cut)])])
        launch(1, [(lambda c: ind.at[l, c, cut:deep], lambda s: rdm.at[l, s],
                    lambda c: od.at[l, at(c * deep + cut, cut, cut)]),
                   (lambda c: inw.at[l, c], lambda s: rw.at[l, s], lambda c: ow.at[l, c])])

    def up_grad_step(l):
        for k in range(2):
            f = slice(k * cols, (k + 1) * cols)
            got = tdot(snd[l, :, f], gub[...]).astype(BF)
            iu[l, :, k] = got.reshape(n, -1, hid)
        launch(0, [(lambda c: iu.at[l, c], lambda s: ru.at[l, s],
                    lambda c: ou.at[l, at(c * iu.shape[3], iu.shape[3])])], swap=swu.at[l])

    def qkv_grad_step(l):
        for k in range(2):
            f = slice(k * cols, (k + 1) * cols)
            got = ntdot(fst[l, :, f].T, gqb_t[...]).astype(BF)
            iq[l, :, k] = got.reshape(n, -1, qw)
        launch(1, [(lambda c: iq.at[l, c], lambda s: rq.at[l, s],
                    lambda c: oq.at[l, at(c * iq.shape[3], iq.shape[3])])], swap=swq.at[l])

    def grad_up_step(l, g):
        def block(i, total):
            rows = at(i * BLK, BLK)
            gu = ntdot(g[rows, :], wd[l]) * slope[l, rows, :].astype(F32)
            gub[rows, :] = gu.astype(BF)
            return total + jnp.sum(gu, axis=0, keepdims=True)
        total = lax.fori_loop(0, blocks, block, jnp.zeros((1, hid), F32))
        thin[l, 1:2, 0:hid] = total

    def attention_back_step(l, g):
        gm_t[...] = ntdot(wo[l], g[...]).astype(BF)

        @pl.loop(0, heads)
        def _(h):
            spot = h * (3 * HD)
            q = qh[l, at(spot, HD), :]
            k = qh[l, at(spot + HD, HD), :]
            v = qh[l, at(spot + 2 * HD, HD), :]
            gm = gm_t[at(h * HD, HD), :]
            mixed = m_t[l, at(h * HD, HD), :]
            delta = jnp.sum(gm.astype(F32) * mixed.astype(F32), axis=0, keepdims=True)
            gqs, gks, gvs = [], [], []
            for b in range(2):
                keys, these = slice(0, (b + 1) * QB), slice(b * QB, (b + 1) * QB)
                probs = p_t[l, h, keys, these]
                gp = tdot(v[:, keys], gm[:, these])
                ds = (probs.astype(F32) * (gp - delta[:, these])).astype(BF)
                gqs.append(ndot(k[:, keys], ds))
                gks.append(ntdot(q[:, these], ds))
                gvs.append(ntdot(gm[:, these], probs))
            gq_h = jnp.concatenate(gqs, axis=1) * SCALE
            gk_h = jnp.concatenate([gks[0] + gks[1][:, :QB], gks[1][:, QB:]], axis=1) * SCALE
            gv_h = jnp.concatenate([gvs[0] + gvs[1][:, :QB], gvs[1][:, QB:]], axis=1)
            base = offset + spot
            for k3, value in enumerate((turn(gq_h, -1.0), turn(gk_h, -1.0), gv_h)):
                gq_t[at(base + k3 * HD, HD), :] = value
                gqb_t[at(spot + k3 * HD, HD), :] = value.astype(BF)

        total = jnp.zeros((1, gq_t.shape[0]), F32)
        for i in range(blocks):
            flat = gq_t[:, i * BLK : (i + 1) * BLK].T
            gq[i * BLK : (i + 1) * BLK, :] = flat.astype(BF)
            total = total + jnp.sum(flat, axis=0, keepdims=True)
        thin[l, 0:1, :] = jnp.concatenate([total, jnp.zeros((1, width - total.shape[1]), F32)], axis=1)

    def back_rows(l):
        def run(base):
            rows = at(base, BLK)
            gf = ntdot(gq[rows, :], wq[l])
            gs = ntdot(gub[rows, :], wu[l])
            normed = nrm[l, rows, :].astype(F32)
            for k, value in enumerate((gf * normed, gf, gs * normed, gs)):
                nar[l, 0, k : k + 1, :] += jnp.sum(value, axis=0, keepdims=True)
            return gf * gain(0, l) + gs * gain(2, l)
        return run

    def centred(l, rows, total):
        normed = nrm[l, rows, :].astype(F32)
        return inv[l, rows, :] * (
            total - jnp.sum(total, axis=1, keepdims=True) / width
            - normed * (jnp.sum(total * normed, axis=1, keepdims=True) / width))

    gq_t[...] = jnp.zeros_like(gq_t)
    shares = 0.25
    c_row.wait_recv()
    c_over.wait_recv()
    nar[1, 0, 4:5, :] = jnp.sum(cb[...].astype(F32), axis=0, keepdims=True) * shares
    down_step(1, cb)
    grad_up_step(1, cb)
    attention_back_step(1, cb)
    pump()
    flight = sum_begin(1, back_rows(1))
    nar_row = over_row(nar.at[1, 0], nar_got.at[1, 0])
    crossing = sum_cross(1, flight)
    pump()
    up_grad_step(1)
    returned = []
    for p in range(pieces):
        here = slice(p * BLK, (p + 1) * BLK)
        crossing[p].wait_recv()
        total = own[1, here, :] + got_col[1, here, :].astype(F32)
        own[1, here, :] = total
        back[1, here, :] = total.astype(BF)
        returned.append(over_row(back.at[1, here], back_got.at[1, here]))
    bout = jnp.zeros((1, width), F32)
    for p in range(pieces):
        here = slice(p * BLK, (p + 1) * BLK)
        rows = at(row * half + p * BLK, BLK)
        change = centred(1, rows, own[1, here, :])
        own[1, here, :] = change
        grad = cb[rows, :].astype(F32) + change
        gb[rows, :] = grad.astype(BF)
        bout = bout + jnp.sum(grad, axis=0, keepdims=True)
    xg[...] = cot[...] + own[1, :, my_cols]
    for p in range(pieces):
        here = slice(p * BLK, (p + 1) * BLK)
        returned[p].wait_recv()
        rows = at(orow * half + p * BLK, BLK)
        grad = cb[rows, :].astype(F32) + centred(1, rows, back_got[1, here, :].astype(F32))
        gb[rows, :] = grad.astype(BF)
        bout = bout + jnp.sum(grad, axis=0, keepdims=True)
    nar[0, 0, 4:5, :] = bout * shares
    nar_row.wait_recv()
    nar[1, 1] = nar[1, 0] + nar_got[1, 0]
    nar_col = over_col(nar.at[1, 1], nar_got.at[1, 1])
    qkv_grad_step(1)
    pump()
    down_step(0, gb)
    pump()
    grad_up_step(0, gb)
    pump()
    attention_back_step(0, gb)
    pump()
    flight_x = sum_begin(3, back_rows(0))
    nar_row0 = over_row(nar.at[0, 0], nar_got.at[0, 0])
    crossing_x = sum_cross(3, flight_x)
    nar_row0.wait_recv()
    nar[0, 1] = nar[0, 0] + nar_got[0, 0]
    nar_col0 = over_col(nar.at[0, 1], nar_got.at[0, 1])
    pump()
    up_grad_step(0)
    pump()
    qkv_grad_step(0)
    pump()
    nar_col.wait_recv()
    nar_col0.wait_recv()
    ism[...] = jnp.zeros_like(ism)
    ism[0] = jnp.concatenate(
        [v for l in range(layers) for v in (
            nar[l, 1, 0:5, :] + nar_got[l, 1, 0:5, :], thin[l, 0:2, :], jnp.zeros((1, width), F32))],
        axis=0).astype(BF)
    launch(0, [(lambda c: ism.at[c], lambda s: rsm.at[s], lambda c: osm.at[c])])
    pump()
    flight_y = sum_begin(2, part_rows(1))
    crossing_y = sum_cross(2, flight_y, narrow=True)
    pump()
    for p in range(pieces):
        here = slice(p * BLK, (p + 1) * BLK)
        crossing_x[p].wait_recv()
        rows = at(row * half + p * BLK, BLK)
        own[1, here, :] = centred(0, rows, own[1, here, :] + got_col[3, here, :].astype(F32))
    xg[...] += own[1, :, my_cols]
    pump()
    for p in range(pieces):
        crossing_y[p].wait_recv()
    y[...] += own[0, :, my_cols] + got_col[2, :, my_cols].astype(F32)
    while active:
        pump()
    for copy in sent:
        copy.wait_send()


def whole_step(x, cot, seg, n1g, n1b, n2g, n2b, wq_in, bq, wu_in, bu, wo_in, bo, wd_in, bd):
    n = lax.axis_size("dp")
    half, cols = x.shape
    layers, _, both_heads = wq_in.shape
    length, width = 2 * half, 2 * cols
    hid = wu_in.shape[2] // 2
    qw = both_heads // 2
    heads = qw // (3 * HD)
    wide = -(-qw // BLK) * BLK
    mix = wo_in.shape[1]
    col = lax.axis_index("col")
    freq = np.float32(10000.0) ** (-(np.arange(ROT // 2, dtype=np.float32) * 2) / np.float32(ROT))
    angle = freq[:, None] * np.arange(length, dtype=np.float32)[None, :]
    cosr, sinr = jnp.asarray(np.cos(angle), F32), jnp.asarray(np.sin(angle), F32)
    bq = lax.dynamic_update_slice(jnp.zeros((layers, wide), F32), bq, (0, col * (wide - qw)))
    per, deep, flat = width // 2 // n, hid // n, mix // n
    cut = deep // 2
    tall = flat + -flat % 16
    small = 8 * layers
    vmem = pl.BlockSpec(memory_space=pltpu.VMEM)
    anyw = pl.BlockSpec(memory_space=pl.ANY)
    V = pltpu.VMEM
    sums = 4
    sems = 256
    out = pl.pallas_call(
        lambda *refs: whole_body(n, *refs),
        out_shape=[
            jax.ShapeDtypeStruct((half, cols), F32), jax.ShapeDtypeStruct((half, cols), F32),
            jax.ShapeDtypeStruct((layers, hid, width), BF),
            jax.ShapeDtypeStruct((layers, n, tall, width), BF),
            jax.ShapeDtypeStruct((layers, width // 2, 2 * hid), BF),
            jax.ShapeDtypeStruct((layers, width // 2, 2 * qw), BF),
            jax.ShapeDtypeStruct((n, small, width), BF),
        ],
        in_specs=[vmem] * 13 + [anyw] * 4,
        out_specs=[vmem] * 7,
        scratch_shapes=[
            V((layers, width, wide), BF), V((layers, width, hid), BF),
            V((layers, mix, width), BF), V((layers, hid, width), BF),
            V((length, width), BF), V((length, width), BF), V((16, width), F32),
            V((length, length), F32), V((length, width), F32),
            V((layers, length, width), BF), V((layers, length, 1), F32),
            V((layers, length, width), BF), V((layers, length, width), BF),
            V((layers, length, hid), BF), V((layers, length, hid), BF),
            V((wide, length), F32), V((layers, qw, length), BF),
            V((layers, heads, length, length), BF), V((layers, mix, length), BF),
            V((mix, length), BF), V((length, hid), BF),
            V((qw, length), BF), V((length, wide), BF), V((length, width), BF),
            V((2, half, width), F32), V((sums, half, width), BF), V((sums, half, width), BF),
            V((sums, half, width), BF), V((sums, half, width), BF),
            V((2, half, width), BF), V((2, half, width), BF),
            V((layers, n, deep, width), BF), V((layers, n, tall, width), BF),
            V((layers, n, 2, per, hid), BF), V((layers, n, 2, per, qw), BF),
            V((n, small, width), BF),
            V((layers, n - 1, cut, width), BF), V((layers, n - 1, deep - cut, width), BF),
            V((layers, n - 1, tall, width), BF),
            V((layers, n - 1, 2, per, hid), BF), V((layers, n - 1, 2, per, qw), BF),
            V((n - 1, small, width), BF),
            V((layers, per, hid), BF), V((layers, per, qw), BF),
            V((layers, 2, 8, width), F32), V((layers, 2, 8, width), F32),
            V((layers, 2, width), F32),
            pltpu.SemaphoreType.DMA((sems,)), pltpu.SemaphoreType.DMA((sems,)),
            pltpu.SemaphoreType.DMA((layers, 4)),
        ],
        compiler_params=pltpu.CompilerParams(
            collective_id=5, has_side_effects=True, vmem_limit_bytes=62 * 1024 * 1024),
        name="whole_step",
    )(x, cot, seg, n1g, n1b, n2g, n2b, bq, bu, bo, bd, cosr, sinr, wq_in, wu_in, wo_in, wd_in)
    y, xg, d, w, u, q, s = out
    g_wqkv, g_wup, g_wdown = q.astype(F32), u.astype(F32), d.astype(F32)
    g_wout = w[:, :, :flat].reshape(layers, mix, width).astype(F32)
    s = s[0].astype(F32).reshape(layers, 8, width)
    narrow = lax.dynamic_slice_in_dim(s[:, :5], col * cols, cols, 2)
    g_bqkv = lax.dynamic_slice_in_dim(s[:, 5], col * (wide - qw), qw, 1)
    g_bup = s[:, 6, :hid]
    g_bout = narrow[:, 4]
    return (
        y, xg, narrow[:, 0], narrow[:, 1], narrow[:, 2], narrow[:, 3],
        g_wqkv, g_bqkv, g_wup, g_bup, g_wout, g_bout, g_wdown, g_bout)


def per_device(*args):
    x, wq, wo, wd = args[0], args[7], args[11], args[13]
    n = lax.axis_size("dp")
    parts = lax.axis_size("row"), lax.axis_size("col")
    cols = x.shape[1]
    fits = (
        parts == (2, 2) and n % 2 == 0 and n >= 4 and cols % n == 0 and (cols // n) % 16 == 0
        and (wd.shape[1] // n) % 32 == 0 and (wo.shape[1] // n) % 8 == 0 and wq.shape[0] == 2)
    return whole_step(*args) if fits else per_device_plain(*args)


def solution(mesh):
    in_specs = (
        P(("dp", "row"), "col"),
        P(("dp", "row"), "col"),
        P("dp", None),
        P(None, "col"),
        P(None, "col"),
        P(None, "col"),
        P(None, "col"),
        P(None, "col", "row"),
        P(None, ("row", "col")),
        P(None, "col", "row"),
        P(None, ("row", "col")),
        P(None, ("row", "col"), None),
        P(None, "col"),
        P(None, ("row", "col"), None),
        P(None, "col"),
    )
    out_specs = (
        P(("dp", "row"), "col"),
        P(("dp", "row"), "col"),
        P(None, "col"),
        P(None, "col"),
        P(None, "col"),
        P(None, "col"),
        P(None, "col", "row"),
        P(None, ("row", "col")),
        P(None, "col", "row"),
        P(None, ("row", "col")),
        P(None, ("row", "col"), None),
        P(None, "col"),
        P(None, ("row", "col"), None),
        P(None, "col"),
    )
    return jax.shard_map(
        per_device, mesh=mesh, in_specs=in_specs, out_specs=out_specs, check_vma=False
    )
```

```python
import jax
import jax.numpy as jnp
import numpy as np
from jax import lax
from jax.experimental import pallas as pl
from jax.experimental.pallas import tpu as pltpu
from jax.sharding import PartitionSpec as P

D = 768
HD = 64
ROT = 16
LAYERS = 2


EPS = 1e-05
NEG = -1e30
SCALE = 0.125
INV_ROOT2 = 0.7071067811865476
INV_ROOT_TWO_PI = 0.3989422804014327


def rope_tables(length):
    half = ROT // 2
    freq = 10000.0 ** (-(jnp.arange(half, dtype=jnp.float32) * 2.0) / ROT)
    angle = jnp.arange(length, dtype=jnp.float32)[:, None] * freq[None, :]
    cosine = jnp.concatenate([jnp.cos(angle), jnp.cos(angle)], axis=1)
    sine = jnp.concatenate([jnp.sin(angle), jnp.sin(angle)], axis=1)
    return (cosine, sine)


def rotate(values, cosine, sine):
    part = values[..., :ROT]
    lower = part[..., : ROT // 2]
    upper = part[..., ROT // 2 :]
    turned = jnp.concatenate([-upper, lower], axis=-1)
    moved = part * cosine[:, None, :] + turned * sine[:, None, :]
    return jnp.concatenate([moved, values[..., ROT:]], axis=-1)


def unrotate(grads, cosine, sine):
    part = grads[..., :ROT]
    lower = part[..., : ROT // 2]
    upper = part[..., ROT // 2 :]
    turned = jnp.concatenate([upper, -lower], axis=-1)
    moved = part * cosine[:, None, :] + turned * sine[:, None, :]
    return jnp.concatenate([moved, grads[..., ROT:]], axis=-1)


def gelu_exact(values):
    return 0.5 * values * (1.0 + jax.scipy.special.erf(values * INV_ROOT2))


def gelu_slope(values):
    return (
        0.5 * (1.0 + jax.scipy.special.erf(values * INV_ROOT2))
        + values * jnp.exp(-0.5 * values * values) * INV_ROOT_TWO_PI
    )


BF = jnp.bfloat16
F32 = jnp.float32
MESH_ID = pl.DeviceIdType.MESH
PIECES = 4


def greet():
    row = 1 - lax.axis_index("row")
    col = 1 - lax.axis_index("col")
    barrier = pltpu.get_barrier_semaphore()
    pl.semaphore_signal(barrier, inc=1, device_id={"row": row}, device_id_type=MESH_ID)
    pl.semaphore_signal(barrier, inc=1, device_id={"col": col}, device_id_type=MESH_ID)
    pl.semaphore_wait(barrier, 2)
    return row, col


def reduce_body(*refs):
    if len(refs) == 7:
        part, out, got_row, mine, got_col, send, recv = refs
        extra = None
    else:
        part, extra, out, extra_out, got_row, mine, got_col, pair, got_extra, send, recv = refs
    half = mine.shape[0]
    piece = half // PIECES
    row, col = greet()
    own = (1 - row) * half
    theirs = row * half
    first, second, third = [], [], []
    for k in range(PIECES):
        at = pl.multiple_of(theirs + k * piece, piece)
        copy = pltpu.make_async_remote_copy(
            part.at[pl.ds(at, piece)], got_row.at[pl.ds(k * piece, piece)],
            send.at[0, k], recv.at[0, k], device_id={"row": row}, device_id_type=MESH_ID)
        copy.start()
        first.append(copy)
    if extra is not None:
        over_row = pltpu.make_async_remote_copy(
            extra, got_extra.at[0], send.at[3, 0], recv.at[3, 0],
            device_id={"row": row}, device_id_type=MESH_ID)
        over_row.start()
    for k in range(PIECES):
        here = pl.ds(k * piece, piece)
        at = pl.multiple_of(own + k * piece, piece)
        first[k].wait_recv()
        mine[here, :] = (part[pl.ds(at, piece), :] + got_row[here, :]).astype(BF)
        copy = pltpu.make_async_remote_copy(
            mine.at[here], got_col.at[here], send.at[1, k], recv.at[1, k],
            device_id={"col": col}, device_id_type=MESH_ID)
        copy.start()
        second.append(copy)
    if extra is not None:
        over_row.wait_recv()
        pair[...] = extra[...] + got_extra[0]
        over_col = pltpu.make_async_remote_copy(
            pair, got_extra.at[1], send.at[3, 1], recv.at[3, 1],
            device_id={"col": col}, device_id_type=MESH_ID)
        over_col.start()
    for k in range(PIECES):
        here = pl.ds(k * piece, piece)
        at = pl.multiple_of(own + k * piece, piece)
        second[k].wait_recv()
        out[pl.ds(at, piece), :] = mine[here, :].astype(F32) + got_col[here, :].astype(F32)
        copy = pltpu.make_async_remote_copy(
            out.at[pl.ds(at, piece)], out.at[pl.ds(at, piece)], send.at[2, k], recv.at[2, k],
            device_id={"row": row}, device_id_type=MESH_ID)
        copy.start()
        third.append(copy)
    if extra is not None:
        over_col.wait_recv()
        extra_out[...] = pair[...] + got_extra[1]
        over_row.wait_send()
        over_col.wait_send()
    for k in range(PIECES):
        third[k].wait_recv()
        for copy in (first[k], second[k], third[k]):
            copy.wait_send()


def group_sum(part, extra=None):
    rows, width = part.shape
    half = rows // lax.axis_size("row")
    vmem = pl.BlockSpec(memory_space=pltpu.VMEM)
    out_shape = [jax.ShapeDtypeStruct((rows, width), F32)]
    scratch = [pltpu.VMEM((half, width), F32), pltpu.VMEM((half, width), BF),
               pltpu.VMEM((half, width), BF)]
    args = [part]
    if extra is not None:
        args.append(extra)
        out_shape.append(jax.ShapeDtypeStruct(extra.shape, F32))
        scratch += [pltpu.VMEM(extra.shape, F32), pltpu.VMEM((2,) + extra.shape, F32)]
    result = pl.pallas_call(
        reduce_body,
        out_shape=out_shape,
        in_specs=[vmem] * len(args),
        out_specs=[vmem] * len(out_shape),
        scratch_shapes=scratch + [
            pltpu.SemaphoreType.DMA((4, PIECES)), pltpu.SemaphoreType.DMA((4, PIECES))],
        compiler_params=pltpu.CompilerParams(
            collective_id=0 if extra is None else 2, has_side_effects=True),
        name="group_sum",
    )(*args)
    return result[0] if extra is None else result


def gather_body(x, cot, vec, x_out, cot_out, vec_out, send, recv):
    half, width = x.shape
    row, col = greet()
    my_rows = pl.ds(pl.multiple_of((1 - row) * half, half), half)
    my_cols = pl.ds(pl.multiple_of((1 - col) * width, width), width)
    their_cols = pl.ds(pl.multiple_of(col * width, width), width)
    every = pl.ds(0, vec.shape[0])
    jobs = [(x, x_out, my_rows), (vec, vec_out, every), (cot, cot_out, my_rows)]
    copies = []
    first = []
    for k, (own, out, rows) in enumerate(jobs):
        copy = pltpu.make_async_remote_copy(
            own, out.at[rows, my_cols], send.at[0, k], recv.at[0, k],
            device_id={"col": col}, device_id_type=MESH_ID)
        copy.start()
        first.append(copy)
    for k, (own, out, rows) in enumerate(jobs):
        if rows is my_rows:
            copy = pltpu.make_async_remote_copy(
                own, out.at[rows, my_cols], send.at[1, k], recv.at[1, k],
                device_id={"row": row}, device_id_type=MESH_ID)
            copy.start()
            copies.append(copy)
    for own, out, rows in jobs:
        out[rows, my_cols] = own[...]
    for k, (own, out, rows) in enumerate(jobs):
        first[k].wait_recv()
        if rows is my_rows:
            copy = pltpu.make_async_remote_copy(
                out.at[rows, their_cols], out.at[rows, their_cols], send.at[2, k], recv.at[2, k],
                device_id={"row": row}, device_id_type=MESH_ID)
            copy.start()
            copies.append(copy)
    for copy in copies:
        copy.wait_recv()
    for copy in first + copies:
        copy.wait_send()


def group_gather(x, cot, vec):
    half, width = x.shape
    rows, wide = half * lax.axis_size("row"), width * lax.axis_size("col")
    vmem = pl.BlockSpec(memory_space=pltpu.VMEM)
    return pl.pallas_call(
        gather_body,
        out_shape=[
            jax.ShapeDtypeStruct((rows, wide), x.dtype),
            jax.ShapeDtypeStruct((rows, wide), cot.dtype),
            jax.ShapeDtypeStruct((vec.shape[0], wide), vec.dtype),
        ],
        in_specs=[vmem] * 3,
        out_specs=[vmem] * 3,
        scratch_shapes=[pltpu.SemaphoreType.DMA((3, 3)), pltpu.SemaphoreType.DMA((3, 3))],
        compiler_params=pltpu.CompilerParams(collective_id=1, has_side_effects=True),
        name="group_gather",
    )(x, cot, vec)


def make_scores(query, key, allowed):
    scores = jnp.einsum("hqd,hkd->hqk", query, key, preferred_element_type=F32) * SCALE
    return jnp.where(allowed[None], scores, NEG)


def swap_col(value):
    return lax.ppermute(value, "col", [(0, 1), (1, 0)])


def columns_whole(own, gate):
    col = lax.axis_index("col")
    depth, width = own.shape[1], own.shape[2] // 2
    later = (gate.reshape(-1)[0].astype(F32) * 0.0).astype(jnp.int32)
    got = swap_col(lax.dynamic_slice_in_dim(own, (1 - col) * width + later, width, 2))
    kept = lax.dynamic_slice_in_dim(own, col * width, width, 2)
    low = jnp.where(col == 0, kept, got)
    high = jnp.where(col == 0, got, kept)
    return jnp.concatenate([low, high], axis=1)


def rows_whole(grad):
    col = lax.axis_index("col")
    depth = grad.shape[0] // 2
    got = swap_col(lax.dynamic_slice_in_dim(grad, (1 - col) * depth, depth, 0))
    kept = lax.dynamic_slice_in_dim(grad, col * depth, depth, 0)
    low = jnp.where(col == 0, kept, got)
    high = jnp.where(col == 0, got, kept)
    return jnp.concatenate([low, high], axis=1)


def forward_layer(state, allowed, cosine, sine, params):
    gain1, bias1, gain2, bias2, w_qkv, b_qkv, w_up, b_up, w_out, w_down, b_both = params
    width = state.shape[1]
    mean = jnp.sum(state, axis=1, keepdims=True) / width
    squares = jnp.sum(state * state, axis=1, keepdims=True) / width
    inverse = lax.rsqrt(squares - mean * mean + EPS)
    normed = (state - mean) * inverse
    first = (normed * gain1 + bias1).astype(BF)
    second = (normed * gain2 + bias2).astype(BF)
    rows = state.shape[0]
    qkv = (jnp.dot(first, w_qkv, preferred_element_type=F32) + b_qkv).reshape(rows, -1, 3, HD)
    query = rotate(qkv[:, :, 0], cosine, sine).astype(BF).transpose(1, 0, 2)
    key = rotate(qkv[:, :, 1], cosine, sine).astype(BF).transpose(1, 0, 2)
    value = qkv[:, :, 2].astype(BF).transpose(1, 0, 2)
    scores = make_scores(query, key, allowed)
    top = jnp.max(scores, axis=-1, keepdims=True)
    lse = top + jnp.log(jnp.sum(jnp.exp(scores - top), axis=-1, keepdims=True))
    probs = jnp.exp(scores - lse).astype(BF)
    mixed = jnp.einsum("hqk,hkd->qhd", probs, value, preferred_element_type=F32)
    mixed = mixed.astype(BF).reshape(rows, -1)
    up = jnp.dot(second, w_up, preferred_element_type=F32) + b_up
    act = gelu_exact(up).astype(BF)
    part = jnp.dot(mixed, w_out, preferred_element_type=F32) + jnp.dot(
        act, w_down, preferred_element_type=F32)
    return part, (normed, inverse, first, second, query, key, value, mixed, lse, up, act)


def backward_layer(grad, allowed, cosine, sine, params, cache):
    gain1, bias1, gain2, bias2, w_qkv, b_qkv, w_up, b_up, w_out, w_down, b_both = params
    normed, inverse, first, second, query, key, value, mixed, lse, up, act = cache
    rows, width = grad.shape
    grad_b = grad.astype(BF)
    g_bout = jnp.sum(grad, axis=0)
    grad_mixed = jnp.einsum("td,kd->tk", grad_b, w_out, preferred_element_type=F32).astype(BF)
    grad_act = jnp.einsum("td,kd->tk", grad_b, w_down, preferred_element_type=F32)
    grad_up = grad_act * gelu_slope(up)
    g_bup = jnp.sum(grad_up, axis=0)
    grad_up_b = grad_up.astype(BF)
    scores = make_scores(query, key, allowed)
    probs = jnp.exp(scores - lse)
    grad_heads = grad_mixed.reshape(rows, -1, HD).transpose(1, 0, 2)
    mixed_heads = mixed.reshape(rows, -1, HD).transpose(1, 0, 2)
    delta = jnp.sum(grad_heads.astype(F32) * mixed_heads.astype(F32), axis=-1, keepdims=True)
    grad_value = jnp.einsum("hqk,hqd->khd", probs.astype(BF), grad_heads, preferred_element_type=F32)
    grad_probs = jnp.einsum("hqd,hkd->hqk", grad_heads, value, preferred_element_type=F32)
    grad_scores = (probs * (grad_probs - delta) * SCALE).astype(BF)
    grad_query = jnp.einsum("hqk,hkd->qhd", grad_scores, key, preferred_element_type=F32)
    grad_key = jnp.einsum("hqk,hqd->khd", grad_scores, query, preferred_element_type=F32)
    grad_query = unrotate(grad_query, cosine, sine)
    grad_key = unrotate(grad_key, cosine, sine)
    grad_qkv = jnp.stack([grad_query, grad_key, grad_value], axis=2).reshape(rows, -1)
    g_bqkv = jnp.sum(grad_qkv, axis=0)
    grad_qkv_b = grad_qkv.astype(BF)
    part_first = jnp.einsum("tn,dn->td", grad_qkv_b, w_qkv, preferred_element_type=F32)
    part_second = jnp.einsum("tn,dn->td", grad_up_b, w_up, preferred_element_type=F32)
    part = part_first * gain1 + part_second * gain2
    g_wout = jnp.einsum("tk,td->kd", mixed, grad_b, preferred_element_type=F32)
    g_wdown = jnp.einsum("tk,td->kd", act, grad_b, preferred_element_type=F32)
    g_wqkv = jnp.einsum("td,tn->dn", first, grad_qkv_b, preferred_element_type=F32)
    g_wup = jnp.einsum("td,tn->dn", second, grad_up_b, preferred_element_type=F32)
    shares = lax.axis_size("row") * lax.axis_size("col")
    narrow = jnp.concatenate([
        jnp.stack([
            jnp.sum(part_first * normed, axis=0), jnp.sum(part_first, axis=0),
            jnp.sum(part_second * normed, axis=0), jnp.sum(part_second, axis=0),
            g_bout / shares,
        ]),
        jnp.zeros((3, width), F32),
    ])
    grad_norm, narrow = group_sum(part, narrow)
    centred = (
        grad_norm
        - jnp.sum(grad_norm, axis=1, keepdims=True) / width
        - normed * (jnp.sum(grad_norm * normed, axis=1, keepdims=True) / width)
    )
    grad_x = grad + inverse * centred
    heavy = (g_wqkv.astype(BF), g_wup.astype(BF), g_wout.astype(BF), g_wdown.astype(BF))
    return grad_x, heavy, (g_bqkv, g_bup), narrow


def per_device_plain(
    x_in, cotangent, segment_ids, norm1_gain, norm1_bias, norm2_gain, norm2_bias,
    w_qkv, b_qkv, w_up, b_up, w_out, b_out, w_down, b_down,
):
    half, part_width = x_in.shape
    row = lax.axis_index("row")
    col = lax.axis_index("col")
    length = segment_ids.shape[1]
    layers = w_qkv.shape[0]
    cosine, sine = rope_tables(length)
    places = jnp.arange(length, dtype=jnp.int32)
    labels = segment_ids[0]
    allowed = (places[:, None] >= places[None, :]) & (labels[:, None] == labels[None, :])
    vec = jnp.stack([norm1_gain, norm1_bias, norm2_gain, norm2_bias, b_out + b_down])
    vec = vec.reshape(-1, part_width)
    pad = -vec.shape[0] % 8
    state_in, cot, vec = group_gather(x_in, cotangent.astype(BF), jnp.pad(vec, ((0, pad), (0, 0))))
    grad_in = cot.astype(F32)
    vectors = vec[: vec.shape[0] - pad].reshape(5, layers, -1)
    wide_qkv, wide_up, gate = [], [], vec
    for l in range(layers):
        wide_qkv.append(columns_whole(w_qkv[l : l + 1], gate)[0])
        wide_up.append(columns_whole(w_up[l : l + 1], gate)[0])
        gate = wide_qkv[-1]

    def own(whole):
        return lax.dynamic_slice(whole, (row * half, col * part_width), (half, part_width))

    params = [
        (vectors[0, l], vectors[1, l], vectors[2, l], vectors[3, l], wide_qkv[l], b_qkv[l],
         wide_up[l], b_up[l], w_out[l], w_down[l], vectors[4, l])
        for l in range(layers)
    ]
    state = state_in
    caches = []
    for layer in range(layers):
        part, cache = forward_layer(state, allowed, cosine, sine, params[layer])
        caches.append(cache)
        if layer < layers - 1:
            state = state + group_sum(part) + params[layer][-1]
    y_base = x_in + own(state - state_in + params[-1][-1])
    grad = grad_in
    heavy = [None] * layers
    thin = [None] * layers
    narrow = [None] * layers
    for layer in reversed(range(layers)):
        grad, heavy[layer], thin[layer], narrow[layer] = backward_layer(
            grad, allowed, cosine, sine, params[layer], caches[layer])
    x_grad = cotangent + own(grad - grad_in)
    y_out = y_base + own(group_sum(part))
    summed = []
    for layer in range(layers):
        a, b, c, d = heavy[layer]
        summed.append(lax.psum((rows_whole(a), rows_whole(b), c, d), "dp"))
    g_bqkv, g_bup, narrow = lax.psum((
        jnp.stack([t[0] for t in thin]), jnp.stack([t[1] for t in thin]),
        jnp.stack([t[:5] for t in narrow])), "dp")
    g_wqkv, g_wup, g_wout, g_wdown = (
        jnp.stack([h[k] for h in summed]).astype(F32) for k in range(4))
    narrow = lax.dynamic_slice_in_dim(narrow, col * part_width, part_width, 2)
    g_bout = narrow[:, 4]
    return (
        y_out, x_grad, narrow[:, 0], narrow[:, 1], narrow[:, 2], narrow[:, 3],
        g_wqkv, g_bqkv, g_wup, g_bup, g_wout, g_bout, g_wdown, g_bout,
    )


BLK = 128
TICKS = (3, 4, 4, 6, 6, 4, 4, 4, 4, 4)


def tdot(a, b):
    return lax.dot_general(a, b, (((0,), (0,)), ((), ())), preferred_element_type=F32)


def ntdot(a, b):
    return lax.dot_general(a, b, (((1,), (1,)), ((), ())), preferred_element_type=F32)


def ndot(a, b):
    return jnp.dot(a, b, preferred_element_type=F32)


def whole_body(
    n, x, cot, seg, n1g, n1b, n2g, n2b, bq, bu, bo, bd, cosr, sinr, wq_in, wu_in, wo_in, wd_in,
    y, xg, od, ow, ou, oq, osm,
    wq, wu, wo, wd, xb, cb, vec, mask, st, nrm, inv, fst, snd, act, slope, qkv_t, qh, p_t, m_t,
    gm_t, gub, gqb_t, gq, gb, own, sb, got_row, mine, got_col, back, back_got,
    ind, inw, iu, iq, ism, rdp, rdm, rw, ru, rq, rsm, swu, swq,
    nar, nar_got, thin, send, recv, local,
):
    layers = wq.shape[0]
    gq_t = qkv_t
    half, cols = x.shape
    length, width = half * 2, cols * 2
    hid = wu.shape[2]
    heads = p_t.shape[1]
    qw = heads * 3 * HD
    row, col, here = lax.axis_index("row"), lax.axis_index("col"), lax.axis_index("dp")
    orow, ocol = 1 - row, 1 - col
    odd = lax.rem(here, 2)
    pos = here // 2 + odd * (n - 1 - 2 * (here // 2))

    def device(place):
        late = place // (n // 2)
        return 2 * (place + late * (n - 1 - 2 * place)) + late

    targets = (device(lax.rem(pos + 1, n)), device(lax.rem(pos + n - 1, n)))
    beside = here + 1 - 2 * odd
    high = lax.rem(here // 2, 2)
    along = here + 2 - 4 * high
    barrier = pltpu.get_barrier_semaphore()
    pl.semaphore_signal(barrier, inc=1, device_id={"dp": beside}, device_id_type=MESH_ID)
    pl.semaphore_signal(barrier, inc=1, device_id={"dp": along}, device_id_type=MESH_ID)
    pl.semaphore_signal(barrier, inc=1, device_id={"dp": targets[0]}, device_id_type=MESH_ID)
    pl.semaphore_signal(barrier, inc=1, device_id={"dp": targets[1]}, device_id_type=MESH_ID)
    pl.semaphore_signal(barrier, inc=1, device_id={"col": ocol}, device_id_type=MESH_ID)
    pl.semaphore_signal(barrier, inc=1, device_id={"row": orow}, device_id_type=MESH_ID)

    count = [0]
    sent = []

    def rc(src, dst, axis, target):
        k = count[0]
        count[0] += 1
        copy = pltpu.make_async_remote_copy(
            src, dst, send.at[k], recv.at[k], device_id={axis: target}, device_id_type=MESH_ID)
        copy.start()
        sent.append(copy)
        return copy

    def over_row(src, dst):
        return rc(src, dst, "row", orow)

    def over_col(src, dst):
        return rc(src, dst, "col", ocol)

    def at(base, size, step=None):
        return pl.ds(pl.multiple_of(base, step or size), size)

    my_rows, their_rows = at(row * half, half), at(orow * half, half)
    my_cols, their_cols = at(col * cols, cols), at(ocol * cols, cols)
    shift = wq_in.shape[2] - wq.shape[2]
    my_heads, their_heads = at(col * shift, wq.shape[2], BLK), at(ocol * shift, wq.shape[2], BLK)
    my_hid, their_hid = at(col * hid, hid), at(ocol * hid, hid)

    loads = []
    for l in range(layers):
        loads.append([
            pltpu.make_async_copy(wq_in.at[l, :, my_heads], wq.at[l, my_cols], local.at[l, 0]),
            pltpu.make_async_copy(wu_in.at[l, :, my_hid], wu.at[l, my_cols], local.at[l, 1]),
            pltpu.make_async_copy(wo_in.at[l], wo.at[l], local.at[l, 2]),
            pltpu.make_async_copy(wd_in.at[l], wd.at[l], local.at[l, 3]),
        ])
        for copy in loads[-1]:
            copy.start()

    xb[my_rows, my_cols] = x[...].astype(BF)
    cb[my_rows, my_cols] = cot[...].astype(BF)
    for k, ref in enumerate((n1g, n1b, n2g, n2b)):
        vec[2 * k : 2 * k + 2, my_cols] = ref[...]
    vec[8:10, my_cols] = bo[...] + bd[...]
    pl.semaphore_wait(barrier, 6)

    x_col = over_col(xb.at[my_rows, my_cols], xb.at[my_rows, my_cols])
    x_row = over_row(xb.at[my_rows, my_cols], xb.at[my_rows, my_cols])
    v_col = over_col(vec.at[:, my_cols], vec.at[:, my_cols])

    some = cols // 4
    few = some // 2
    mine_of, y_of, z_of = odd + 2 * high, 1 - odd + 2 * high, odd + 2 * (1 - high)

    def fetch(kind, l):
        src, lanes, dst = ((wq_in, their_heads, wq), (wu_in, their_hid, wu))[kind]
        return dst, l, over_col(
            src.at[l, at(mine_of * some, some), lanes], dst.at[l, at(col * cols + mine_of * some, some)])

    def spread(got):
        dst, l, copy = got
        copy.wait_recv()
        spot = dst.at[l, at(ocol * cols + mine_of * some, some)]
        return dst, l, rc(spot, spot, "dp", beside), rc(spot, spot, "dp", along)

    def relay(got):
        dst, l, by_y, by_z = got
        by_y.wait_recv()
        spot = dst.at[l, at(ocol * cols + y_of * some, few)]
        on_z = rc(spot, spot, "dp", along)
        by_z.wait_recv()
        spot = dst.at[l, at(ocol * cols + z_of * some + few, few, few)]
        return on_z, rc(spot, spot, "dp", beside)

    def arrived(got):
        for copy in got:
            copy.wait_recv()

    q_0, u_0 = fetch(0, 0), fetch(1, 0)
    c_row = over_row(cb.at[my_rows, my_cols], cb.at[my_rows, my_cols])

    label = seg[...].astype(F32)
    tall = jnp.broadcast_to(label, (BLK, length)).T
    for k in range(length // BLK):
        here_rows = slice(k * BLK, (k + 1) * BLK)
        key_at = lax.broadcasted_iota(jnp.int32, (BLK, length), 0) + k * BLK
        query_at = lax.broadcasted_iota(jnp.int32, (BLK, length), 1)
        same = tall[here_rows, 0:1] == label
        mask[here_rows, :] = jnp.where(same & (key_at <= query_at), 0.0, NEG)
    nar[...] = jnp.zeros_like(nar)
    offset = col * (wq.shape[2] - qw)

    x_col.wait_recv()
    x_over = over_row(xb.at[my_rows, their_cols], xb.at[my_rows, their_cols])
    v_col.wait_recv()
    x_row.wait_recv()
    x_over.wait_recv()

    def gain(k, l):
        return vec[2 * k + l : 2 * k + l + 1, :]

    blocks = length // BLK

    def norm_step(l):
        @pl.loop(0, blocks)
        def _(i):
            rows = at(i * BLK, BLK)
            s = xb[rows, :].astype(F32) if l == 0 else st[rows, :]
            mean = jnp.sum(s, axis=1, keepdims=True) / width
            squares = jnp.sum(s * s, axis=1, keepdims=True) / width
            inverse = lax.rsqrt(squares - mean * mean + EPS)
            normed = (s - mean) * inverse
            inv[l, rows, :] = inverse
            nrm[l, rows, :] = normed.astype(BF)
            fst[l, rows, :] = (normed * gain(0, l) + gain(1, l)).astype(BF)
            snd[l, rows, :] = (normed * gain(2, l) + gain(3, l)).astype(BF)

    def qkv_step(l):
        @pl.loop(0, blocks)
        def _(i):
            rows = at(i * BLK, BLK)
            got = ndot(fst[l, rows, :], wq[l]) + bq[l : l + 1, :]
            qkv_t[:, rows] = got.T

    def turn(v, sign):
        a, b = v[0:8], v[8:16]
        c, s = cosr[...], sinr[...] * sign
        return jnp.concatenate([a * c - b * s, b * c + a * s, v[16:]], axis=0)

    QB = length // 2

    def attention_step(l):
        @pl.loop(0, heads)
        def _(h):
            base = offset + h * (3 * HD)
            q = turn(qkv_t[at(base, HD), :], 1.0).astype(BF)
            k = turn(qkv_t[at(base + HD, HD), :], 1.0).astype(BF)
            v = qkv_t[at(base + 2 * HD, HD), :].astype(BF)
            spot = h * (3 * HD)
            qh[l, at(spot, HD), :] = q
            qh[l, at(spot + HD, HD), :] = k
            qh[l, at(spot + 2 * HD, HD), :] = v
            q = q * jnp.asarray(SCALE, BF)
            for b in range(2):
                keys, these = slice(0, (b + 1) * QB), slice(b * QB, (b + 1) * QB)
                scores = tdot(k[:, keys], q[:, these]) + mask[keys, these]
                top = jnp.max(scores, axis=0, keepdims=True)
                e = jnp.exp(scores - top)
                total = jnp.sum(e, axis=0, keepdims=True)
                probs = (e * (1.0 / total)).astype(BF)
                p_t[l, h, keys, these] = probs
                m_t[l, at(h * HD, HD), these] = ndot(v[:, keys], probs).astype(BF)

    def up_step(l):
        @pl.loop(0, blocks)
        def _(i):
            rows = at(i * BLK, BLK)
            up = ndot(snd[l, rows, :], wu[l]) + bu[l : l + 1, :]
            phi = 0.5 * (1.0 + lax.erf(up * INV_ROOT2))
            act[l, rows, :] = (up * phi).astype(BF)
            slope[l, rows, :] = (phi + up * jnp.exp(-0.5 * up * up) * INV_ROOT_TWO_PI).astype(BF)

    def part_rows(l):
        def run(base):
            rows = at(base, BLK)
            return tdot(m_t[l, :, rows], wo[l]) + ndot(act[l, rows, :], wd[l])
        return run

    pieces = half // BLK

    def sum_begin(k, fn):
        flight = []
        for p in range(pieces):
            here = slice(p * BLK, (p + 1) * BLK)
            sb[k, here, :] = fn(orow * half + p * BLK).astype(BF)
            flight.append(over_row(sb.at[k, here], got_row.at[k, here]))
        for p in range(pieces):
            here = slice(p * BLK, (p + 1) * BLK)
            own[k % 2, here, :] = fn(row * half + p * BLK)
        return flight

    def sum_cross(k, flight, narrow=False):
        crossing = []
        for p in range(pieces):
            here = slice(p * BLK, (p + 1) * BLK)
            flight[p].wait_recv()
            t = own[k % 2, here, :] + got_row[k, here, :].astype(F32)
            own[k % 2, here, :] = t
            mine[k, here, :] = t.astype(BF)
            if narrow:
                crossing.append(over_col(
                    mine.at[k, here, their_cols], got_col.at[k, here, their_cols]))
            else:
                crossing.append(over_col(mine.at[k, here], got_col.at[k, here]))
        return crossing


    norm_step(0)
    q_0 = spread(q_0)
    u_0 = spread(u_0)
    c_col = over_col(cb.at[my_rows, my_cols], cb.at[my_rows, my_cols])
    u_1, q_1 = fetch(1, 1), fetch(0, 1)
    q_0 = relay(q_0)
    u_0 = relay(u_0)
    loads[0][0].wait()
    arrived(q_0)
    qkv_step(0)
    attention_step(0)
    loads[0][1].wait()
    arrived(u_0)
    up_step(0)
    loads[0][2].wait()
    loads[0][3].wait()
    flight = sum_begin(0, part_rows(0))
    crossing = sum_cross(0, flight)
    u_1 = spread(u_1)
    q_1 = spread(q_1)
    c_col.wait_recv()
    c_over = over_row(cb.at[my_rows, their_cols], cb.at[my_rows, their_cols])
    both = vec[8:9, :]
    returned = []
    for p in range(pieces):
        here = slice(p * BLK, (p + 1) * BLK)
        crossing[p].wait_recv()
        total = own[0, here, :] + got_col[0, here, :].astype(F32)
        own[0, here, :] = total
        back[0, here, :] = total.astype(BF)
        returned.append(over_row(back.at[0, here], back_got.at[0, here]))
    for p in range(pieces):
        here = slice(p * BLK, (p + 1) * BLK)
        rows = at(row * half + p * BLK, BLK)
        st[rows, :] = xb[rows, :].astype(F32) + own[0, here, :] + both
    y[...] = x[...] + own[0, :, my_cols] + vec[8:9, my_cols] + vec[9:10, my_cols]
    u_1 = relay(u_1)
    q_1 = relay(q_1)
    for p in range(pieces):
        here = slice(p * BLK, (p + 1) * BLK)
        returned[p].wait_recv()
        rows = at(orow * half + p * BLK, BLK)
        st[rows, :] = xb[rows, :].astype(F32) + back_got[0, here, :].astype(F32) + both

    def chunk(d, behind):
        sign = 1 if d == 0 else -1
        return lax.rem(pos - sign * behind + 2 * n, n)

    def stream(d, parts, swap=None):
        def go(pairs):
            return [rc(src, dst, "dp", targets[d]) for src, dst in pairs]
        copies = go([(rin(chunk(d, 0)), got(0)) for rin, got, out in parts])
        for s in range(n - 1):
            yield
            for k, (rin, got, out) in enumerate(parts):
                copies[k].wait_recv()
                got(s)[...] = got(s)[...] + rin(chunk(d, s + 1))[...]
                if s < n - 2:
                    copies[k] = go([(got(s), got(s + 1))])[0]
        where = chunk(d, n - 1)
        if swap is None:
            for rin, got, out in parts:
                out(where)[...] = got(n - 2)[...]
        else:
            last, out = parts[0][1](n - 2), parts[0][2]
            over = over_col(last.at[ocol], swap)
            yield
            over.wait_recv()
            wide = last.shape[2]
            if wide % BLK == 0:
                out(where).at[:, at(col * wide, wide)][...] = last[col]
                out(where).at[:, at(ocol * wide, wide)][...] = swap[...]
            else:
                a, b = last[col].astype(F32), swap[...].astype(F32)
                first = col == 0
                out(where)[...] = jnp.concatenate(
                    [jnp.where(first, a, b), jnp.where(first, b, a)], axis=1).astype(BF)
        copies = go([(out(where), out(where)) for rin, got, out in parts])
        for s in range(n - 1):
            yield
            for k, (rin, got, out) in enumerate(parts):
                copies[k].wait_recv()
                if s < n - 2:
                    where = chunk(d, s)
                    copies[k] = go([(out(where), out(where))])[0]

    active = []

    def launch(*args, **kw):
        g = stream(*args, **kw)
        next(g)
        active.append(g)

    def pump(times):
        for _ in range(times):
            if active:
                g = active.pop(0)
                try:
                    next(g)
                    active.append(g)
                except StopIteration:
                    pass

    deep = hid // n
    cut = deep // 2

    def tick(k):
        pump(TICKS[k])

    def down_step(l, g):
        for k in range(2):
            f = slice(k * (hid // 2), (k + 1) * (hid // 2))
            got = tdot(act[l, :, f], g[...]).astype(BF)
            ind[l, k * (n // 2) : (k + 1) * (n // 2)] = got.reshape(n // 2, deep, width)
        launch(0, [(lambda c: ind.at[l, c, 0:cut], lambda s: rdp.at[l, s],
                    lambda c: od.at[l, at(c * deep, cut, cut)])])
        launch(1, [(lambda c: ind.at[l, c, cut:deep], lambda s: rdm.at[l, s],
                    lambda c: od.at[l, at(c * deep + cut, cut, cut)])])

    def out_step(l, g):
        got = ndot(m_t[l], g[...]).reshape(n, -1, width)
        pad = jnp.zeros((n, inw.shape[2] - got.shape[1], width), F32)
        inw[l] = jnp.concatenate([got, pad], axis=1).astype(BF)
        launch(1, [(lambda c: inw.at[l, c], lambda s: rw.at[l, s], lambda c: ow.at[l, c])])

    def up_grad_step(l):
        for k in range(2):
            f = slice(k * cols, (k + 1) * cols)
            got = tdot(snd[l, :, f], gub[...]).astype(BF)
            iu[l, :, k] = got.reshape(n, -1, hid)
        launch(0, [(lambda c: iu.at[l, c], lambda s: ru.at[l, s],
                    lambda c: ou.at[l, at(c * iu.shape[3], iu.shape[3])])], swap=swu.at[l])

    def qkv_grad_step(l):
        for k in range(2):
            f = slice(k * cols, (k + 1) * cols)
            got = ntdot(fst[l, :, f].T, gqb_t[...]).astype(BF)
            iq[l, :, k] = got.reshape(n, -1, qw)
        launch(1, [(lambda c: iq.at[l, c], lambda s: rq.at[l, s],
                    lambda c: oq.at[l, at(c * iq.shape[3], iq.shape[3])])], swap=swq.at[l])

    def grad_up_step(l, g):
        def block(i, total):
            rows = at(i * BLK, BLK)
            gu = ntdot(g[rows, :], wd[l]) * slope[l, rows, :].astype(F32)
            gub[rows, :] = gu.astype(BF)
            return total + jnp.sum(gu, axis=0, keepdims=True)
        total = lax.fori_loop(0, blocks, block, jnp.zeros((1, hid), F32))
        thin[l, 1:2, 0:hid] = total

    def attention_back_step(l, g):
        gm_t[...] = ntdot(wo[l], g[...]).astype(BF)

        @pl.loop(0, heads)
        def _(h):
            spot = h * (3 * HD)
            q = qh[l, at(spot, HD), :]
            k = qh[l, at(spot + HD, HD), :]
            v = qh[l, at(spot + 2 * HD, HD), :]
            gm = gm_t[at(h * HD, HD), :]
            mixed = m_t[l, at(h * HD, HD), :]
            delta = jnp.sum(gm.astype(F32) * mixed.astype(F32), axis=0, keepdims=True)
            gqs, gks, gvs = [], [], []
            for b in range(2):
                keys, these = slice(0, (b + 1) * QB), slice(b * QB, (b + 1) * QB)
                probs = p_t[l, h, keys, these]
                gp = tdot(v[:, keys], gm[:, these])
                ds = (probs.astype(F32) * (gp - delta[:, these])).astype(BF)
                gqs.append(ndot(k[:, keys], ds))
                gks.append(ntdot(q[:, these], ds))
                gvs.append(ntdot(gm[:, these], probs))
            gq_h = jnp.concatenate(gqs, axis=1) * SCALE
            gk_h = jnp.concatenate([gks[0] + gks[1][:, :QB], gks[1][:, QB:]], axis=1) * SCALE
            gv_h = jnp.concatenate([gvs[0] + gvs[1][:, :QB], gvs[1][:, QB:]], axis=1)
            base = offset + spot
            for k3, value in enumerate((turn(gq_h, -1.0), turn(gk_h, -1.0), gv_h)):
                gq_t[at(base + k3 * HD, HD), :] = value
                gqb_t[at(spot + k3 * HD, HD), :] = value.astype(BF)

        total = jnp.zeros((1, gq_t.shape[0]), F32)
        for i in range(blocks):
            flat = gq_t[:, i * BLK : (i + 1) * BLK].T
            gq[i * BLK : (i + 1) * BLK, :] = flat.astype(BF)
            total = total + jnp.sum(flat, axis=0, keepdims=True)
        thin[l, 0:1, :] = jnp.concatenate([total, jnp.zeros((1, width - total.shape[1]), F32)], axis=1)

    def back_rows(l):
        def run(base):
            rows = at(base, BLK)
            gf = ntdot(gq[rows, :], wq[l])
            gs = ntdot(gub[rows, :], wu[l])
            normed = nrm[l, rows, :].astype(F32)
            for k, value in enumerate((gf * normed, gf, gs * normed, gs)):
                nar[l, 0, k : k + 1, :] += jnp.sum(value, axis=0, keepdims=True)
            return gf * gain(0, l) + gs * gain(2, l)
        return run

    def centred(l, rows, total):
        normed = nrm[l, rows, :].astype(F32)
        return inv[l, rows, :] * (
            total - jnp.sum(total, axis=1, keepdims=True) / width
            - normed * (jnp.sum(total * normed, axis=1, keepdims=True) / width))

    shares = 0.25
    norm_step(1)
    loads[1][1].wait()
    arrived(u_1)
    up_step(1)
    c_row.wait_recv()
    c_over.wait_recv()
    loads[1][2].wait()
    loads[1][3].wait()
    down_step(1, cb)
    grad_up_step(1, cb)
    up_grad_step(1)
    loads[1][0].wait()
    arrived(q_1)
    qkv_step(1)
    tick(0)
    attention_step(1)
    tick(1)
    out_step(1, cb)
    nar[1, 0, 4:5, :] = jnp.sum(cb[...].astype(F32), axis=0, keepdims=True) * shares
    gq_t[...] = jnp.zeros_like(gq_t)
    attention_back_step(1, cb)
    tick(2)
    flight = sum_begin(1, back_rows(1))
    nar_row = over_row(nar.at[1, 0], nar_got.at[1, 0])
    qkv_grad_step(1)
    crossing = sum_cross(1, flight)
    tick(3)
    returned = []
    for p in range(pieces):
        here = slice(p * BLK, (p + 1) * BLK)
        crossing[p].wait_recv()
        total = own[1, here, :] + got_col[1, here, :].astype(F32)
        own[1, here, :] = total
        back[1, here, :] = total.astype(BF)
        returned.append(over_row(back.at[1, here], back_got.at[1, here]))
    bout = jnp.zeros((1, width), F32)
    for p in range(pieces):
        here = slice(p * BLK, (p + 1) * BLK)
        rows = at(row * half + p * BLK, BLK)
        change = centred(1, rows, own[1, here, :])
        own[1, here, :] = change
        grad = cb[rows, :].astype(F32) + change
        gb[rows, :] = grad.astype(BF)
        bout = bout + jnp.sum(grad, axis=0, keepdims=True)
    xg[...] = cot[...] + own[1, :, my_cols]
    for p in range(pieces):
        here = slice(p * BLK, (p + 1) * BLK)
        returned[p].wait_recv()
        rows = at(orow * half + p * BLK, BLK)
        grad = cb[rows, :].astype(F32) + centred(1, rows, back_got[1, here, :].astype(F32))
        gb[rows, :] = grad.astype(BF)
        bout = bout + jnp.sum(grad, axis=0, keepdims=True)
    nar[0, 0, 4:5, :] = bout * shares
    nar_row.wait_recv()
    nar[1, 1] = nar[1, 0] + nar_got[1, 0]
    nar_col = over_col(nar.at[1, 1], nar_got.at[1, 1])
    tick(4)
    down_step(0, gb)
    tick(5)
    out_step(0, gb)
    grad_up_step(0, gb)
    up_grad_step(0)
    tick(6)
    attention_back_step(0, gb)
    tick(7)
    flight_x = sum_begin(3, back_rows(0))
    nar_row0 = over_row(nar.at[0, 0], nar_got.at[0, 0])
    qkv_grad_step(0)
    tick(8)
    crossing_x = sum_cross(3, flight_x)
    nar_row0.wait_recv()
    nar[0, 1] = nar[0, 0] + nar_got[0, 0]
    nar_col0 = over_col(nar.at[0, 1], nar_got.at[0, 1])
    tick(9)
    nar_col.wait_recv()
    nar_col0.wait_recv()
    ism[...] = jnp.zeros_like(ism)
    ism[0] = jnp.concatenate(
        [v for l in range(layers) for v in (
            nar[l, 1, 0:5, :] + nar_got[l, 1, 0:5, :], thin[l, 0:2, :], jnp.zeros((1, width), F32))],
        axis=0).astype(BF)
    launch(0, [(lambda c: ism.at[c], lambda s: rsm.at[s], lambda c: osm.at[c])])
    pump(2)
    flight_y = sum_begin(2, part_rows(1))
    crossing_y = sum_cross(2, flight_y, narrow=True)
    pump(2)
    for p in range(pieces):
        here = slice(p * BLK, (p + 1) * BLK)
        crossing_x[p].wait_recv()
        rows = at(row * half + p * BLK, BLK)
        own[1, here, :] = centred(0, rows, own[1, here, :] + got_col[3, here, :].astype(F32))
    xg[...] += own[1, :, my_cols]
    pump(2)
    for p in range(pieces):
        crossing_y[p].wait_recv()
    y[...] += own[0, :, my_cols] + got_col[2, :, my_cols].astype(F32)
    while active:
        pump(1)
    for copy in sent:
        copy.wait_send()


def whole_step(x, cot, seg, n1g, n1b, n2g, n2b, wq_in, bq, wu_in, bu, wo_in, bo, wd_in, bd):
    n = lax.axis_size("dp")
    half, cols = x.shape
    layers, _, both_heads = wq_in.shape
    length, width = 2 * half, 2 * cols
    hid = wu_in.shape[2] // 2
    qw = both_heads // 2
    heads = qw // (3 * HD)
    wide = -(-qw // BLK) * BLK
    mix = wo_in.shape[1]
    col = lax.axis_index("col")
    freq = np.float32(10000.0) ** (-(np.arange(ROT // 2, dtype=np.float32) * 2) / np.float32(ROT))
    angle = freq[:, None] * np.arange(length, dtype=np.float32)[None, :]
    cosr, sinr = jnp.asarray(np.cos(angle), F32), jnp.asarray(np.sin(angle), F32)
    bq = lax.dynamic_update_slice(jnp.zeros((layers, wide), F32), bq, (0, col * (wide - qw)))
    per, deep, flat = width // 2 // n, hid // n, mix // n
    cut = deep // 2
    tall = flat + -flat % 16
    small = 8 * layers
    vmem = pl.BlockSpec(memory_space=pltpu.VMEM)
    anyw = pl.BlockSpec(memory_space=pl.ANY)
    V = pltpu.VMEM
    sums = 4
    sems = 256
    out = pl.pallas_call(
        lambda *refs: whole_body(n, *refs),
        out_shape=[
            jax.ShapeDtypeStruct((half, cols), F32), jax.ShapeDtypeStruct((half, cols), F32),
            jax.ShapeDtypeStruct((layers, hid, width), BF),
            jax.ShapeDtypeStruct((layers, n, tall, width), BF),
            jax.ShapeDtypeStruct((layers, width // 2, 2 * hid), BF),
            jax.ShapeDtypeStruct((layers, width // 2, 2 * qw), BF),
            jax.ShapeDtypeStruct((n, small, width), BF),
        ],
        in_specs=[vmem] * 13 + [anyw] * 4,
        out_specs=[vmem] * 7,
        scratch_shapes=[
            V((layers, width, wide), BF), V((layers, width, hid), BF),
            V((layers, mix, width), BF), V((layers, hid, width), BF),
            V((length, width), BF), V((length, width), BF), V((16, width), F32),
            V((length, length), F32), V((length, width), F32),
            V((layers, length, width), BF), V((layers, length, 1), F32),
            V((layers, length, width), BF), V((layers, length, width), BF),
            V((layers, length, hid), BF), V((layers, length, hid), BF),
            V((wide, length), F32), V((layers, qw, length), BF),
            V((layers, heads, length, length), BF), V((layers, mix, length), BF),
            V((mix, length), BF), V((length, hid), BF),
            V((qw, length), BF), V((length, wide), BF), V((length, width), BF),
            V((2, half, width), F32), V((sums, half, width), BF), V((sums, half, width), BF),
            V((sums, half, width), BF), V((sums, half, width), BF),
            V((2, half, width), BF), V((2, half, width), BF),
            V((layers, n, deep, width), BF), V((layers, n, tall, width), BF),
            V((layers, n, 2, per, hid), BF), V((layers, n, 2, per, qw), BF),
            V((n, small, width), BF),
            V((layers, n - 1, cut, width), BF), V((layers, n - 1, deep - cut, width), BF),
            V((layers, n - 1, tall, width), BF),
            V((layers, n - 1, 2, per, hid), BF), V((layers, n - 1, 2, per, qw), BF),
            V((n - 1, small, width), BF),
            V((layers, per, hid), BF), V((layers, per, qw), BF),
            V((layers, 2, 8, width), F32), V((layers, 2, 8, width), F32),
            V((layers, 2, width), F32),
            pltpu.SemaphoreType.DMA((sems,)), pltpu.SemaphoreType.DMA((sems,)),
            pltpu.SemaphoreType.DMA((layers, 4)),
        ],
        compiler_params=pltpu.CompilerParams(
            collective_id=5, has_side_effects=True, vmem_limit_bytes=62 * 1024 * 1024),
        name="whole_step",
    )(x, cot, seg, n1g, n1b, n2g, n2b, bq, bu, bo, bd, cosr, sinr, wq_in, wu_in, wo_in, wd_in)
    y, xg, d, w, u, q, s = out
    g_wqkv, g_wup, g_wdown = q.astype(F32), u.astype(F32), d.astype(F32)
    g_wout = w[:, :, :flat].reshape(layers, mix, width).astype(F32)
    s = s[0].astype(F32).reshape(layers, 8, width)
    narrow = lax.dynamic_slice_in_dim(s[:, :5], col * cols, cols, 2)
    g_bqkv = lax.dynamic_slice_in_dim(s[:, 5], col * (wide - qw), qw, 1)
    g_bup = s[:, 6, :hid]
    g_bout = narrow[:, 4]
    return (
        y, xg, narrow[:, 0], narrow[:, 1], narrow[:, 2], narrow[:, 3],
        g_wqkv, g_bqkv, g_wup, g_bup, g_wout, g_bout, g_wdown, g_bout)


def per_device(*args):
    x, wq, wo, wd = args[0], args[7], args[11], args[13]
    n = lax.axis_size("dp")
    parts = lax.axis_size("row"), lax.axis_size("col")
    cols = x.shape[1]
    fits = (
        parts == (2, 2) and n % 2 == 0 and n >= 4 and cols % n == 0 and (cols // n) % 16 == 0
        and (wd.shape[1] // n) % 32 == 0 and (wo.shape[1] // n) % 8 == 0 and wq.shape[0] == 2)
    return whole_step(*args) if fits else per_device_plain(*args)


def solution(mesh):
    in_specs = (
        P(("dp", "row"), "col"),
        P(("dp", "row"), "col"),
        P("dp", None),
        P(None, "col"),
        P(None, "col"),
        P(None, "col"),
        P(None, "col"),
        P(None, "col", "row"),
        P(None, ("row", "col")),
        P(None, "col", "row"),
        P(None, ("row", "col")),
        P(None, ("row", "col"), None),
        P(None, "col"),
        P(None, ("row", "col"), None),
        P(None, "col"),
    )
    out_specs = (
        P(("dp", "row"), "col"),
        P(("dp", "row"), "col"),
        P(None, "col"),
        P(None, "col"),
        P(None, "col"),
        P(None, "col"),
        P(None, "col", "row"),
        P(None, ("row", "col")),
        P(None, "col", "row"),
        P(None, ("row", "col")),
        P(None, ("row", "col"), None),
        P(None, "col"),
        P(None, ("row", "col"), None),
        P(None, "col"),
    )
    return jax.shard_map(
        per_device, mesh=mesh, in_specs=in_specs, out_specs=out_specs, check_vma=False
    )
```

```python
import jax
import jax.numpy as jnp
import numpy as np
from jax import lax
from jax.experimental import pallas as pl
from jax.experimental.pallas import tpu as pltpu
from jax.sharding import PartitionSpec as P

D = 768
HD = 64
ROT = 16
LAYERS = 2


EPS = 1e-05
NEG = -1e30
SCALE = 0.125
INV_ROOT2 = 0.7071067811865476
INV_ROOT_TWO_PI = 0.3989422804014327


def rope_tables(length):
    half = ROT // 2
    freq = 10000.0 ** (-(jnp.arange(half, dtype=jnp.float32) * 2.0) / ROT)
    angle = jnp.arange(length, dtype=jnp.float32)[:, None] * freq[None, :]
    cosine = jnp.concatenate([jnp.cos(angle), jnp.cos(angle)], axis=1)
    sine = jnp.concatenate([jnp.sin(angle), jnp.sin(angle)], axis=1)
    return (cosine, sine)


def rotate(values, cosine, sine):
    part = values[..., :ROT]
    lower = part[..., : ROT // 2]
    upper = part[..., ROT // 2 :]
    turned = jnp.concatenate([-upper, lower], axis=-1)
    moved = part * cosine[:, None, :] + turned * sine[:, None, :]
    return jnp.concatenate([moved, values[..., ROT:]], axis=-1)


def unrotate(grads, cosine, sine):
    part = grads[..., :ROT]
    lower = part[..., : ROT // 2]
    upper = part[..., ROT // 2 :]
    turned = jnp.concatenate([upper, -lower], axis=-1)
    moved = part * cosine[:, None, :] + turned * sine[:, None, :]
    return jnp.concatenate([moved, grads[..., ROT:]], axis=-1)


def gelu_exact(values):
    return 0.5 * values * (1.0 + jax.scipy.special.erf(values * INV_ROOT2))


def gelu_slope(values):
    return (
        0.5 * (1.0 + jax.scipy.special.erf(values * INV_ROOT2))
        + values * jnp.exp(-0.5 * values * values) * INV_ROOT_TWO_PI
    )


BF = jnp.bfloat16
F32 = jnp.float32
MESH_ID = pl.DeviceIdType.MESH
PIECES = 4


def greet():
    row = 1 - lax.axis_index("row")
    col = 1 - lax.axis_index("col")
    barrier = pltpu.get_barrier_semaphore()
    pl.semaphore_signal(barrier, inc=1, device_id={"row": row}, device_id_type=MESH_ID)
    pl.semaphore_signal(barrier, inc=1, device_id={"col": col}, device_id_type=MESH_ID)
    pl.semaphore_wait(barrier, 2)
    return row, col


def reduce_body(*refs):
    if len(refs) == 7:
        part, out, got_row, mine, got_col, send, recv = refs
        extra = None
    else:
        part, extra, out, extra_out, got_row, mine, got_col, pair, got_extra, send, recv = refs
    half = mine.shape[0]
    piece = half // PIECES
    row, col = greet()
    own = (1 - row) * half
    theirs = row * half
    first, second, third = [], [], []
    for k in range(PIECES):
        at = pl.multiple_of(theirs + k * piece, piece)
        copy = pltpu.make_async_remote_copy(
            part.at[pl.ds(at, piece)], got_row.at[pl.ds(k * piece, piece)],
            send.at[0, k], recv.at[0, k], device_id={"row": row}, device_id_type=MESH_ID)
        copy.start()
        first.append(copy)
    if extra is not None:
        over_row = pltpu.make_async_remote_copy(
            extra, got_extra.at[0], send.at[3, 0], recv.at[3, 0],
            device_id={"row": row}, device_id_type=MESH_ID)
        over_row.start()
    for k in range(PIECES):
        here = pl.ds(k * piece, piece)
        at = pl.multiple_of(own + k * piece, piece)
        first[k].wait_recv()
        mine[here, :] = (part[pl.ds(at, piece), :] + got_row[here, :]).astype(BF)
        copy = pltpu.make_async_remote_copy(
            mine.at[here], got_col.at[here], send.at[1, k], recv.at[1, k],
            device_id={"col": col}, device_id_type=MESH_ID)
        copy.start()
        second.append(copy)
    if extra is not None:
        over_row.wait_recv()
        pair[...] = extra[...] + got_extra[0]
        over_col = pltpu.make_async_remote_copy(
            pair, got_extra.at[1], send.at[3, 1], recv.at[3, 1],
            device_id={"col": col}, device_id_type=MESH_ID)
        over_col.start()
    for k in range(PIECES):
        here = pl.ds(k * piece, piece)
        at = pl.multiple_of(own + k * piece, piece)
        second[k].wait_recv()
        out[pl.ds(at, piece), :] = mine[here, :].astype(F32) + got_col[here, :].astype(F32)
        copy = pltpu.make_async_remote_copy(
            out.at[pl.ds(at, piece)], out.at[pl.ds(at, piece)], send.at[2, k], recv.at[2, k],
            device_id={"row": row}, device_id_type=MESH_ID)
        copy.start()
        third.append(copy)
    if extra is not None:
        over_col.wait_recv()
        extra_out[...] = pair[...] + got_extra[1]
        over_row.wait_send()
        over_col.wait_send()
    for k in range(PIECES):
        third[k].wait_recv()
        for copy in (first[k], second[k], third[k]):
            copy.wait_send()


def group_sum(part, extra=None):
    rows, width = part.shape
    half = rows // lax.axis_size("row")
    vmem = pl.BlockSpec(memory_space=pltpu.VMEM)
    out_shape = [jax.ShapeDtypeStruct((rows, width), F32)]
    scratch = [pltpu.VMEM((half, width), F32), pltpu.VMEM((half, width), BF),
               pltpu.VMEM((half, width), BF)]
    args = [part]
    if extra is not None:
        args.append(extra)
        out_shape.append(jax.ShapeDtypeStruct(extra.shape, F32))
        scratch += [pltpu.VMEM(extra.shape, F32), pltpu.VMEM((2,) + extra.shape, F32)]
    result = pl.pallas_call(
        reduce_body,
        out_shape=out_shape,
        in_specs=[vmem] * len(args),
        out_specs=[vmem] * len(out_shape),
        scratch_shapes=scratch + [
            pltpu.SemaphoreType.DMA((4, PIECES)), pltpu.SemaphoreType.DMA((4, PIECES))],
        compiler_params=pltpu.CompilerParams(
            collective_id=0 if extra is None else 2, has_side_effects=True),
        name="group_sum",
    )(*args)
    return result[0] if extra is None else result


def gather_body(x, cot, vec, x_out, cot_out, vec_out, send, recv):
    half, width = x.shape
    row, col = greet()
    my_rows = pl.ds(pl.multiple_of((1 - row) * half, half), half)
    my_cols = pl.ds(pl.multiple_of((1 - col) * width, width), width)
    their_cols = pl.ds(pl.multiple_of(col * width, width), width)
    every = pl.ds(0, vec.shape[0])
    jobs = [(x, x_out, my_rows), (vec, vec_out, every), (cot, cot_out, my_rows)]
    copies = []
    first = []
    for k, (own, out, rows) in enumerate(jobs):
        copy = pltpu.make_async_remote_copy(
            own, out.at[rows, my_cols], send.at[0, k], recv.at[0, k],
            device_id={"col": col}, device_id_type=MESH_ID)
        copy.start()
        first.append(copy)
    for k, (own, out, rows) in enumerate(jobs):
        if rows is my_rows:
            copy = pltpu.make_async_remote_copy(
                own, out.at[rows, my_cols], send.at[1, k], recv.at[1, k],
                device_id={"row": row}, device_id_type=MESH_ID)
            copy.start()
            copies.append(copy)
    for own, out, rows in jobs:
        out[rows, my_cols] = own[...]
    for k, (own, out, rows) in enumerate(jobs):
        first[k].wait_recv()
        if rows is my_rows:
            copy = pltpu.make_async_remote_copy(
                out.at[rows, their_cols], out.at[rows, their_cols], send.at[2, k], recv.at[2, k],
                device_id={"row": row}, device_id_type=MESH_ID)
            copy.start()
            copies.append(copy)
    for copy in copies:
        copy.wait_recv()
    for copy in first + copies:
        copy.wait_send()


def group_gather(x, cot, vec):
    half, width = x.shape
    rows, wide = half * lax.axis_size("row"), width * lax.axis_size("col")
    vmem = pl.BlockSpec(memory_space=pltpu.VMEM)
    return pl.pallas_call(
        gather_body,
        out_shape=[
            jax.ShapeDtypeStruct((rows, wide), x.dtype),
            jax.ShapeDtypeStruct((rows, wide), cot.dtype),
            jax.ShapeDtypeStruct((vec.shape[0], wide), vec.dtype),
        ],
        in_specs=[vmem] * 3,
        out_specs=[vmem] * 3,
        scratch_shapes=[pltpu.SemaphoreType.DMA((3, 3)), pltpu.SemaphoreType.DMA((3, 3))],
        compiler_params=pltpu.CompilerParams(collective_id=1, has_side_effects=True),
        name="group_gather",
    )(x, cot, vec)


def make_scores(query, key, allowed):
    scores = jnp.einsum("hqd,hkd->hqk", query, key, preferred_element_type=F32) * SCALE
    return jnp.where(allowed[None], scores, NEG)


def swap_col(value):
    return lax.ppermute(value, "col", [(0, 1), (1, 0)])


def columns_whole(own, gate):
    col = lax.axis_index("col")
    depth, width = own.shape[1], own.shape[2] // 2
    later = (gate.reshape(-1)[0].astype(F32) * 0.0).astype(jnp.int32)
    got = swap_col(lax.dynamic_slice_in_dim(own, (1 - col) * width + later, width, 2))
    kept = lax.dynamic_slice_in_dim(own, col * width, width, 2)
    low = jnp.where(col == 0, kept, got)
    high = jnp.where(col == 0, got, kept)
    return jnp.concatenate([low, high], axis=1)


def rows_whole(grad):
    col = lax.axis_index("col")
    depth = grad.shape[0] // 2
    got = swap_col(lax.dynamic_slice_in_dim(grad, (1 - col) * depth, depth, 0))
    kept = lax.dynamic_slice_in_dim(grad, col * depth, depth, 0)
    low = jnp.where(col == 0, kept, got)
    high = jnp.where(col == 0, got, kept)
    return jnp.concatenate([low, high], axis=1)


def forward_layer(state, allowed, cosine, sine, params):
    gain1, bias1, gain2, bias2, w_qkv, b_qkv, w_up, b_up, w_out, w_down, b_both = params
    width = state.shape[1]
    mean = jnp.sum(state, axis=1, keepdims=True) / width
    squares = jnp.sum(state * state, axis=1, keepdims=True) / width
    inverse = lax.rsqrt(squares - mean * mean + EPS)
    normed = (state - mean) * inverse
    first = (normed * gain1 + bias1).astype(BF)
    second = (normed * gain2 + bias2).astype(BF)
    rows = state.shape[0]
    qkv = (jnp.dot(first, w_qkv, preferred_element_type=F32) + b_qkv).reshape(rows, -1, 3, HD)
    query = rotate(qkv[:, :, 0], cosine, sine).astype(BF).transpose(1, 0, 2)
    key = rotate(qkv[:, :, 1], cosine, sine).astype(BF).transpose(1, 0, 2)
    value = qkv[:, :, 2].astype(BF).transpose(1, 0, 2)
    scores = make_scores(query, key, allowed)
    top = jnp.max(scores, axis=-1, keepdims=True)
    lse = top + jnp.log(jnp.sum(jnp.exp(scores - top), axis=-1, keepdims=True))
    probs = jnp.exp(scores - lse).astype(BF)
    mixed = jnp.einsum("hqk,hkd->qhd", probs, value, preferred_element_type=F32)
    mixed = mixed.astype(BF).reshape(rows, -1)
    up = jnp.dot(second, w_up, preferred_element_type=F32) + b_up
    act = gelu_exact(up).astype(BF)
    part = jnp.dot(mixed, w_out, preferred_element_type=F32) + jnp.dot(
        act, w_down, preferred_element_type=F32)
    return part, (normed, inverse, first, second, query, key, value, mixed, lse, up, act)


def backward_layer(grad, allowed, cosine, sine, params, cache):
    gain1, bias1, gain2, bias2, w_qkv, b_qkv, w_up, b_up, w_out, w_down, b_both = params
    normed, inverse, first, second, query, key, value, mixed, lse, up, act = cache
    rows, width = grad.shape
    grad_b = grad.astype(BF)
    g_bout = jnp.sum(grad, axis=0)
    grad_mixed = jnp.einsum("td,kd->tk", grad_b, w_out, preferred_element_type=F32).astype(BF)
    grad_act = jnp.einsum("td,kd->tk", grad_b, w_down, preferred_element_type=F32)
    grad_up = grad_act * gelu_slope(up)
    g_bup = jnp.sum(grad_up, axis=0)
    grad_up_b = grad_up.astype(BF)
    scores = make_scores(query, key, allowed)
    probs = jnp.exp(scores - lse)
    grad_heads = grad_mixed.reshape(rows, -1, HD).transpose(1, 0, 2)
    mixed_heads = mixed.reshape(rows, -1, HD).transpose(1, 0, 2)
    delta = jnp.sum(grad_heads.astype(F32) * mixed_heads.astype(F32), axis=-1, keepdims=True)
    grad_value = jnp.einsum("hqk,hqd->khd", probs.astype(BF), grad_heads, preferred_element_type=F32)
    grad_probs = jnp.einsum("hqd,hkd->hqk", grad_heads, value, preferred_element_type=F32)
    grad_scores = (probs * (grad_probs - delta) * SCALE).astype(BF)
    grad_query = jnp.einsum("hqk,hkd->qhd", grad_scores, key, preferred_element_type=F32)
    grad_key = jnp.einsum("hqk,hqd->khd", grad_scores, query, preferred_element_type=F32)
    grad_query = unrotate(grad_query, cosine, sine)
    grad_key = unrotate(grad_key, cosine, sine)
    grad_qkv = jnp.stack([grad_query, grad_key, grad_value], axis=2).reshape(rows, -1)
    g_bqkv = jnp.sum(grad_qkv, axis=0)
    grad_qkv_b = grad_qkv.astype(BF)
    part_first = jnp.einsum("tn,dn->td", grad_qkv_b, w_qkv, preferred_element_type=F32)
    part_second = jnp.einsum("tn,dn->td", grad_up_b, w_up, preferred_element_type=F32)
    part = part_first * gain1 + part_second * gain2
    g_wout = jnp.einsum("tk,td->kd", mixed, grad_b, preferred_element_type=F32)
    g_wdown = jnp.einsum("tk,td->kd", act, grad_b, preferred_element_type=F32)
    g_wqkv = jnp.einsum("td,tn->dn", first, grad_qkv_b, preferred_element_type=F32)
    g_wup = jnp.einsum("td,tn->dn", second, grad_up_b, preferred_element_type=F32)
    shares = lax.axis_size("row") * lax.axis_size("col")
    narrow = jnp.concatenate([
        jnp.stack([
            jnp.sum(part_first * normed, axis=0), jnp.sum(part_first, axis=0),
            jnp.sum(part_second * normed, axis=0), jnp.sum(part_second, axis=0),
            g_bout / shares,
        ]),
        jnp.zeros((3, width), F32),
    ])
    grad_norm, narrow = group_sum(part, narrow)
    centred = (
        grad_norm
        - jnp.sum(grad_norm, axis=1, keepdims=True) / width
        - normed * (jnp.sum(grad_norm * normed, axis=1, keepdims=True) / width)
    )
    grad_x = grad + inverse * centred
    heavy = (g_wqkv.astype(BF), g_wup.astype(BF), g_wout.astype(BF), g_wdown.astype(BF))
    return grad_x, heavy, (g_bqkv, g_bup), narrow


def per_device_plain(
    x_in, cotangent, segment_ids, norm1_gain, norm1_bias, norm2_gain, norm2_bias,
    w_qkv, b_qkv, w_up, b_up, w_out, b_out, w_down, b_down,
):
    half, part_width = x_in.shape
    row = lax.axis_index("row")
    col = lax.axis_index("col")
    length = segment_ids.shape[1]
    layers = w_qkv.shape[0]
    cosine, sine = rope_tables(length)
    places = jnp.arange(length, dtype=jnp.int32)
    labels = segment_ids[0]
    allowed = (places[:, None] >= places[None, :]) & (labels[:, None] == labels[None, :])
    vec = jnp.stack([norm1_gain, norm1_bias, norm2_gain, norm2_bias, b_out + b_down])
    vec = vec.reshape(-1, part_width)
    pad = -vec.shape[0] % 8
    state_in, cot, vec = group_gather(x_in, cotangent.astype(BF), jnp.pad(vec, ((0, pad), (0, 0))))
    grad_in = cot.astype(F32)
    vectors = vec[: vec.shape[0] - pad].reshape(5, layers, -1)
    wide_qkv, wide_up, gate = [], [], vec
    for l in range(layers):
        wide_qkv.append(columns_whole(w_qkv[l : l + 1], gate)[0])
        wide_up.append(columns_whole(w_up[l : l + 1], gate)[0])
        gate = wide_qkv[-1]

    def own(whole):
        return lax.dynamic_slice(whole, (row * half, col * part_width), (half, part_width))

    params = [
        (vectors[0, l], vectors[1, l], vectors[2, l], vectors[3, l], wide_qkv[l], b_qkv[l],
         wide_up[l], b_up[l], w_out[l], w_down[l], vectors[4, l])
        for l in range(layers)
    ]
    state = state_in
    caches = []
    for layer in range(layers):
        part, cache = forward_layer(state, allowed, cosine, sine, params[layer])
        caches.append(cache)
        if layer < layers - 1:
            state = state + group_sum(part) + params[layer][-1]
    y_base = x_in + own(state - state_in + params[-1][-1])
    grad = grad_in
    heavy = [None] * layers
    thin = [None] * layers
    narrow = [None] * layers
    for layer in reversed(range(layers)):
        grad, heavy[layer], thin[layer], narrow[layer] = backward_layer(
            grad, allowed, cosine, sine, params[layer], caches[layer])
    x_grad = cotangent + own(grad - grad_in)
    y_out = y_base + own(group_sum(part))
    summed = []
    for layer in range(layers):
        a, b, c, d = heavy[layer]
        summed.append(lax.psum((rows_whole(a), rows_whole(b), c, d), "dp"))
    g_bqkv, g_bup, narrow = lax.psum((
        jnp.stack([t[0] for t in thin]), jnp.stack([t[1] for t in thin]),
        jnp.stack([t[:5] for t in narrow])), "dp")
    g_wqkv, g_wup, g_wout, g_wdown = (
        jnp.stack([h[k] for h in summed]).astype(F32) for k in range(4))
    narrow = lax.dynamic_slice_in_dim(narrow, col * part_width, part_width, 2)
    g_bout = narrow[:, 4]
    return (
        y_out, x_grad, narrow[:, 0], narrow[:, 1], narrow[:, 2], narrow[:, 3],
        g_wqkv, g_bqkv, g_wup, g_bup, g_wout, g_bout, g_wdown, g_bout,
    )


BLK = 128
TICKS = (3, 3, 4, 8, 8, 5, 5, 5, 5, 5)


def tdot(a, b):
    return lax.dot_general(a, b, (((0,), (0,)), ((), ())), preferred_element_type=F32)


def ntdot(a, b):
    return lax.dot_general(a, b, (((1,), (1,)), ((), ())), preferred_element_type=F32)


def ndot(a, b):
    return jnp.dot(a, b, preferred_element_type=F32)


def whole_body(
    n, x, cot, seg, n1g, n1b, n2g, n2b, bq, bu, bo, bd, cosr, sinr, wq_in, wu_in, wo_in, wd_in,
    y, xg, od, ow, ou, oq, osm,
    wq, wu, wo, wd, xb, cb, vec, mask, st, nrm, inv, fst, snd, act, slope, qkv_t, qh, p_t, m_t,
    gm_t, gub, gqb_t, gq, gb, own, sb, got_row, mine, got_col, back, back_got,
    ind, inw, iu, iq, ism, rd, rw, ru, rq, rsm, swu, swq,
    nar, nar_got, thin, send, recv, local,
):
    layers = wq.shape[0]
    gq_t = qkv_t
    half, cols = x.shape
    length, width = half * 2, cols * 2
    hid = wu.shape[2]
    heads = p_t.shape[1]
    qw = heads * 3 * HD
    row, col, here = lax.axis_index("row"), lax.axis_index("col"), lax.axis_index("dp")
    orow, ocol = 1 - row, 1 - col
    odd = lax.rem(here, 2)
    pos = here // 2 + odd * (n - 1 - 2 * (here // 2))

    def device(place):
        late = place // (n // 2)
        return 2 * (place + late * (n - 1 - 2 * place)) + late

    targets = (device(lax.rem(pos + 1, n)), device(lax.rem(pos + n - 1, n)))
    beside = here + 1 - 2 * odd
    high = lax.rem(here // 2, 2)
    along = here + 2 - 4 * high
    barrier = pltpu.get_barrier_semaphore()
    pl.semaphore_signal(barrier, inc=1, device_id={"dp": beside}, device_id_type=MESH_ID)
    pl.semaphore_signal(barrier, inc=1, device_id={"dp": along}, device_id_type=MESH_ID)
    pl.semaphore_signal(barrier, inc=1, device_id={"dp": targets[0]}, device_id_type=MESH_ID)
    pl.semaphore_signal(barrier, inc=1, device_id={"dp": targets[1]}, device_id_type=MESH_ID)
    pl.semaphore_signal(barrier, inc=1, device_id={"col": ocol}, device_id_type=MESH_ID)
    pl.semaphore_signal(barrier, inc=1, device_id={"row": orow}, device_id_type=MESH_ID)

    count = [0]
    sent = []

    def rc(src, dst, axis, target):
        k = count[0]
        count[0] += 1
        copy = pltpu.make_async_remote_copy(
            src, dst, send.at[k], recv.at[k], device_id={axis: target}, device_id_type=MESH_ID)
        copy.start()
        sent.append(copy)
        return copy

    def over_row(src, dst):
        return rc(src, dst, "row", orow)

    def over_col(src, dst):
        return rc(src, dst, "col", ocol)

    def at(base, size, step=None):
        return pl.ds(pl.multiple_of(base, step or size), size)

    my_rows, their_rows = at(row * half, half), at(orow * half, half)
    my_cols, their_cols = at(col * cols, cols), at(ocol * cols, cols)
    shift = wq_in.shape[2] - wq.shape[2]
    my_heads, their_heads = at(col * shift, wq.shape[2], BLK), at(ocol * shift, wq.shape[2], BLK)
    my_hid, their_hid = at(col * hid, hid), at(ocol * hid, hid)

    loads = []
    for l in range(layers):
        loads.append([
            pltpu.make_async_copy(wq_in.at[l, :, my_heads], wq.at[l, my_cols], local.at[l, 0]),
            pltpu.make_async_copy(wu_in.at[l, :, my_hid], wu.at[l, my_cols], local.at[l, 1]),
            pltpu.make_async_copy(wo_in.at[l], wo.at[l], local.at[l, 2]),
            pltpu.make_async_copy(wd_in.at[l], wd.at[l], local.at[l, 3]),
        ])
        for copy in loads[-1]:
            copy.start()

    xb[my_rows, my_cols] = x[...].astype(BF)
    cb[my_rows, my_cols] = cot[...].astype(BF)
    for k, ref in enumerate((n1g, n1b, n2g, n2b)):
        vec[2 * k : 2 * k + 2, my_cols] = ref[...]
    vec[8:10, my_cols] = bo[...] + bd[...]
    pl.semaphore_wait(barrier, 6)

    x_col = over_col(xb.at[my_rows, my_cols], xb.at[my_rows, my_cols])
    x_row = over_row(xb.at[my_rows, my_cols], xb.at[my_rows, my_cols])
    v_col = over_col(vec.at[:, my_cols], vec.at[:, my_cols])

    some = cols // 4
    few = some // 2
    mine_of, y_of, z_of = odd + 2 * high, 1 - odd + 2 * high, odd + 2 * (1 - high)

    def fetch(kind, l):
        src, lanes, dst = ((wq_in, their_heads, wq), (wu_in, their_hid, wu))[kind]
        return dst, l, over_col(
            src.at[l, at(mine_of * some, some), lanes], dst.at[l, at(col * cols + mine_of * some, some)])

    def spread(got):
        dst, l, copy = got
        copy.wait_recv()
        spot = dst.at[l, at(ocol * cols + mine_of * some, some)]
        return dst, l, rc(spot, spot, "dp", beside), rc(spot, spot, "dp", along)

    def relay(got):
        dst, l, by_y, by_z = got
        by_y.wait_recv()
        spot = dst.at[l, at(ocol * cols + y_of * some, few)]
        on_z = rc(spot, spot, "dp", along)
        by_z.wait_recv()
        spot = dst.at[l, at(ocol * cols + z_of * some + few, few, few)]
        return on_z, rc(spot, spot, "dp", beside)

    def arrived(got):
        for copy in got:
            copy.wait_recv()

    q_0, u_0 = fetch(0, 0), fetch(1, 0)
    c_row = over_row(cb.at[my_rows, my_cols], cb.at[my_rows, my_cols])

    label = seg[...].astype(F32)
    tall = jnp.broadcast_to(label, (BLK, length)).T
    for k in range(length // BLK):
        here_rows = slice(k * BLK, (k + 1) * BLK)
        key_at = lax.broadcasted_iota(jnp.int32, (BLK, length), 0) + k * BLK
        query_at = lax.broadcasted_iota(jnp.int32, (BLK, length), 1)
        same = tall[here_rows, 0:1] == label
        mask[here_rows, :] = jnp.where(same & (key_at <= query_at), 0.0, NEG)
    nar[...] = jnp.zeros_like(nar)
    offset = col * (wq.shape[2] - qw)

    x_col.wait_recv()
    x_over = over_row(xb.at[my_rows, their_cols], xb.at[my_rows, their_cols])
    v_col.wait_recv()
    x_row.wait_recv()
    x_over.wait_recv()

    def gain(k, l):
        return vec[2 * k + l : 2 * k + l + 1, :]

    blocks = length // BLK

    def norm_step(l):
        @pl.loop(0, blocks)
        def _(i):
            rows = at(i * BLK, BLK)
            s = xb[rows, :].astype(F32) if l == 0 else st[rows, :]
            mean = jnp.sum(s, axis=1, keepdims=True) / width
            squares = jnp.sum(s * s, axis=1, keepdims=True) / width
            inverse = lax.rsqrt(squares - mean * mean + EPS)
            normed = (s - mean) * inverse
            inv[l, rows, :] = inverse
            nrm[l, rows, :] = normed.astype(BF)
            fst[l, rows, :] = (normed * gain(0, l) + gain(1, l)).astype(BF)
            snd[l, rows, :] = (normed * gain(2, l) + gain(3, l)).astype(BF)

    def qkv_step(l):
        @pl.loop(0, blocks)
        def _(i):
            rows = at(i * BLK, BLK)
            got = ndot(fst[l, rows, :], wq[l]) + bq[l : l + 1, :]
            qkv_t[:, rows] = got.T

    def turn(v, sign):
        a, b = v[0:8], v[8:16]
        c, s = cosr[...], sinr[...] * sign
        return jnp.concatenate([a * c - b * s, b * c + a * s, v[16:]], axis=0)

    QB = length // 2

    def attention_step(l):
        @pl.loop(0, heads)
        def _(h):
            base = offset + h * (3 * HD)
            q = turn(qkv_t[at(base, HD), :], 1.0).astype(BF)
            k = turn(qkv_t[at(base + HD, HD), :], 1.0).astype(BF)
            v = qkv_t[at(base + 2 * HD, HD), :].astype(BF)
            spot = h * (3 * HD)
            qh[l, at(spot, HD), :] = q
            qh[l, at(spot + HD, HD), :] = k
            qh[l, at(spot + 2 * HD, HD), :] = v
            q = q * jnp.asarray(SCALE, BF)
            for b in range(2):
                keys, these = slice(0, (b + 1) * QB), slice(b * QB, (b + 1) * QB)
                scores = tdot(k[:, keys], q[:, these]) + mask[keys, these]
                top = jnp.max(scores, axis=0, keepdims=True)
                e = jnp.exp(scores - top)
                total = jnp.sum(e, axis=0, keepdims=True)
                probs = (e * (1.0 / total)).astype(BF)
                p_t[l, h, keys, these] = probs
                m_t[l, at(h * HD, HD), these] = ndot(v[:, keys], probs).astype(BF)

    def up_step(l):
        @pl.loop(0, blocks)
        def _(i):
            rows = at(i * BLK, BLK)
            up = ndot(snd[l, rows, :], wu[l]) + bu[l : l + 1, :]
            phi = 0.5 * (1.0 + lax.erf(up * INV_ROOT2))
            act[l, rows, :] = (up * phi).astype(BF)
            slope[l, rows, :] = (phi + up * jnp.exp(-0.5 * up * up) * INV_ROOT_TWO_PI).astype(BF)

    def part_rows(l):
        def run(base):
            rows = at(base, BLK)
            return tdot(m_t[l, :, rows], wo[l]) + ndot(act[l, rows, :], wd[l])
        return run

    pieces = half // BLK

    def sum_begin(k, fn):
        flight = []
        for p in range(pieces):
            here = slice(p * BLK, (p + 1) * BLK)
            sb[k, here, :] = fn(orow * half + p * BLK).astype(BF)
            flight.append(over_row(sb.at[k, here], got_row.at[k, here]))
        for p in range(pieces):
            here = slice(p * BLK, (p + 1) * BLK)
            own[k % 2, here, :] = fn(row * half + p * BLK)
        return flight

    def sum_cross(k, flight, narrow=False):
        crossing = []
        for p in range(pieces):
            here = slice(p * BLK, (p + 1) * BLK)
            flight[p].wait_recv()
            t = own[k % 2, here, :] + got_row[k, here, :].astype(F32)
            own[k % 2, here, :] = t
            mine[k, here, :] = t.astype(BF)
            if narrow:
                crossing.append(over_col(
                    mine.at[k, here, their_cols], got_col.at[k, here, their_cols]))
            else:
                crossing.append(over_col(mine.at[k, here], got_col.at[k, here]))
        return crossing


    norm_step(0)
    q_0 = spread(q_0)
    u_0 = spread(u_0)
    c_col = over_col(cb.at[my_rows, my_cols], cb.at[my_rows, my_cols])
    u_1, q_1 = fetch(1, 1), fetch(0, 1)
    q_0 = relay(q_0)
    u_0 = relay(u_0)
    loads[0][0].wait()
    arrived(q_0)
    qkv_step(0)
    attention_step(0)
    loads[0][1].wait()
    arrived(u_0)
    up_step(0)
    loads[0][2].wait()
    loads[0][3].wait()
    flight = sum_begin(0, part_rows(0))
    crossing = sum_cross(0, flight)
    u_1 = spread(u_1)
    q_1 = spread(q_1)
    c_col.wait_recv()
    c_over = over_row(cb.at[my_rows, their_cols], cb.at[my_rows, their_cols])
    both = vec[8:9, :]
    returned = []
    for p in range(pieces):
        here = slice(p * BLK, (p + 1) * BLK)
        crossing[p].wait_recv()
        total = own[0, here, :] + got_col[0, here, :].astype(F32)
        own[0, here, :] = total
        back[0, here, :] = total.astype(BF)
        returned.append(over_row(back.at[0, here], back_got.at[0, here]))
    for p in range(pieces):
        here = slice(p * BLK, (p + 1) * BLK)
        rows = at(row * half + p * BLK, BLK)
        st[rows, :] = xb[rows, :].astype(F32) + own[0, here, :] + both
    y[...] = x[...] + own[0, :, my_cols] + vec[8:9, my_cols] + vec[9:10, my_cols]
    u_1 = relay(u_1)
    q_1 = relay(q_1)
    for p in range(pieces):
        here = slice(p * BLK, (p + 1) * BLK)
        returned[p].wait_recv()
        rows = at(orow * half + p * BLK, BLK)
        st[rows, :] = xb[rows, :].astype(F32) + back_got[0, here, :].astype(F32) + both

    def chunk(d, behind):
        sign = 1 if d == 0 else -1
        return lax.rem(pos - sign * behind + 2 * n, n)

    def stream(d, parts, swap=None, lane=0, reach=0):
        def go(pairs):
            return [rc(src, dst, "dp", targets[d]) for src, dst in pairs]
        copies = go([(rin(chunk(d, 0)), got(0)) for rin, got, out in parts])
        for s in range(n - 1):
            yield
            for k, (rin, got, out) in enumerate(parts):
                copies[k].wait_recv()
                got(s)[...] = got(s)[...] + rin(chunk(d, s + 1))[...]
                if s < n - 2:
                    copies[k] = go([(got(s), got(s + 1))])[0]
        where = chunk(d, n - 1)
        if swap is None:
            for rin, got, out in parts:
                out(where)[...] = got(n - 2)[...]
        else:
            last, out = parts[0][1](n - 2), parts[0][2]
            over = over_col(last.at[ocol], swap)
            yield
            over.wait_recv()
            wide = last.shape[2]
            if reach:
                out(where, at(col * reach + lane, wide, BLK))[...] = last[col]
                out(where, at(ocol * reach + lane, wide, BLK))[...] = swap[...]
            else:
                a, b = last[col].astype(F32), swap[...].astype(F32)
                first = col == 0
                out(where)[...] = jnp.concatenate(
                    [jnp.where(first, a, b), jnp.where(first, b, a)], axis=1).astype(BF)
        if reach:
            spots = [lambda c, k=k: parts[0][2](c, slice(k * reach + lane, k * reach + lane + wide))
                     for k in range(2)]
        else:
            spots = [part[2] for part in parts]
        copies = go([(spot(where), spot(where)) for spot in spots])
        for s in range(n - 1):
            yield
            for k, spot in enumerate(spots):
                copies[k].wait_recv()
                if s < n - 2:
                    where = chunk(d, s)
                    copies[k] = go([(spot(where), spot(where))])[0]

    active = []

    def launch(*args, **kw):
        g = stream(*args, **kw)
        next(g)
        active.append(g)

    def pump(times):
        for _ in range(times):
            if active:
                g = active.pop(0)
                try:
                    next(g)
                    active.append(g)
                except StopIteration:
                    pass

    deep = hid // n

    def tick(k):
        pump(TICKS[k])

    def down_step(l, g):
        for k in range(2):
            f = slice(k * (hid // 2), (k + 1) * (hid // 2))
            got = tdot(act[l, :, f], g[...]).astype(BF)
            ind[l, k * (n // 2) : (k + 1) * (n // 2)] = got.reshape(n // 2, deep, width)
        cut = deep - 16 * (l + 1)
        launch(0, [(lambda c: ind.at[l, c, 0:cut], lambda s: rd.at[l, s, 0:cut],
                    lambda c: od.at[l, at(c * deep, cut, 16)])])
        launch(1, [(lambda c: ind.at[l, c, cut:deep], lambda s: rd.at[l, s, cut:deep],
                    lambda c: od.at[l, at(c * deep + cut, deep - cut, 16)])])

    def out_step():
        both = [ndot(m_t[l], g[...]).reshape(n, -1, width) for l, g in enumerate((gb, cb))]
        inw[...] = jnp.concatenate(both, axis=1).astype(BF)
        launch(0, [(lambda c: inw.at[c], lambda s: rw.at[s], lambda c: ow.at[c])])

    def up_grad_step(l):
        for k in range(2):
            f = slice(k * cols, (k + 1) * cols)
            got = tdot(snd[l, :, f], gub[...]).astype(BF)
            iu[l, :, k] = got.reshape(n, -1, hid)
        part, tall = hid // 2, iu.shape[3]
        for d in range(2):
            lanes = slice(d * part, (d + 1) * part)
            launch(d, [(lambda c, lanes=lanes: iu.at[l, c, :, :, lanes],
                        lambda s, lanes=lanes: ru.at[l, s, :, :, lanes],
                        lambda c, lanes: ou.at[l, at(c * tall, tall), lanes])],
                   swap=swu.at[l, :, lanes], lane=d * part, reach=hid)

    def qkv_grad_step(l):
        for k in range(2):
            f = slice(k * cols, (k + 1) * cols)
            got = ntdot(fst[l, :, f].T, gqb_t[...]).astype(BF)
            iq[l, :, k] = got.reshape(n, -1, qw)
        launch(1, [(lambda c: iq.at[l, c], lambda s: rq.at[l, s],
                    lambda c: oq.at[l, at(c * iq.shape[3], iq.shape[3])])], swap=swq.at[l])

    def grad_up_step(l, g):
        def block(i, total):
            rows = at(i * BLK, BLK)
            gu = ntdot(g[rows, :], wd[l]) * slope[l, rows, :].astype(F32)
            gub[rows, :] = gu.astype(BF)
            return total + jnp.sum(gu, axis=0, keepdims=True)
        total = lax.fori_loop(0, blocks, block, jnp.zeros((1, hid), F32))
        thin[l, 1:2, 0:hid] = total

    def attention_back_step(l, g):
        gm_t[...] = ntdot(wo[l], g[...]).astype(BF)

        @pl.loop(0, heads)
        def _(h):
            spot = h * (3 * HD)
            q = qh[l, at(spot, HD), :]
            k = qh[l, at(spot + HD, HD), :]
            v = qh[l, at(spot + 2 * HD, HD), :]
            gm = gm_t[at(h * HD, HD), :]
            mixed = m_t[l, at(h * HD, HD), :]
            delta = jnp.sum(gm.astype(F32) * mixed.astype(F32), axis=0, keepdims=True)
            gqs, gks, gvs = [], [], []
            for b in range(2):
                keys, these = slice(0, (b + 1) * QB), slice(b * QB, (b + 1) * QB)
                probs = p_t[l, h, keys, these]
                gp = tdot(v[:, keys], gm[:, these])
                ds = (probs.astype(F32) * (gp - delta[:, these])).astype(BF)
                gqs.append(ndot(k[:, keys], ds))
                gks.append(ntdot(q[:, these], ds))
                gvs.append(ntdot(gm[:, these], probs))
            gq_h = jnp.concatenate(gqs, axis=1) * SCALE
            gk_h = jnp.concatenate([gks[0] + gks[1][:, :QB], gks[1][:, QB:]], axis=1) * SCALE
            gv_h = jnp.concatenate([gvs[0] + gvs[1][:, :QB], gvs[1][:, QB:]], axis=1)
            base = offset + spot
            for k3, value in enumerate((turn(gq_h, -1.0), turn(gk_h, -1.0), gv_h)):
                gq_t[at(base + k3 * HD, HD), :] = value
                gqb_t[at(spot + k3 * HD, HD), :] = value.astype(BF)

        total = jnp.zeros((1, gq_t.shape[0]), F32)
        for i in range(blocks):
            flat = gq_t[:, i * BLK : (i + 1) * BLK].T
            gq[i * BLK : (i + 1) * BLK, :] = flat.astype(BF)
            total = total + jnp.sum(flat, axis=0, keepdims=True)
        thin[l, 0:1, :] = jnp.concatenate([total, jnp.zeros((1, width - total.shape[1]), F32)], axis=1)

    def back_rows(l):
        def run(base):
            rows = at(base, BLK)
            gf = ntdot(gq[rows, :], wq[l])
            gs = ntdot(gub[rows, :], wu[l])
            normed = nrm[l, rows, :].astype(F32)
            for k, value in enumerate((gf * normed, gf, gs * normed, gs)):
                nar[l, 0, k : k + 1, :] += jnp.sum(value, axis=0, keepdims=True)
            return gf * gain(0, l) + gs * gain(2, l)
        return run

    def centred(l, rows, total):
        normed = nrm[l, rows, :].astype(F32)
        return inv[l, rows, :] * (
            total - jnp.sum(total, axis=1, keepdims=True) / width
            - normed * (jnp.sum(total * normed, axis=1, keepdims=True) / width))

    shares = 0.25
    norm_step(1)
    loads[1][1].wait()
    arrived(u_1)
    up_step(1)
    c_row.wait_recv()
    c_over.wait_recv()
    loads[1][2].wait()
    loads[1][3].wait()
    down_step(1, cb)
    grad_up_step(1, cb)
    up_grad_step(1)
    loads[1][0].wait()
    arrived(q_1)
    qkv_step(1)
    tick(0)
    attention_step(1)
    tick(1)
    nar[1, 0, 4:5, :] = jnp.sum(cb[...].astype(F32), axis=0, keepdims=True) * shares
    gq_t[...] = jnp.zeros_like(gq_t)
    attention_back_step(1, cb)
    tick(2)
    flight = sum_begin(1, back_rows(1))
    nar_row = over_row(nar.at[1, 0], nar_got.at[1, 0])
    qkv_grad_step(1)
    crossing = sum_cross(1, flight)
    tick(3)
    returned = []
    for p in range(pieces):
        here = slice(p * BLK, (p + 1) * BLK)
        crossing[p].wait_recv()
        total = own[1, here, :] + got_col[1, here, :].astype(F32)
        own[1, here, :] = total
        back[1, here, :] = total.astype(BF)
        returned.append(over_row(back.at[1, here], back_got.at[1, here]))
    bout = jnp.zeros((1, width), F32)
    for p in range(pieces):
        here = slice(p * BLK, (p + 1) * BLK)
        rows = at(row * half + p * BLK, BLK)
        change = centred(1, rows, own[1, here, :])
        own[1, here, :] = change
        grad = cb[rows, :].astype(F32) + change
        gb[rows, :] = grad.astype(BF)
        bout = bout + jnp.sum(grad, axis=0, keepdims=True)
    xg[...] = cot[...] + own[1, :, my_cols]
    for p in range(pieces):
        here = slice(p * BLK, (p + 1) * BLK)
        returned[p].wait_recv()
        rows = at(orow * half + p * BLK, BLK)
        grad = cb[rows, :].astype(F32) + centred(1, rows, back_got[1, here, :].astype(F32))
        gb[rows, :] = grad.astype(BF)
        bout = bout + jnp.sum(grad, axis=0, keepdims=True)
    nar[0, 0, 4:5, :] = bout * shares
    nar_row.wait_recv()
    nar[1, 1] = nar[1, 0] + nar_got[1, 0]
    nar_col = over_col(nar.at[1, 1], nar_got.at[1, 1])
    tick(4)
    down_step(0, gb)
    tick(5)
    out_step()
    grad_up_step(0, gb)
    up_grad_step(0)
    tick(6)
    attention_back_step(0, gb)
    tick(7)
    flight_x = sum_begin(3, back_rows(0))
    nar_row0 = over_row(nar.at[0, 0], nar_got.at[0, 0])
    qkv_grad_step(0)
    tick(8)
    crossing_x = sum_cross(3, flight_x)
    nar_row0.wait_recv()
    nar[0, 1] = nar[0, 0] + nar_got[0, 0]
    nar_col0 = over_col(nar.at[0, 1], nar_got.at[0, 1])
    tick(9)
    nar_col.wait_recv()
    nar_col0.wait_recv()
    ism[...] = jnp.zeros_like(ism)
    few_rows = jnp.concatenate(
        [v for l in range(layers) for v in (
            nar[l, 1, 0:5, :] + nar_got[l, 1, 0:5, :], thin[l, 0:2, :], jnp.zeros((1, width), F32))],
        axis=0).astype(BF)
    for k in range(width // BLK):
        ism[k] = few_rows[:, k * BLK : (k + 1) * BLK]
    launch(0, [(lambda c: ism.at[c], lambda s: rsm.at[s], lambda c: osm.at[c])])
    pump(2)
    flight_y = sum_begin(2, part_rows(1))
    crossing_y = sum_cross(2, flight_y, narrow=True)
    pump(2)
    for p in range(pieces):
        here = slice(p * BLK, (p + 1) * BLK)
        crossing_x[p].wait_recv()
        rows = at(row * half + p * BLK, BLK)
        own[1, here, :] = centred(0, rows, own[1, here, :] + got_col[3, here, :].astype(F32))
    xg[...] += own[1, :, my_cols]
    pump(2)
    for p in range(pieces):
        crossing_y[p].wait_recv()
    y[...] += own[0, :, my_cols] + got_col[2, :, my_cols].astype(F32)
    while active:
        pump(1)
    for copy in sent:
        copy.wait_send()


def whole_step(x, cot, seg, n1g, n1b, n2g, n2b, wq_in, bq, wu_in, bu, wo_in, bo, wd_in, bd):
    n = lax.axis_size("dp")
    half, cols = x.shape
    layers, _, both_heads = wq_in.shape
    length, width = 2 * half, 2 * cols
    hid = wu_in.shape[2] // 2
    qw = both_heads // 2
    heads = qw // (3 * HD)
    wide = -(-qw // BLK) * BLK
    mix = wo_in.shape[1]
    col = lax.axis_index("col")
    freq = np.float32(10000.0) ** (-(np.arange(ROT // 2, dtype=np.float32) * 2) / np.float32(ROT))
    angle = freq[:, None] * np.arange(length, dtype=np.float32)[None, :]
    cosr, sinr = jnp.asarray(np.cos(angle), F32), jnp.asarray(np.sin(angle), F32)
    bq = lax.dynamic_update_slice(jnp.zeros((layers, wide), F32), bq, (0, col * (wide - qw)))
    per, deep, flat = width // 2 // n, hid // n, mix // n
    tall = layers * flat
    small = 8 * layers
    vmem = pl.BlockSpec(memory_space=pltpu.VMEM)
    anyw = pl.BlockSpec(memory_space=pl.ANY)
    V = pltpu.VMEM
    sums = 4
    sems = 384
    out = pl.pallas_call(
        lambda *refs: whole_body(n, *refs),
        out_shape=[
            jax.ShapeDtypeStruct((half, cols), F32), jax.ShapeDtypeStruct((half, cols), F32),
            jax.ShapeDtypeStruct((layers, hid, width), BF),
            jax.ShapeDtypeStruct((n, tall, width), BF),
            jax.ShapeDtypeStruct((layers, width // 2, 2 * hid), BF),
            jax.ShapeDtypeStruct((layers, width // 2, 2 * qw), BF),
            jax.ShapeDtypeStruct((n, small, BLK), BF),
        ],
        in_specs=[vmem] * 13 + [anyw] * 4,
        out_specs=[vmem] * 7,
        scratch_shapes=[
            V((layers, width, wide), BF), V((layers, width, hid), BF),
            V((layers, mix, width), BF), V((layers, hid, width), BF),
            V((length, width), BF), V((length, width), BF), V((16, width), F32),
            V((length, length), F32), V((length, width), F32),
            V((layers, length, width), BF), V((layers, length, 1), F32),
            V((layers, length, width), BF), V((layers, length, width), BF),
            V((layers, length, hid), BF), V((layers, length, hid), BF),
            V((wide, length), F32), V((layers, qw, length), BF),
            V((layers, heads, length, length), BF), V((layers, mix, length), BF),
            V((mix, length), BF), V((length, hid), BF),
            V((qw, length), BF), V((length, wide), BF), V((length, width), BF),
            V((2, half, width), F32), V((sums, half, width), BF), V((sums, half, width), BF),
            V((sums, half, width), BF), V((sums, half, width), BF),
            V((2, half, width), BF), V((2, half, width), BF),
            V((layers, n, deep, width), BF), V((n, tall, width), BF),
            V((layers, n, 2, per, hid), BF), V((layers, n, 2, per, qw), BF),
            V((n, small, BLK), BF),
            V((layers, n - 1, deep, width), BF), V((n - 1, tall, width), BF),
            V((layers, n - 1, 2, per, hid), BF), V((layers, n - 1, 2, per, qw), BF),
            V((n - 1, small, BLK), BF),
            V((layers, per, hid), BF), V((layers, per, qw), BF),
            V((layers, 2, 8, width), F32), V((layers, 2, 8, width), F32),
            V((layers, 2, width), F32),
            pltpu.SemaphoreType.DMA((sems,)), pltpu.SemaphoreType.DMA((sems,)),
            pltpu.SemaphoreType.DMA((layers, 4)),
        ],
        compiler_params=pltpu.CompilerParams(
            collective_id=5, has_side_effects=True, vmem_limit_bytes=62 * 1024 * 1024),
        name="whole_step",
    )(x, cot, seg, n1g, n1b, n2g, n2b, bq, bu, bo, bd, cosr, sinr, wq_in, wu_in, wo_in, wd_in)
    y, xg, d, w, u, q, s = out
    g_wqkv, g_wup, g_wdown = q.astype(F32), u.astype(F32), d.astype(F32)
    g_wout = w.reshape(n, layers, flat, width).transpose(1, 0, 2, 3).reshape(layers, mix, width).astype(F32)
    s = s[: width // BLK].transpose(1, 0, 2).astype(F32).reshape(layers, 8, width)
    narrow = lax.dynamic_slice_in_dim(s[:, :5], col * cols, cols, 2)
    g_bqkv = lax.dynamic_slice_in_dim(s[:, 5], col * (wide - qw), qw, 1)
    g_bup = s[:, 6, :hid]
    g_bout = narrow[:, 4]
    return (
        y, xg, narrow[:, 0], narrow[:, 1], narrow[:, 2], narrow[:, 3],
        g_wqkv, g_bqkv, g_wup, g_bup, g_wout, g_bout, g_wdown, g_bout)


def per_device(*args):
    x, wq, wo, wd = args[0], args[7], args[11], args[13]
    n = lax.axis_size("dp")
    parts = lax.axis_size("row"), lax.axis_size("col")
    cols = x.shape[1]
    fits = (
        parts == (2, 2) and n % 2 == 0 and n >= 4 and cols % n == 0 and (cols // n) % 16 == 0
        and (wd.shape[1] // n) % 32 == 0 and (wo.shape[1] // n) % 8 == 0 and n * BLK >= 2 * cols and wq.shape[0] == 2)
    return whole_step(*args) if fits else per_device_plain(*args)


def solution(mesh):
    in_specs = (
        P(("dp", "row"), "col"),
        P(("dp", "row"), "col"),
        P("dp", None),
        P(None, "col"),
        P(None, "col"),
        P(None, "col"),
        P(None, "col"),
        P(None, "col", "row"),
        P(None, ("row", "col")),
        P(None, "col", "row"),
        P(None, ("row", "col")),
        P(None, ("row", "col"), None),
        P(None, "col"),
        P(None, ("row", "col"), None),
        P(None, "col"),
    )
    out_specs = (
        P(("dp", "row"), "col"),
        P(("dp", "row"), "col"),
        P(None, "col"),
        P(None, "col"),
        P(None, "col"),
        P(None, "col"),
        P(None, "col", "row"),
        P(None, ("row", "col")),
        P(None, "col", "row"),
        P(None, ("row", "col")),
        P(None, ("row", "col"), None),
        P(None, "col"),
        P(None, ("row", "col"), None),
        P(None, "col"),
    )
    return jax.shard_map(
        per_device, mesh=mesh, in_specs=in_specs, out_specs=out_specs, check_vma=False
    )
```

```python
import jax
import jax.numpy as jnp
import numpy as np
from jax import lax
from jax.experimental import pallas as pl
from jax.experimental.pallas import tpu as pltpu
from jax.sharding import PartitionSpec as P

D = 768
HD = 64
ROT = 16
LAYERS = 2


EPS = 1e-05
NEG = -1e30
SCALE = 0.125
INV_ROOT2 = 0.7071067811865476
INV_ROOT_TWO_PI = 0.3989422804014327


def rope_tables(length):
    half = ROT // 2
    freq = 10000.0 ** (-(jnp.arange(half, dtype=jnp.float32) * 2.0) / ROT)
    angle = jnp.arange(length, dtype=jnp.float32)[:, None] * freq[None, :]
    cosine = jnp.concatenate([jnp.cos(angle), jnp.cos(angle)], axis=1)
    sine = jnp.concatenate([jnp.sin(angle), jnp.sin(angle)], axis=1)
    return (cosine, sine)


def rotate(values, cosine, sine):
    part = values[..., :ROT]
    lower = part[..., : ROT // 2]
    upper = part[..., ROT // 2 :]
    turned = jnp.concatenate([-upper, lower], axis=-1)
    moved = part * cosine[:, None, :] + turned * sine[:, None, :]
    return jnp.concatenate([moved, values[..., ROT:]], axis=-1)


def unrotate(grads, cosine, sine):
    part = grads[..., :ROT]
    lower = part[..., : ROT // 2]
    upper = part[..., ROT // 2 :]
    turned = jnp.concatenate([upper, -lower], axis=-1)
    moved = part * cosine[:, None, :] + turned * sine[:, None, :]
    return jnp.concatenate([moved, grads[..., ROT:]], axis=-1)


def gelu_exact(values):
    return 0.5 * values * (1.0 + jax.scipy.special.erf(values * INV_ROOT2))


def gelu_slope(values):
    return (
        0.5 * (1.0 + jax.scipy.special.erf(values * INV_ROOT2))
        + values * jnp.exp(-0.5 * values * values) * INV_ROOT_TWO_PI
    )


BF = jnp.bfloat16
F32 = jnp.float32
MESH_ID = pl.DeviceIdType.MESH
PIECES = 4


def greet():
    row = 1 - lax.axis_index("row")
    col = 1 - lax.axis_index("col")
    barrier = pltpu.get_barrier_semaphore()
    pl.semaphore_signal(barrier, inc=1, device_id={"row": row}, device_id_type=MESH_ID)
    pl.semaphore_signal(barrier, inc=1, device_id={"col": col}, device_id_type=MESH_ID)
    pl.semaphore_wait(barrier, 2)
    return row, col


def reduce_body(*refs):
    if len(refs) == 7:
        part, out, got_row, mine, got_col, send, recv = refs
        extra = None
    else:
        part, extra, out, extra_out, got_row, mine, got_col, pair, got_extra, send, recv = refs
    half = mine.shape[0]
    piece = half // PIECES
    row, col = greet()
    own = (1 - row) * half
    theirs = row * half
    first, second, third = [], [], []
    for k in range(PIECES):
        at = pl.multiple_of(theirs + k * piece, piece)
        copy = pltpu.make_async_remote_copy(
            part.at[pl.ds(at, piece)], got_row.at[pl.ds(k * piece, piece)],
            send.at[0, k], recv.at[0, k], device_id={"row": row}, device_id_type=MESH_ID)
        copy.start()
        first.append(copy)
    if extra is not None:
        over_row = pltpu.make_async_remote_copy(
            extra, got_extra.at[0], send.at[3, 0], recv.at[3, 0],
            device_id={"row": row}, device_id_type=MESH_ID)
        over_row.start()
    for k in range(PIECES):
        here = pl.ds(k * piece, piece)
        at = pl.multiple_of(own + k * piece, piece)
        first[k].wait_recv()
        mine[here, :] = (part[pl.ds(at, piece), :] + got_row[here, :]).astype(BF)
        copy = pltpu.make_async_remote_copy(
            mine.at[here], got_col.at[here], send.at[1, k], recv.at[1, k],
            device_id={"col": col}, device_id_type=MESH_ID)
        copy.start()
        second.append(copy)
    if extra is not None:
        over_row.wait_recv()
        pair[...] = extra[...] + got_extra[0]
        over_col = pltpu.make_async_remote_copy(
            pair, got_extra.at[1], send.at[3, 1], recv.at[3, 1],
            device_id={"col": col}, device_id_type=MESH_ID)
        over_col.start()
    for k in range(PIECES):
        here = pl.ds(k * piece, piece)
        at = pl.multiple_of(own + k * piece, piece)
        second[k].wait_recv()
        out[pl.ds(at, piece), :] = mine[here, :].astype(F32) + got_col[here, :].astype(F32)
        copy = pltpu.make_async_remote_copy(
            out.at[pl.ds(at, piece)], out.at[pl.ds(at, piece)], send.at[2, k], recv.at[2, k],
            device_id={"row": row}, device_id_type=MESH_ID)
        copy.start()
        third.append(copy)
    if extra is not None:
        over_col.wait_recv()
        extra_out[...] = pair[...] + got_extra[1]
        over_row.wait_send()
        over_col.wait_send()
    for k in range(PIECES):
        third[k].wait_recv()
        for copy in (first[k], second[k], third[k]):
            copy.wait_send()


def group_sum(part, extra=None):
    rows, width = part.shape
    half = rows // lax.axis_size("row")
    vmem = pl.BlockSpec(memory_space=pltpu.VMEM)
    out_shape = [jax.ShapeDtypeStruct((rows, width), F32)]
    scratch = [pltpu.VMEM((half, width), F32), pltpu.VMEM((half, width), BF),
               pltpu.VMEM((half, width), BF)]
    args = [part]
    if extra is not None:
        args.append(extra)
        out_shape.append(jax.ShapeDtypeStruct(extra.shape, F32))
        scratch += [pltpu.VMEM(extra.shape, F32), pltpu.VMEM((2,) + extra.shape, F32)]
    result = pl.pallas_call(
        reduce_body,
        out_shape=out_shape,
        in_specs=[vmem] * len(args),
        out_specs=[vmem] * len(out_shape),
        scratch_shapes=scratch + [
            pltpu.SemaphoreType.DMA((4, PIECES)), pltpu.SemaphoreType.DMA((4, PIECES))],
        compiler_params=pltpu.CompilerParams(
            collective_id=0 if extra is None else 2, has_side_effects=True),
        name="group_sum",
    )(*args)
    return result[0] if extra is None else result


def gather_body(x, cot, vec, x_out, cot_out, vec_out, send, recv):
    half, width = x.shape
    row, col = greet()
    my_rows = pl.ds(pl.multiple_of((1 - row) * half, half), half)
    my_cols = pl.ds(pl.multiple_of((1 - col) * width, width), width)
    their_cols = pl.ds(pl.multiple_of(col * width, width), width)
    every = pl.ds(0, vec.shape[0])
    jobs = [(x, x_out, my_rows), (vec, vec_out, every), (cot, cot_out, my_rows)]
    copies = []
    first = []
    for k, (own, out, rows) in enumerate(jobs):
        copy = pltpu.make_async_remote_copy(
            own, out.at[rows, my_cols], send.at[0, k], recv.at[0, k],
            device_id={"col": col}, device_id_type=MESH_ID)
        copy.start()
        first.append(copy)
    for k, (own, out, rows) in enumerate(jobs):
        if rows is my_rows:
            copy = pltpu.make_async_remote_copy(
                own, out.at[rows, my_cols], send.at[1, k], recv.at[1, k],
                device_id={"row": row}, device_id_type=MESH_ID)
            copy.start()
            copies.append(copy)
    for own, out, rows in jobs:
        out[rows, my_cols] = own[...]
    for k, (own, out, rows) in enumerate(jobs):
        first[k].wait_recv()
        if rows is my_rows:
            copy = pltpu.make_async_remote_copy(
                out.at[rows, their_cols], out.at[rows, their_cols], send.at[2, k], recv.at[2, k],
                device_id={"row": row}, device_id_type=MESH_ID)
            copy.start()
            copies.append(copy)
    for copy in copies:
        copy.wait_recv()
    for copy in first + copies:
        copy.wait_send()


def group_gather(x, cot, vec):
    half, width = x.shape
    rows, wide = half * lax.axis_size("row"), width * lax.axis_size("col")
    vmem = pl.BlockSpec(memory_space=pltpu.VMEM)
    return pl.pallas_call(
        gather_body,
        out_shape=[
            jax.ShapeDtypeStruct((rows, wide), x.dtype),
            jax.ShapeDtypeStruct((rows, wide), cot.dtype),
            jax.ShapeDtypeStruct((vec.shape[0], wide), vec.dtype),
        ],
        in_specs=[vmem] * 3,
        out_specs=[vmem] * 3,
        scratch_shapes=[pltpu.SemaphoreType.DMA((3, 3)), pltpu.SemaphoreType.DMA((3, 3))],
        compiler_params=pltpu.CompilerParams(collective_id=1, has_side_effects=True),
        name="group_gather",
    )(x, cot, vec)


def make_scores(query, key, allowed):
    scores = jnp.einsum("hqd,hkd->hqk", query, key, preferred_element_type=F32) * SCALE
    return jnp.where(allowed[None], scores, NEG)


def swap_col(value):
    return lax.ppermute(value, "col", [(0, 1), (1, 0)])


def columns_whole(own, gate):
    col = lax.axis_index("col")
    depth, width = own.shape[1], own.shape[2] // 2
    later = (gate.reshape(-1)[0].astype(F32) * 0.0).astype(jnp.int32)
    got = swap_col(lax.dynamic_slice_in_dim(own, (1 - col) * width + later, width, 2))
    kept = lax.dynamic_slice_in_dim(own, col * width, width, 2)
    low = jnp.where(col == 0, kept, got)
    high = jnp.where(col == 0, got, kept)
    return jnp.concatenate([low, high], axis=1)


def rows_whole(grad):
    col = lax.axis_index("col")
    depth = grad.shape[0] // 2
    got = swap_col(lax.dynamic_slice_in_dim(grad, (1 - col) * depth, depth, 0))
    kept = lax.dynamic_slice_in_dim(grad, col * depth, depth, 0)
    low = jnp.where(col == 0, kept, got)
    high = jnp.where(col == 0, got, kept)
    return jnp.concatenate([low, high], axis=1)


def forward_layer(state, allowed, cosine, sine, params):
    gain1, bias1, gain2, bias2, w_qkv, b_qkv, w_up, b_up, w_out, w_down, b_both = params
    width = state.shape[1]
    mean = jnp.sum(state, axis=1, keepdims=True) / width
    squares = jnp.sum(state * state, axis=1, keepdims=True) / width
    inverse = lax.rsqrt(squares - mean * mean + EPS)
    normed = (state - mean) * inverse
    first = (normed * gain1 + bias1).astype(BF)
    second = (normed * gain2 + bias2).astype(BF)
    rows = state.shape[0]
    qkv = (jnp.dot(first, w_qkv, preferred_element_type=F32) + b_qkv).reshape(rows, -1, 3, HD)
    query = rotate(qkv[:, :, 0], cosine, sine).astype(BF).transpose(1, 0, 2)
    key = rotate(qkv[:, :, 1], cosine, sine).astype(BF).transpose(1, 0, 2)
    value = qkv[:, :, 2].astype(BF).transpose(1, 0, 2)
    scores = make_scores(query, key, allowed)
    top = jnp.max(scores, axis=-1, keepdims=True)
    lse = top + jnp.log(jnp.sum(jnp.exp(scores - top), axis=-1, keepdims=True))
    probs = jnp.exp(scores - lse).astype(BF)
    mixed = jnp.einsum("hqk,hkd->qhd", probs, value, preferred_element_type=F32)
    mixed = mixed.astype(BF).reshape(rows, -1)
    up = jnp.dot(second, w_up, preferred_element_type=F32) + b_up
    act = gelu_exact(up).astype(BF)
    part = jnp.dot(mixed, w_out, preferred_element_type=F32) + jnp.dot(
        act, w_down, preferred_element_type=F32)
    return part, (normed, inverse, first, second, query, key, value, mixed, lse, up, act)


def backward_layer(grad, allowed, cosine, sine, params, cache):
    gain1, bias1, gain2, bias2, w_qkv, b_qkv, w_up, b_up, w_out, w_down, b_both = params
    normed, inverse, first, second, query, key, value, mixed, lse, up, act = cache
    rows, width = grad.shape
    grad_b = grad.astype(BF)
    g_bout = jnp.sum(grad, axis=0)
    grad_mixed = jnp.einsum("td,kd->tk", grad_b, w_out, preferred_element_type=F32).astype(BF)
    grad_act = jnp.einsum("td,kd->tk", grad_b, w_down, preferred_element_type=F32)
    grad_up = grad_act * gelu_slope(up)
    g_bup = jnp.sum(grad_up, axis=0)
    grad_up_b = grad_up.astype(BF)
    scores = make_scores(query, key, allowed)
    probs = jnp.exp(scores - lse)
    grad_heads = grad_mixed.reshape(rows, -1, HD).transpose(1, 0, 2)
    mixed_heads = mixed.reshape(rows, -1, HD).transpose(1, 0, 2)
    delta = jnp.sum(grad_heads.astype(F32) * mixed_heads.astype(F32), axis=-1, keepdims=True)
    grad_value = jnp.einsum("hqk,hqd->khd", probs.astype(BF), grad_heads, preferred_element_type=F32)
    grad_probs = jnp.einsum("hqd,hkd->hqk", grad_heads, value, preferred_element_type=F32)
    grad_scores = (probs * (grad_probs - delta) * SCALE).astype(BF)
    grad_query = jnp.einsum("hqk,hkd->qhd", grad_scores, key, preferred_element_type=F32)
    grad_key = jnp.einsum("hqk,hqd->khd", grad_scores, query, preferred_element_type=F32)
    grad_query = unrotate(grad_query, cosine, sine)
    grad_key = unrotate(grad_key, cosine, sine)
    grad_qkv = jnp.stack([grad_query, grad_key, grad_value], axis=2).reshape(rows, -1)
    g_bqkv = jnp.sum(grad_qkv, axis=0)
    grad_qkv_b = grad_qkv.astype(BF)
    part_first = jnp.einsum("tn,dn->td", grad_qkv_b, w_qkv, preferred_element_type=F32)
    part_second = jnp.einsum("tn,dn->td", grad_up_b, w_up, preferred_element_type=F32)
    part = part_first * gain1 + part_second * gain2
    g_wout = jnp.einsum("tk,td->kd", mixed, grad_b, preferred_element_type=F32)
    g_wdown = jnp.einsum("tk,td->kd", act, grad_b, preferred_element_type=F32)
    g_wqkv = jnp.einsum("td,tn->dn", first, grad_qkv_b, preferred_element_type=F32)
    g_wup = jnp.einsum("td,tn->dn", second, grad_up_b, preferred_element_type=F32)
    shares = lax.axis_size("row") * lax.axis_size("col")
    narrow = jnp.concatenate([
        jnp.stack([
            jnp.sum(part_first * normed, axis=0), jnp.sum(part_first, axis=0),
            jnp.sum(part_second * normed, axis=0), jnp.sum(part_second, axis=0),
            g_bout / shares,
        ]),
        jnp.zeros((3, width), F32),
    ])
    grad_norm, narrow = group_sum(part, narrow)
    centred = (
        grad_norm
        - jnp.sum(grad_norm, axis=1, keepdims=True) / width
        - normed * (jnp.sum(grad_norm * normed, axis=1, keepdims=True) / width)
    )
    grad_x = grad + inverse * centred
    heavy = (g_wqkv.astype(BF), g_wup.astype(BF), g_wout.astype(BF), g_wdown.astype(BF))
    return grad_x, heavy, (g_bqkv, g_bup), narrow


def per_device_plain(
    x_in, cotangent, segment_ids, norm1_gain, norm1_bias, norm2_gain, norm2_bias,
    w_qkv, b_qkv, w_up, b_up, w_out, b_out, w_down, b_down,
):
    half, part_width = x_in.shape
    row = lax.axis_index("row")
    col = lax.axis_index("col")
    length = segment_ids.shape[1]
    layers = w_qkv.shape[0]
    cosine, sine = rope_tables(length)
    places = jnp.arange(length, dtype=jnp.int32)
    labels = segment_ids[0]
    allowed = (places[:, None] >= places[None, :]) & (labels[:, None] == labels[None, :])
    vec = jnp.stack([norm1_gain, norm1_bias, norm2_gain, norm2_bias, b_out + b_down])
    vec = vec.reshape(-1, part_width)
    pad = -vec.shape[0] % 8
    state_in, cot, vec = group_gather(x_in, cotangent.astype(BF), jnp.pad(vec, ((0, pad), (0, 0))))
    grad_in = cot.astype(F32)
    vectors = vec[: vec.shape[0] - pad].reshape(5, layers, -1)
    wide_qkv, wide_up, gate = [], [], vec
    for l in range(layers):
        wide_qkv.append(columns_whole(w_qkv[l : l + 1], gate)[0])
        wide_up.append(columns_whole(w_up[l : l + 1], gate)[0])
        gate = wide_qkv[-1]

    def own(whole):
        return lax.dynamic_slice(whole, (row * half, col * part_width), (half, part_width))

    params = [
        (vectors[0, l], vectors[1, l], vectors[2, l], vectors[3, l], wide_qkv[l], b_qkv[l],
         wide_up[l], b_up[l], w_out[l], w_down[l], vectors[4, l])
        for l in range(layers)
    ]
    state = state_in
    caches = []
    for layer in range(layers):
        part, cache = forward_layer(state, allowed, cosine, sine, params[layer])
        caches.append(cache)
        if layer < layers - 1:
            state = state + group_sum(part) + params[layer][-1]
    y_base = x_in + own(state - state_in + params[-1][-1])
    grad = grad_in
    heavy = [None] * layers
    thin = [None] * layers
    narrow = [None] * layers
    for layer in reversed(range(layers)):
        grad, heavy[layer], thin[layer], narrow[layer] = backward_layer(
            grad, allowed, cosine, sine, params[layer], caches[layer])
    x_grad = cotangent + own(grad - grad_in)
    y_out = y_base + own(group_sum(part))
    summed = []
    for layer in range(layers):
        a, b, c, d = heavy[layer]
        summed.append(lax.psum((rows_whole(a), rows_whole(b), c, d), "dp"))
    g_bqkv, g_bup, narrow = lax.psum((
        jnp.stack([t[0] for t in thin]), jnp.stack([t[1] for t in thin]),
        jnp.stack([t[:5] for t in narrow])), "dp")
    g_wqkv, g_wup, g_wout, g_wdown = (
        jnp.stack([h[k] for h in summed]).astype(F32) for k in range(4))
    narrow = lax.dynamic_slice_in_dim(narrow, col * part_width, part_width, 2)
    g_bout = narrow[:, 4]
    return (
        y_out, x_grad, narrow[:, 0], narrow[:, 1], narrow[:, 2], narrow[:, 3],
        g_wqkv, g_bqkv, g_wup, g_bup, g_wout, g_bout, g_wdown, g_bout,
    )


BLK = 128
TICKS = (3, 3, 4, 8, 8, 5, 5, 5, 5, 5)


def tdot(a, b):
    return lax.dot_general(a, b, (((0,), (0,)), ((), ())), preferred_element_type=F32)


def ntdot(a, b):
    return lax.dot_general(a, b, (((1,), (1,)), ((), ())), preferred_element_type=F32)


def ndot(a, b):
    return jnp.dot(a, b, preferred_element_type=F32)


def whole_body(
    n, x, cot, seg, n1g, n1b, n2g, n2b, bq, bu, bo, bd, cosr, sinr, wq_in, wu_in, wo_in, wd_in,
    y, xg, od_out, ow, ou_out, oq_out, osm,
    wq, wu, wo, wd, xb, cb, vec, mask, st, nrm, inv, fst, snd, act, slope, qkv_t, qh, p_t, m_t,
    gm_t, gub, gqb_t, gq, gb, own, sb, got_row, mine, got_col, back, back_got,
    ind, inw, iu, iq, ism, rd, rw, ru, rq, rsm, swu, swq,
    nar, nar_got, thin, bqw, od, ou, oq, send, recv, local, leave,
):
    layers = wq.shape[0]
    gq_t = qkv_t
    half, cols = x.shape
    length, width = half * 2, cols * 2
    hid = wu.shape[2]
    heads = p_t.shape[1]
    qw = heads * 3 * HD
    row, col, here = lax.axis_index("row"), lax.axis_index("col"), lax.axis_index("dp")
    orow, ocol = 1 - row, 1 - col
    odd = lax.rem(here, 2)
    pos = here // 2 + odd * (n - 1 - 2 * (here // 2))

    def device(place):
        late = place // (n // 2)
        return 2 * (place + late * (n - 1 - 2 * place)) + late

    targets = (device(lax.rem(pos + 1, n)), device(lax.rem(pos + n - 1, n)))
    beside = here + 1 - 2 * odd
    high = lax.rem(here // 2, 2)
    along = here + 2 - 4 * high
    barrier = pltpu.get_barrier_semaphore()
    pl.semaphore_signal(barrier, inc=1, device_id={"dp": beside}, device_id_type=MESH_ID)
    pl.semaphore_signal(barrier, inc=1, device_id={"dp": along}, device_id_type=MESH_ID)
    pl.semaphore_signal(barrier, inc=1, device_id={"dp": targets[0]}, device_id_type=MESH_ID)
    pl.semaphore_signal(barrier, inc=1, device_id={"dp": targets[1]}, device_id_type=MESH_ID)
    pl.semaphore_signal(barrier, inc=1, device_id={"col": ocol}, device_id_type=MESH_ID)
    pl.semaphore_signal(barrier, inc=1, device_id={"row": orow}, device_id_type=MESH_ID)

    count = [0]
    sent = []

    def rc(src, dst, axis, target):
        k = count[0]
        count[0] += 1
        copy = pltpu.make_async_remote_copy(
            src, dst, send.at[k], recv.at[k], device_id={axis: target}, device_id_type=MESH_ID)
        copy.start()
        sent.append(copy)
        return copy

    def over_row(src, dst):
        return rc(src, dst, "row", orow)

    def over_col(src, dst):
        return rc(src, dst, "col", ocol)

    def at(base, size, step=None):
        return pl.ds(pl.multiple_of(base, step or size), size)

    my_rows, their_rows = at(row * half, half), at(orow * half, half)
    my_cols, their_cols = at(col * cols, cols), at(ocol * cols, cols)
    shift = wq_in.shape[2] - wq.shape[2]
    my_heads, their_heads = at(col * shift, wq.shape[2], BLK), at(ocol * shift, wq.shape[2], BLK)
    my_hid, their_hid = at(col * hid, hid), at(ocol * hid, hid)

    loads = []
    for l in range(layers):
        loads.append([
            pltpu.make_async_copy(wq_in.at[l, :, my_heads], wq.at[l, my_cols], local.at[l, 0]),
            pltpu.make_async_copy(wu_in.at[l, :, my_hid], wu.at[l, my_cols], local.at[l, 1]),
            pltpu.make_async_copy(wo_in.at[l], wo.at[l], local.at[l, 2]),
            pltpu.make_async_copy(wd_in.at[l], wd.at[l], local.at[l, 3]),
        ])
        for copy in loads[-1]:
            copy.start()

    xb[my_rows, my_cols] = x[...].astype(BF)
    cb[my_rows, my_cols] = cot[...].astype(BF)
    for k, ref in enumerate((n1g, n1b, n2g, n2b)):
        vec[2 * k : 2 * k + 2, my_cols] = ref[...]
    vec[8:10, my_cols] = bo[...] + bd[...]
    pl.semaphore_wait(barrier, 6)

    x_col = over_col(xb.at[my_rows, my_cols], xb.at[my_rows, my_cols])
    x_row = over_row(xb.at[my_rows, my_cols], xb.at[my_rows, my_cols])
    v_col = over_col(vec.at[:, my_cols], vec.at[:, my_cols])

    some = cols // 4
    few = some // 2
    mine_of, y_of, z_of = odd + 2 * high, 1 - odd + 2 * high, odd + 2 * (1 - high)

    def fetch(kind, l):
        src, lanes, dst = ((wq_in, their_heads, wq), (wu_in, their_hid, wu))[kind]
        return dst, l, over_col(
            src.at[l, at(mine_of * some, some), lanes], dst.at[l, at(col * cols + mine_of * some, some)])

    def spread(got):
        dst, l, copy = got
        copy.wait_recv()
        spot = dst.at[l, at(ocol * cols + mine_of * some, some)]
        return dst, l, rc(spot, spot, "dp", beside), rc(spot, spot, "dp", along)

    def relay(got):
        dst, l, by_y, by_z = got
        by_y.wait_recv()
        spot = dst.at[l, at(ocol * cols + y_of * some, few)]
        on_z = rc(spot, spot, "dp", along)
        by_z.wait_recv()
        spot = dst.at[l, at(ocol * cols + z_of * some + few, few, few)]
        return on_z, rc(spot, spot, "dp", beside)

    def arrived(got):
        for copy in got:
            copy.wait_recv()

    q_0, u_0 = fetch(0, 0), fetch(1, 0)
    c_row = over_row(cb.at[my_rows, my_cols], cb.at[my_rows, my_cols])

    label = seg[...].astype(F32)
    tall = jnp.broadcast_to(label, (BLK, length)).T
    for k in range(length // BLK):
        here_rows = slice(k * BLK, (k + 1) * BLK)
        key_at = lax.broadcasted_iota(jnp.int32, (BLK, length), 0) + k * BLK
        query_at = lax.broadcasted_iota(jnp.int32, (BLK, length), 1)
        same = tall[here_rows, 0:1] == label
        mask[here_rows, :] = jnp.where(same & (key_at <= query_at), 0.0, NEG)
    nar[...] = jnp.zeros_like(nar)
    pad = jnp.zeros((layers, wq.shape[2] - qw), F32)
    bqw[...] = jnp.where(
        col == 0, jnp.concatenate([bq[...], pad], axis=1), jnp.concatenate([pad, bq[...]], axis=1))
    offset = col * (wq.shape[2] - qw)

    x_col.wait_recv()
    x_over = over_row(xb.at[my_rows, their_cols], xb.at[my_rows, their_cols])
    v_col.wait_recv()
    x_row.wait_recv()
    x_over.wait_recv()

    def gain(k, l):
        return vec[2 * k + l : 2 * k + l + 1, :]

    blocks = length // BLK

    def norm_step(l):
        @pl.loop(0, blocks)
        def _(i):
            rows = at(i * BLK, BLK)
            s = xb[rows, :].astype(F32) if l == 0 else st[rows, :]
            mean = jnp.sum(s, axis=1, keepdims=True) / width
            squares = jnp.sum(s * s, axis=1, keepdims=True) / width
            inverse = lax.rsqrt(squares - mean * mean + EPS)
            normed = (s - mean) * inverse
            inv[l, rows, :] = inverse
            nrm[l, rows, :] = normed.astype(BF)
            fst[l, rows, :] = (normed * gain(0, l) + gain(1, l)).astype(BF)
            snd[l, rows, :] = (normed * gain(2, l) + gain(3, l)).astype(BF)

    def qkv_step(l):
        @pl.loop(0, blocks)
        def _(i):
            rows = at(i * BLK, BLK)
            got = ndot(fst[l, rows, :], wq[l]) + bqw[l : l + 1, :]
            qkv_t[:, rows] = got.T

    def turn(v, sign):
        a, b = v[0:8], v[8:16]
        c, s = cosr[...], sinr[...] * sign
        return jnp.concatenate([a * c - b * s, b * c + a * s, v[16:]], axis=0)

    QB = length // 2

    def attention_step(l):
        @pl.loop(0, heads)
        def _(h):
            base = offset + h * (3 * HD)
            q = turn(qkv_t[at(base, HD), :], 1.0).astype(BF)
            k = turn(qkv_t[at(base + HD, HD), :], 1.0).astype(BF)
            v = qkv_t[at(base + 2 * HD, HD), :].astype(BF)
            spot = h * (3 * HD)
            qh[l, at(spot, HD), :] = q
            qh[l, at(spot + HD, HD), :] = k
            qh[l, at(spot + 2 * HD, HD), :] = v
            q = q * jnp.asarray(SCALE, BF)
            for b in range(2):
                keys, these = slice(0, (b + 1) * QB), slice(b * QB, (b + 1) * QB)
                scores = tdot(k[:, keys], q[:, these]) + mask[keys, these]
                top = jnp.max(scores, axis=0, keepdims=True)
                e = jnp.exp(scores - top)
                total = jnp.sum(e, axis=0, keepdims=True)
                probs = (e * (1.0 / total)).astype(BF)
                p_t[l, h, keys, these] = probs
                m_t[l, at(h * HD, HD), these] = ndot(v[:, keys], probs).astype(BF)

    def up_step(l):
        @pl.loop(0, blocks)
        def _(i):
            rows = at(i * BLK, BLK)
            up = ndot(snd[l, rows, :], wu[l]) + bu[l : l + 1, :]
            phi = 0.5 * (1.0 + lax.erf(up * INV_ROOT2))
            act[l, rows, :] = (up * phi).astype(BF)
            slope[l, rows, :] = (phi + up * jnp.exp(-0.5 * up * up) * INV_ROOT_TWO_PI).astype(BF)

    def part_rows(l):
        def run(base):
            rows = at(base, BLK)
            return tdot(m_t[l, :, rows], wo[l]) + ndot(act[l, rows, :], wd[l])
        return run

    pieces = half // BLK

    def sum_begin(k, fn):
        flight = []
        for p in range(pieces):
            here = slice(p * BLK, (p + 1) * BLK)
            sb[k, here, :] = fn(orow * half + p * BLK).astype(BF)
            flight.append(over_row(sb.at[k, here], got_row.at[k, here]))
        for p in range(pieces):
            here = slice(p * BLK, (p + 1) * BLK)
            own[k % 2, here, :] = fn(row * half + p * BLK)
        return flight

    def sum_cross(k, flight, narrow=False):
        crossing = []
        for p in range(pieces):
            here = slice(p * BLK, (p + 1) * BLK)
            flight[p].wait_recv()
            t = own[k % 2, here, :] + got_row[k, here, :].astype(F32)
            own[k % 2, here, :] = t
            mine[k, here, :] = t.astype(BF)
            if narrow:
                crossing.append(over_col(
                    mine.at[k, here, their_cols], got_col.at[k, here, their_cols]))
            else:
                crossing.append(over_col(mine.at[k, here], got_col.at[k, here]))
        return crossing


    norm_step(0)
    q_0 = spread(q_0)
    u_0 = spread(u_0)
    c_col = over_col(cb.at[my_rows, my_cols], cb.at[my_rows, my_cols])
    u_1, q_1 = fetch(1, 1), fetch(0, 1)
    q_0 = relay(q_0)
    u_0 = relay(u_0)
    loads[0][0].wait()
    arrived(q_0)
    qkv_step(0)
    attention_step(0)
    loads[0][1].wait()
    arrived(u_0)
    up_step(0)
    loads[0][2].wait()
    loads[0][3].wait()
    flight = sum_begin(0, part_rows(0))
    crossing = sum_cross(0, flight)
    u_1 = spread(u_1)
    q_1 = spread(q_1)
    c_col.wait_recv()
    c_over = over_row(cb.at[my_rows, their_cols], cb.at[my_rows, their_cols])
    both = vec[8:9, :]
    returned = []
    for p in range(pieces):
        here = slice(p * BLK, (p + 1) * BLK)
        crossing[p].wait_recv()
        total = own[0, here, :] + got_col[0, here, :].astype(F32)
        own[0, here, :] = total
        back[0, here, :] = total.astype(BF)
        returned.append(over_row(back.at[0, here], back_got.at[0, here]))
    for p in range(pieces):
        here = slice(p * BLK, (p + 1) * BLK)
        rows = at(row * half + p * BLK, BLK)
        st[rows, :] = xb[rows, :].astype(F32) + own[0, here, :] + both
    y[...] = x[...] + own[0, :, my_cols] + vec[8:9, my_cols] + vec[9:10, my_cols]
    u_1 = relay(u_1)
    q_1 = relay(q_1)
    for p in range(pieces):
        here = slice(p * BLK, (p + 1) * BLK)
        returned[p].wait_recv()
        rows = at(orow * half + p * BLK, BLK)
        st[rows, :] = xb[rows, :].astype(F32) + back_got[0, here, :].astype(F32) + both

    def chunk(d, behind):
        sign = 1 if d == 0 else -1
        return lax.rem(pos - sign * behind + 2 * n, n)

    left = {(k, l): (2, 2, 1)[k] for k in range(3) for l in range(layers)}
    leaving = []

    def finish(k, l):
        left[k, l] -= 1
        if left[k, l] == 0:
            src, dst = ((od, od_out), (ou, ou_out), (oq, oq_out))[k]
            copy = pltpu.make_async_copy(src.at[l], dst.at[l], leave.at[l, k])
            copy.start()
            leaving.append(copy)

    def stream(d, parts, swap=None, lane=0, reach=0, done=None):
        def go(pairs):
            return [rc(src, dst, "dp", targets[d]) for src, dst in pairs]
        copies = go([(rin(chunk(d, 0)), got(0)) for rin, got, out in parts])
        for s in range(n - 1):
            yield
            for k, (rin, got, out) in enumerate(parts):
                copies[k].wait_recv()
                got(s)[...] = got(s)[...] + rin(chunk(d, s + 1))[...]
                if s < n - 2:
                    copies[k] = go([(got(s), got(s + 1))])[0]
        where = chunk(d, n - 1)
        if swap is None:
            for rin, got, out in parts:
                out(where)[...] = got(n - 2)[...]
        else:
            last, out = parts[0][1](n - 2), parts[0][2]
            over = over_col(last.at[ocol], swap)
            yield
            over.wait_recv()
            wide = last.shape[2]
            if reach:
                out(where, at(col * reach + lane, wide, BLK))[...] = last[col]
                out(where, at(ocol * reach + lane, wide, BLK))[...] = swap[...]
            else:
                a, b = last[col].astype(F32), swap[...].astype(F32)
                first = col == 0
                out(where)[...] = jnp.concatenate(
                    [jnp.where(first, a, b), jnp.where(first, b, a)], axis=1).astype(BF)
        if reach:
            spots = [lambda c, k=k: parts[0][2](c, slice(k * reach + lane, k * reach + lane + wide))
                     for k in range(2)]
        else:
            spots = [part[2] for part in parts]
        copies = go([(spot(where), spot(where)) for spot in spots])
        for s in range(n - 1):
            yield
            for k, spot in enumerate(spots):
                copies[k].wait_recv()
                if s < n - 2:
                    where = chunk(d, s)
                    copies[k] = go([(spot(where), spot(where))])[0]
        if done is not None:
            finish(*done)

    active = []

    def launch(*args, **kw):
        g = stream(*args, **kw)
        next(g)
        active.append(g)

    def pump(times):
        for _ in range(times):
            if active:
                g = active.pop(0)
                try:
                    next(g)
                    active.append(g)
                except StopIteration:
                    pass

    deep = hid // n

    def tick(k):
        pump(TICKS[k])

    def down_step(l, g):
        for k in range(2):
            f = slice(k * (hid // 2), (k + 1) * (hid // 2))
            got = tdot(act[l, :, f], g[...]).astype(BF)
            ind[l, k * (n // 2) : (k + 1) * (n // 2)] = got.reshape(n // 2, deep, width)
        cut = deep - 16 * (l + 1)
        launch(0, [(lambda c: ind.at[l, c, 0:cut], lambda s: rd.at[l, s, 0:cut],
                    lambda c: od.at[l, at(c * deep, cut, 16)])], done=(0, l))
        launch(1, [(lambda c: ind.at[l, c, cut:deep], lambda s: rd.at[l, s, cut:deep],
                    lambda c: od.at[l, at(c * deep + cut, deep - cut, 16)])], done=(0, l))

    def out_step():
        both = [ndot(m_t[l], g[...]).reshape(n, -1, width) for l, g in enumerate((gb, cb))]
        inw[...] = jnp.concatenate(both, axis=1).astype(BF)
        launch(0, [(lambda c: inw.at[c], lambda s: rw.at[s], lambda c: ow.at[c])])

    def up_grad_step(l):
        for k in range(2):
            f = slice(k * cols, (k + 1) * cols)
            got = tdot(snd[l, :, f], gub[...]).astype(BF)
            iu[l, :, k] = got.reshape(n, -1, hid)
        part, tall = hid // 2, iu.shape[3]
        for d in range(2):
            lanes = slice(d * part, (d + 1) * part)
            launch(d, [(lambda c, lanes=lanes: iu.at[l, c, :, :, lanes],
                        lambda s, lanes=lanes: ru.at[l, s, :, :, lanes],
                        lambda c, lanes: ou.at[l, at(c * tall, tall), lanes])],
                   swap=swu.at[l, :, lanes], lane=d * part, reach=hid, done=(1, l))

    def qkv_grad_step(l):
        for k in range(2):
            f = slice(k * cols, (k + 1) * cols)
            got = ntdot(fst[l, :, f].T, gqb_t[...]).astype(BF)
            iq[l, :, k] = got.reshape(n, -1, qw)
        launch(1, [(lambda c: iq.at[l, c], lambda s: rq.at[l, s],
                    lambda c: oq.at[l, at(c * iq.shape[3], iq.shape[3])])], swap=swq.at[l], done=(2, l))

    def grad_up_step(l, g):
        def block(i, total):
            rows = at(i * BLK, BLK)
            gu = ntdot(g[rows, :], wd[l]) * slope[l, rows, :].astype(F32)
            gub[rows, :] = gu.astype(BF)
            return total + jnp.sum(gu, axis=0, keepdims=True)
        total = lax.fori_loop(0, blocks, block, jnp.zeros((1, hid), F32))
        thin[l, 1:2, 0:hid] = total

    def attention_back_step(l, g):
        gm_t[...] = ntdot(wo[l], g[...]).astype(BF)

        @pl.loop(0, heads)
        def _(h):
            spot = h * (3 * HD)
            q = qh[l, at(spot, HD), :]
            k = qh[l, at(spot + HD, HD), :]
            v = qh[l, at(spot + 2 * HD, HD), :]
            gm = gm_t[at(h * HD, HD), :]
            mixed = m_t[l, at(h * HD, HD), :]
            delta = jnp.sum(gm.astype(F32) * mixed.astype(F32), axis=0, keepdims=True)
            gqs, gks, gvs = [], [], []
            for b in range(2):
                keys, these = slice(0, (b + 1) * QB), slice(b * QB, (b + 1) * QB)
                probs = p_t[l, h, keys, these]
                gp = tdot(v[:, keys], gm[:, these])
                ds = (probs.astype(F32) * (gp - delta[:, these])).astype(BF)
                gqs.append(ndot(k[:, keys], ds))
                gks.append(ntdot(q[:, these], ds))
                gvs.append(ntdot(gm[:, these], probs))
            gq_h = jnp.concatenate(gqs, axis=1) * SCALE
            gk_h = jnp.concatenate([gks[0] + gks[1][:, :QB], gks[1][:, QB:]], axis=1) * SCALE
            gv_h = jnp.concatenate([gvs[0] + gvs[1][:, :QB], gvs[1][:, QB:]], axis=1)
            base = offset + spot
            for k3, value in enumerate((turn(gq_h, -1.0), turn(gk_h, -1.0), gv_h)):
                gq_t[at(base + k3 * HD, HD), :] = value
                gqb_t[at(spot + k3 * HD, HD), :] = value.astype(BF)

        total = jnp.zeros((1, gq_t.shape[0]), F32)
        for i in range(blocks):
            flat = gq_t[:, i * BLK : (i + 1) * BLK].T
            gq[i * BLK : (i + 1) * BLK, :] = flat.astype(BF)
            total = total + jnp.sum(flat, axis=0, keepdims=True)
        thin[l, 0:1, :] = jnp.concatenate([total, jnp.zeros((1, width - total.shape[1]), F32)], axis=1)

    def back_rows(l):
        def run(base):
            rows = at(base, BLK)
            gf = ntdot(gq[rows, :], wq[l])
            gs = ntdot(gub[rows, :], wu[l])
            normed = nrm[l, rows, :].astype(F32)
            for k, value in enumerate((gf * normed, gf, gs * normed, gs)):
                nar[l, 0, k : k + 1, :] += jnp.sum(value, axis=0, keepdims=True)
            return gf * gain(0, l) + gs * gain(2, l)
        return run

    def centred(l, rows, total):
        normed = nrm[l, rows, :].astype(F32)
        return inv[l, rows, :] * (
            total - jnp.sum(total, axis=1, keepdims=True) / width
            - normed * (jnp.sum(total * normed, axis=1, keepdims=True) / width))

    shares = 0.25
    norm_step(1)
    loads[1][1].wait()
    arrived(u_1)
    up_step(1)
    c_row.wait_recv()
    c_over.wait_recv()
    loads[1][2].wait()
    loads[1][3].wait()
    down_step(1, cb)
    grad_up_step(1, cb)
    up_grad_step(1)
    loads[1][0].wait()
    arrived(q_1)
    qkv_step(1)
    tick(0)
    attention_step(1)
    tick(1)
    nar[1, 0, 4:5, :] = jnp.sum(cb[...].astype(F32), axis=0, keepdims=True) * shares
    gq_t[...] = jnp.zeros_like(gq_t)
    attention_back_step(1, cb)
    tick(2)
    flight = sum_begin(1, back_rows(1))
    nar_row = over_row(nar.at[1, 0], nar_got.at[1, 0])
    qkv_grad_step(1)
    crossing = sum_cross(1, flight)
    tick(3)
    returned = []
    for p in range(pieces):
        here = slice(p * BLK, (p + 1) * BLK)
        crossing[p].wait_recv()
        total = own[1, here, :] + got_col[1, here, :].astype(F32)
        own[1, here, :] = total
        back[1, here, :] = total.astype(BF)
        returned.append(over_row(back.at[1, here], back_got.at[1, here]))
    bout = jnp.zeros((1, width), F32)
    for p in range(pieces):
        here = slice(p * BLK, (p + 1) * BLK)
        rows = at(row * half + p * BLK, BLK)
        change = centred(1, rows, own[1, here, :])
        own[1, here, :] = change
        grad = cb[rows, :].astype(F32) + change
        gb[rows, :] = grad.astype(BF)
        bout = bout + jnp.sum(grad, axis=0, keepdims=True)
    xg[...] = cot[...] + own[1, :, my_cols]
    for p in range(pieces):
        here = slice(p * BLK, (p + 1) * BLK)
        returned[p].wait_recv()
        rows = at(orow * half + p * BLK, BLK)
        grad = cb[rows, :].astype(F32) + centred(1, rows, back_got[1, here, :].astype(F32))
        gb[rows, :] = grad.astype(BF)
        bout = bout + jnp.sum(grad, axis=0, keepdims=True)
    nar[0, 0, 4:5, :] = bout * shares
    nar_row.wait_recv()
    nar[1, 1] = nar[1, 0] + nar_got[1, 0]
    nar_col = over_col(nar.at[1, 1], nar_got.at[1, 1])
    tick(4)
    down_step(0, gb)
    tick(5)
    out_step()
    grad_up_step(0, gb)
    up_grad_step(0)
    tick(6)
    attention_back_step(0, gb)
    tick(7)
    flight_x = sum_begin(3, back_rows(0))
    nar_row0 = over_row(nar.at[0, 0], nar_got.at[0, 0])
    qkv_grad_step(0)
    tick(8)
    crossing_x = sum_cross(3, flight_x)
    nar_row0.wait_recv()
    nar[0, 1] = nar[0, 0] + nar_got[0, 0]
    nar_col0 = over_col(nar.at[0, 1], nar_got.at[0, 1])
    tick(9)
    nar_col.wait_recv()
    nar_col0.wait_recv()
    ism[...] = jnp.zeros_like(ism)
    few_rows = jnp.concatenate(
        [v for l in range(layers) for v in (
            nar[l, 1, 0:5, :] + nar_got[l, 1, 0:5, :], thin[l, 0:2, :], jnp.zeros((1, width), F32))],
        axis=0).astype(BF)
    for k in range(width // BLK):
        ism[k] = few_rows[:, k * BLK : (k + 1) * BLK]
    launch(0, [(lambda c: ism.at[c], lambda s: rsm.at[s], lambda c: osm.at[c])])
    pump(2)
    flight_y = sum_begin(2, part_rows(1))
    crossing_y = sum_cross(2, flight_y, narrow=True)
    pump(2)
    for p in range(pieces):
        here = slice(p * BLK, (p + 1) * BLK)
        crossing_x[p].wait_recv()
        rows = at(row * half + p * BLK, BLK)
        own[1, here, :] = centred(0, rows, own[1, here, :] + got_col[3, here, :].astype(F32))
    xg[...] += own[1, :, my_cols]
    pump(2)
    for p in range(pieces):
        crossing_y[p].wait_recv()
    y[...] += own[0, :, my_cols] + got_col[2, :, my_cols].astype(F32)
    while active:
        pump(1)
    for copy in sent:
        copy.wait_send()
    for copy in leaving:
        copy.wait()


def whole_step(x, cot, seg, n1g, n1b, n2g, n2b, wq_in, bq, wu_in, bu, wo_in, bo, wd_in, bd):
    n = lax.axis_size("dp")
    half, cols = x.shape
    layers, _, both_heads = wq_in.shape
    length, width = 2 * half, 2 * cols
    hid = wu_in.shape[2] // 2
    qw = both_heads // 2
    heads = qw // (3 * HD)
    wide = -(-qw // BLK) * BLK
    mix = wo_in.shape[1]
    col = lax.axis_index("col")
    freq = np.float32(10000.0) ** (-(np.arange(ROT // 2, dtype=np.float32) * 2) / np.float32(ROT))
    angle = freq[:, None] * np.arange(length, dtype=np.float32)[None, :]
    cosr, sinr = jnp.asarray(np.cos(angle), F32), jnp.asarray(np.sin(angle), F32)
    per, deep, flat = width // 2 // n, hid // n, mix // n
    tall = layers * flat
    small = 8 * layers
    vmem = pl.BlockSpec(memory_space=pltpu.VMEM)
    anyw = pl.BlockSpec(memory_space=pl.ANY)
    V = pltpu.VMEM
    sums = 4
    sems = 384
    out = pl.pallas_call(
        lambda *refs: whole_body(n, *refs),
        out_shape=[
            jax.ShapeDtypeStruct((half, cols), F32), jax.ShapeDtypeStruct((half, cols), F32),
            jax.ShapeDtypeStruct((layers, hid, width), BF),
            jax.ShapeDtypeStruct((n, tall, width), BF),
            jax.ShapeDtypeStruct((layers, width // 2, 2 * hid), BF),
            jax.ShapeDtypeStruct((layers, width // 2, 2 * qw), BF),
            jax.ShapeDtypeStruct((n, small, BLK), BF),
        ],
        in_specs=[vmem] * 13 + [anyw] * 4,
        out_specs=[vmem, vmem, anyw, vmem, anyw, anyw, vmem],
        scratch_shapes=[
            V((layers, width, wide), BF), V((layers, width, hid), BF),
            V((layers, mix, width), BF), V((layers, hid, width), BF),
            V((length, width), BF), V((length, width), BF), V((16, width), F32),
            V((length, length), F32), V((length, width), F32),
            V((layers, length, width), BF), V((layers, length, 1), F32),
            V((layers, length, width), BF), V((layers, length, width), BF),
            V((layers, length, hid), BF), V((layers, length, hid), BF),
            V((wide, length), F32), V((layers, qw, length), BF),
            V((layers, heads, length, length), BF), V((layers, mix, length), BF),
            V((mix, length), BF), V((length, hid), BF),
            V((qw, length), BF), V((length, wide), BF), V((length, width), BF),
            V((2, half, width), F32), V((sums, half, width), BF), V((sums, half, width), BF),
            V((sums, half, width), BF), V((sums, half, width), BF),
            V((2, half, width), BF), V((2, half, width), BF),
            V((layers, n, deep, width), BF), V((n, tall, width), BF),
            V((layers, n, 2, per, hid), BF), V((layers, n, 2, per, qw), BF),
            V((n, small, BLK), BF),
            V((layers, n - 1, deep, width), BF), V((n - 1, tall, width), BF),
            V((layers, n - 1, 2, per, hid), BF), V((layers, n - 1, 2, per, qw), BF),
            V((n - 1, small, BLK), BF),
            V((layers, per, hid), BF), V((layers, per, qw), BF),
            V((layers, 2, 8, width), F32), V((layers, 2, 8, width), F32),
            V((layers, 2, width), F32), V((layers, wide), F32),
            V((layers, hid, width), BF), V((layers, width // 2, 2 * hid), BF),
            V((layers, width // 2, 2 * qw), BF),
            pltpu.SemaphoreType.DMA((sems,)), pltpu.SemaphoreType.DMA((sems,)),
            pltpu.SemaphoreType.DMA((layers, 4)), pltpu.SemaphoreType.DMA((layers, 3)),
        ],
        compiler_params=pltpu.CompilerParams(
            collective_id=5, has_side_effects=True, vmem_limit_bytes=62 * 1024 * 1024),
        name="whole_step",
    )(x, cot, seg, n1g, n1b, n2g, n2b, bq, bu, bo, bd, cosr, sinr, wq_in, wu_in, wo_in, wd_in)
    y, xg, d, w, u, q, s = out
    g_wqkv, g_wup, g_wdown = q.astype(F32), u.astype(F32), d.astype(F32)
    g_wout = w.reshape(n, layers, flat, width).transpose(1, 0, 2, 3).reshape(layers, mix, width).astype(F32)
    s = s[: width // BLK].transpose(1, 0, 2).astype(F32).reshape(layers, 8, width)
    narrow = lax.dynamic_slice_in_dim(s[:, :5], col * cols, cols, 2)
    g_bqkv = lax.dynamic_slice_in_dim(s[:, 5], col * (wide - qw), qw, 1)
    g_bup = s[:, 6, :hid]
    g_bout = narrow[:, 4]
    return (
        y, xg, narrow[:, 0], narrow[:, 1], narrow[:, 2], narrow[:, 3],
        g_wqkv, g_bqkv, g_wup, g_bup, g_wout, g_bout, g_wdown, g_bout)


def per_device(*args):
    x, wq, wo, wd = args[0], args[7], args[11], args[13]
    n = lax.axis_size("dp")
    parts = lax.axis_size("row"), lax.axis_size("col")
    cols = x.shape[1]
    fits = (
        parts == (2, 2) and n % 2 == 0 and n >= 4 and cols % n == 0 and (cols // n) % 16 == 0
        and (wd.shape[1] // n) % 32 == 0 and (wo.shape[1] // n) % 8 == 0 and n * BLK >= 2 * cols and wq.shape[0] == 2)
    return whole_step(*args) if fits else per_device_plain(*args)


def solution(mesh):
    in_specs = (
        P(("dp", "row"), "col"),
        P(("dp", "row"), "col"),
        P("dp", None),
        P(None, "col"),
        P(None, "col"),
        P(None, "col"),
        P(None, "col"),
        P(None, "col", "row"),
        P(None, ("row", "col")),
        P(None, "col", "row"),
        P(None, ("row", "col")),
        P(None, ("row", "col"), None),
        P(None, "col"),
        P(None, ("row", "col"), None),
        P(None, "col"),
    )
    out_specs = (
        P(("dp", "row"), "col"),
        P(("dp", "row"), "col"),
        P(None, "col"),
        P(None, "col"),
        P(None, "col"),
        P(None, "col"),
        P(None, "col", "row"),
        P(None, ("row", "col")),
        P(None, "col", "row"),
        P(None, ("row", "col")),
        P(None, ("row", "col"), None),
        P(None, "col"),
        P(None, ("row", "col"), None),
        P(None, "col"),
    )
    return jax.shard_map(
        per_device, mesh=mesh, in_specs=in_specs, out_specs=out_specs, check_vma=False
    )
```
